32 devices in a mesh: rep: 4 (over y, core), seq: 8 (over z, x).
Axes of the slice: x: 2, y: 2, z: 4, core: 2. Of those that a mesh axis runs over, the one named last changes fastest.
Arguments:
- tokens: float32 [4, 1024, 768], P('rep', 'seq'), may hold values from -6 to 6
- cotangent: float32 [4, 1024, 768], P('rep', 'seq'), may hold values from -6 to 6
- gain_attn: float32 [768], replicated, may hold values from 0.5 to 1.5
- gain_mlp: float32 [768], replicated, may hold values from 0.5 to 1.5
- w_qkv: float32 [768, 2304], P('seq'), may hold values from -0.21875 to 0.21875
- w_attn_out: float32 [768, 768], P('seq'), may hold values from -3 to 3
- router: float32 [768, 8], P('seq'), may hold values from -0.21875 to 0.21875
- rel_table: float32 [12, 32], replicated, may hold values from -4 to 4
- w_in: bfloat16 [8, 768, 3072], P('seq'), may hold values from -0.21875 to 0.21875
- w_out: bfloat16 [8, 3072, 768], P('seq'), may hold values from -0.109375 to 0.109375
- segment_ids: int32 [4, 1024], P('rep'), may hold values from 0 to 3, never falling along the last dimension, each value on 1 to 768 neighbouring positions
- expert_ids: int32 [4, 1024, 2], P('rep', 'seq'), may hold values from 0 to 7, all different within a row; in each aligned block of 128 rows (0 to 127, 128 to 255, ..., all dimensions but the last counted through in order) at most 64 rows name the same one
- rel_bucket: int32 [1024], replicated, may hold values from 0 to 31
Outputs:
- output: float32 [4, 1024, 768], P('rep', 'seq')
- input_grad: float32 [4, 1024, 768], P('rep', 'seq')
- grad_gain_attn: float32 [768], replicated
- grad_gain_mlp: float32 [768], replicated
- grad_w_qkv: float32 [768, 2304], P('seq')
- grad_w_attn_out: float32 [768, 768], P('seq')
- grad_router: float32 [768, 8], P('seq')
- grad_rel_table: float32 [12, 32], replicated
- grad_w_in: float32 [8, 768, 3072], P('seq', None, 'rep')
- grad_w_out: float32 [8, 3072, 768], P('seq', 'rep')
The draws below stay inside these ranges and needn't reach their ends.
Inputs may be any that keep to these rules, and one draw needn't show every extreme that they name: `segment_ids`: segment numbers never fall along a sequence; each segment has 1 to 768 positions and one has exactly 768. `expert_ids`: the two experts of a token differ. Among the tokens of one device (aligned blocks of 128 positions) no expert is named more than 64 times, a bound that some block reaches.
All inputs are finite; a program needn't handle non-finite values.
Results may differ from the reference program's by a relative error of at most 0.015.
The reference program's roundings to bfloat16 on the way count: a program that leaves them out, or rounds other values in their place, can miss the bound.
Values may be sent and summed in bfloat16 or wider, within the bound.
No kernel may reach another device: no remote copies, remote signals or barrier semaphores. Data moves between devices by JAX's collectives and lax.ppermute only.
A program may use at most 320 MiB of HBM per device.

```python
import math
import jax
import jax.numpy as jnp
import numpy as np
from jax import lax

D = 768
HEADS = 12
HEAD = 64
FF = 3072
BUCKETS = 32
TOP = 2
SEGS = 4
TOK_DEV = 128
SEQLEN = 1024
SEQS = 4
EXPERTS = 8
CAP = 64
SEGMAX = 768
N_SEQ = 8


def with_ends(drawn, stream_key, smallest, top_value):
    shape = drawn.shape
    place = [jax.random.randint(jax.random.fold_in(stream_key, axis), (), 0, shape[axis]) for axis in range(len(shape))]
    drawn = drawn.at[tuple(place)].set(smallest)
    longest = shape.index(max(shape))
    place[longest] = (place[longest] + 1) % shape[longest]
    return drawn.at[tuple(place)].set(top_value)


def block_scale(key, extent, cuts, least, largest):
    level, own = 1.0, jax.random.fold_in(key, 6)
    for dim, blocks in cuts:
        steps = jnp.exp(jax.random.uniform(jax.random.fold_in(own, dim), (blocks,), jnp.float32, least / len(cuts), largest / len(cuts)))
        level = level * jnp.repeat(steps, extent[dim] // blocks).reshape([-1 if axis == dim else 1 for axis in range(len(extent))])
    return level


def split_up(amount, total, reach, skew):
    loads = [(1 << 20) // math.isqrt(grade ** skew) + 1 for grade in range(2, amount + 1)]
    surplus, given = total - reach - (amount - 1), [1] * (amount - 1)
    while surplus > 0:
        movable = [i for i in range(amount - 1) if given[i] < reach]
        pool, left = sum([loads[i] for i in movable]), surplus
        for i in movable:
            more = min(reach - given[i], max(1, left * loads[i] // pool), surplus)
            given[i] = given[i] + more
            surplus = surplus - more
    return np.array([reach] + given)


def ragged_sizes(stream_key, amount, total, most, lean):
    if amount == 2:
        one = jax.random.randint(stream_key, (), max(1, total - most), min(most, total - 1) + 1)
        return jnp.stack([one, total - one])
    lengths = jnp.asarray(split_up(amount, total, most, lean), jnp.int32)
    pairs = (amount - 1) // 2
    source_of, taker = lengths[1:1 + 2 * pairs:2], lengths[2:2 + 2 * pairs:2]
    margin = jnp.minimum(source_of - 1, most - taker)
    passed = jax.random.randint(jax.random.fold_in(stream_key, 1), (pairs,), 0, 1 << 20) % (margin + 1)
    lengths = lengths.at[1:1 + 2 * pairs:2].set(source_of - passed).at[2:2 + 2 * pairs:2].set(taker + passed)
    return lengths[jax.random.permutation(jax.random.fold_in(stream_key, 2), amount)]


def deal_out(own_key, own, number, rows, number_of, top, bound, skew):
    sequence = jax.random.permutation(own_key, number_of)
    crowded, ordinary = shares(number_of, rows * top, bound, skew, True), shares(number_of, rows * top, bound, skew, False)
    places = jnp.arange(number_of)

    def named(sizes, rotation):
        used = int((sizes > 0).sum())
        fixed = max(1, used // 4)
        passed = fixed + (places - fixed + rotation * (used - fixed)) % max(1, number_of - fixed)
        return jnp.zeros((number_of,), jnp.int32).at[sequence[jnp.where(places < fixed, places, passed)]].set(jnp.asarray(sizes, jnp.int32))

    sizes = jnp.where(number % 4 == 0, named(crowded, number // 4), named(ordinary, number - number // 4 - 1))
    mixed = jax.random.permutation(jax.random.fold_in(own, 3), number_of)
    donor, receiver = mixed[0:number_of // 2 * 2:2], mixed[1:number_of // 2 * 2:2]
    slack = jnp.minimum(sizes[donor] - 1, bound - sizes[receiver]) // 2
    slack = jnp.where((donor == sequence[0]) | (receiver == sequence[0]) | (sizes[receiver] == 0), 0, jnp.maximum(slack, 0))
    passed = jax.random.randint(jax.random.fold_in(own, 4), (number_of // 2,), 0, 1 << 20) % (slack + 1)
    sizes = sizes.at[donor].add(-passed).at[receiver].add(passed)
    members = jnp.searchsorted(jnp.cumsum(sizes), jnp.arange(rows * top), side="right").astype(jnp.int32)
    listing = members.reshape(top, rows).T
    listing = listing[jax.random.permutation(jax.random.fold_in(own, 1), rows)]
    rotation = jax.random.randint(jax.random.fold_in(own, 2), (rows, 1), 0, top)
    return jnp.take_along_axis(listing, (jnp.arange(top)[None, :] + rotation) % top, axis=1)


def shares(number_of, total, most, lean, full):
    portions = [(1 << 20) // math.isqrt(standing ** lean) + 1 for standing in range(1, number_of + 1)]
    largest = most if full else min(most, max(-(-total // number_of), total * portions[0] // sum(portions)))
    least = 1 if total - largest >= number_of - 1 else 0
    counts, rest = [largest] + [least] * (number_of - 1), total - largest - least * (number_of - 1)
    while rest > 0:
        movable = [i for i in range(1, number_of) if counts[i] < largest] or [i for i in range(1, number_of) if counts[i] < most]
        mass, remaining = sum([portions[i] for i in movable]), rest
        for i in movable:
            extra = min(most - counts[i], max(1, remaining * portions[i] // mass), rest)
            counts[i] = counts[i] + extra
            rest = rest - extra
    return np.array(counts)


def gaussian(rng, extent, scale, most, split=(), held_as=jnp.bfloat16):
    factor_of = block_scale(rng, extent, split, -0.22, 0.18) if split else 1.0
    values = jax.random.normal(rng, extent, jnp.float32) * scale * factor_of
    return jnp.minimum(jnp.maximum(values, -most), most).astype(held_as)


def setup_inputs(seed: int = 0) -> dict:
    arg_keys = jax.random.split(jax.random.key(seed), 14)
    tokens = gaussian(arg_keys[0], (SEQS, SEQLEN, D), 1.0, 6.0, ((0, 4), (1, 8)), jnp.float32)
    cotangent = gaussian(arg_keys[1], (SEQS, SEQLEN, D), 1.0, 6.0, ((0, 4), (1, 8)), jnp.float32)
    gain_attn = jnp.clip(1.0 + 0.1 * jax.random.normal(arg_keys[2], (D,), jnp.float32), 0.5, 1.5)
    gain_mlp = jnp.clip(1.0 + 0.1 * jax.random.normal(arg_keys[3], (D,), jnp.float32), 0.5, 1.5)
    w_qkv = gaussian(arg_keys[4], (D, 3 * D), D ** -0.5, 0.21875, ((0, 8),), jnp.float32)
    w_attn_out = gaussian(arg_keys[5], (D, D), 4 ** -0.5, 3.0, ((0, 8),), jnp.float32)
    router = gaussian(arg_keys[6], (D, EXPERTS), D ** -0.5, 0.21875, ((0, 8),), jnp.float32)
    rel_table = gaussian(arg_keys[7], (HEADS, BUCKETS), 1.0, 4.0, (), jnp.float32)
    w_in = gaussian(arg_keys[8], (EXPERTS, D, FF), D ** -0.5, 0.21875, ((0, 8),))
    w_out = gaussian(arg_keys[9], (EXPERTS, FF, D), FF ** -0.5, 0.109375, ((0, 8),))
    segment_ids = jax.vmap(lambda own: jnp.searchsorted(jnp.cumsum(ragged_sizes(own, SEGS, SEQLEN, SEGMAX, 2)), jnp.arange(SEQLEN), side="right"))(jax.random.split(arg_keys[10], SEQS)).reshape((SEQS, SEQLEN)).astype(jnp.int32)
    expert_ids_keys = jax.random.split(jax.random.fold_in(arg_keys[11], 1), SEQS * SEQLEN // TOK_DEV)
    expert_ids_turns = jax.random.permutation(jax.random.fold_in(arg_keys[11], 3), SEQS * SEQLEN // TOK_DEV)
    expert_ids = jax.vmap(lambda own, number: deal_out(jax.random.fold_in(arg_keys[11], 2), own, number, TOK_DEV, EXPERTS, TOP, CAP, 2))(expert_ids_keys, expert_ids_turns).reshape((SEQS, SEQLEN, TOP))
    rel_bucket = with_ends(jax.random.randint(arg_keys[12], (SEQLEN,), 0, BUCKETS), jax.random.fold_in(arg_keys[12], 1), 0, BUCKETS - 1).astype(jnp.int32)
    return {"tokens": tokens, "cotangent": cotangent, "gain_attn": gain_attn, "gain_mlp": gain_mlp, "w_qkv": w_qkv, "w_attn_out": w_attn_out, "router": router, "rel_table": rel_table, "w_in": w_in, "w_out": w_out, "segment_ids": segment_ids, "expert_ids": expert_ids, "rel_bucket": rel_bucket}


@jax.custom_vjp
def low(v):
    return lax.optimization_barrier(v.astype(jnp.bfloat16)).astype(jnp.float32)

@jax.custom_vjp
def low_back(v):
    return v

def low_keep(v):
    return (low(v), None)

def low_pass(kept, grad):
    return (grad,)

def back_keep(v):
    return (v, None)

def back_low(kept, grad):
    return (low(grad),)
low.defvjp(low_keep, low_pass)
low_back.defvjp(back_keep, back_low)
EPS = 1e-06
HIGHEST = lax.Precision.HIGHEST

def rms_scale(value, gain):
    return value * lax.rsqrt(lax.optimization_barrier(jnp.mean(value * value, axis=-1, keepdims=True)) + EPS) * gain

def attend(queries, keys, values, seg_ids, bias_dist):
    block_size = math.gcd(SEQLEN, 512)
    positions = jnp.arange(SEQLEN, dtype=jnp.int32)

    def one_block(index):
        first = (index * block_size).astype(jnp.int32)
        query_block = lax.dynamic_slice_in_dim(queries, first, block_size, 0)
        query_pos = first + jnp.arange(block_size, dtype=jnp.int32)
        query_segs = lax.dynamic_slice_in_dim(seg_ids, first, block_size, 0)
        scores = jnp.einsum('qhd,khd->hqk', query_block, keys, precision=HIGHEST) * 0.125
        distance = jnp.maximum(query_pos[:, None] - positions[None, :], 0)
        scores = low_back(scores + jnp.take(bias_dist, distance, axis=1))
        allowed = (query_segs[:, None] == seg_ids[None, :]) & (positions[None, :] <= query_pos[:, None])
        scores = jnp.where(allowed[None], scores, -1e+30)
        probs = jax.nn.softmax(scores, axis=-1)
        return jnp.einsum('hqk,khd->qhd', low(probs), values, precision=HIGHEST)
    pieces = lax.map(jax.checkpoint(one_block), jnp.arange(SEQLEN // block_size, dtype=jnp.int32))
    return pieces.reshape(SEQLEN, D)

def expert_apply(pieces):
    rows_in, weight_in, weight_out = pieces
    hidden = low_back(jnp.dot(rows_in, weight_in, precision=HIGHEST))
    active = low(jax.nn.gelu(hidden))
    return low_back(low(jnp.dot(active, weight_out, precision=HIGHEST)))

def layer(inputs, params, seg_ids, chosen_ids, rel_bucket):
    gain_attn, gain_mlp, w_qkv, w_attn_out, router, rel_table, w_in, w_out = params
    h_attn = low(rms_scale(inputs, gain_attn))
    proj_all = low_back(low(jnp.dot(h_attn, low(w_qkv), precision=HIGHEST)))
    queries = proj_all[:, :D].reshape(SEQLEN, HEADS, HEAD)
    keys = proj_all[:, D:2 * D].reshape(SEQLEN, HEADS, HEAD)
    values = proj_all[:, 2 * D:].reshape(SEQLEN, HEADS, HEAD)
    bias_dist = jnp.take(rel_table, rel_bucket, axis=1)
    attended = low_back(low(attend(queries, keys, values, seg_ids, bias_dist)))
    residual = inputs + low_back(jnp.dot(attended, low(w_attn_out), precision=HIGHEST))
    h_mlp = low(rms_scale(residual, gain_mlp))
    logits = jnp.dot(h_mlp, low(router), precision=HIGHEST)
    gate_probs = jax.nn.softmax(jnp.take_along_axis(logits, chosen_ids, axis=1), axis=-1)
    flat_ids = chosen_ids.reshape(N_SEQ, TOK_DEV * TOP)
    flat_hot = (flat_ids[:, :, None] == jnp.arange(EXPERTS, dtype=jnp.int32)[None, None, :]).astype(jnp.int32)
    earlier = jnp.cumsum(flat_hot, axis=1, dtype=jnp.int32) - flat_hot
    slot_index = lax.optimization_barrier(jnp.sum(earlier * flat_hot, axis=2, dtype=jnp.int32))
    source = jnp.broadcast_to(jnp.arange(N_SEQ, dtype=jnp.int32)[:, None], slot_index.shape)
    rows_out = jnp.repeat(h_mlp, TOP, axis=0).reshape(N_SEQ, TOK_DEV * TOP, D)
    buffer = jnp.zeros((EXPERTS, N_SEQ, CAP, D), jnp.float32).at[flat_ids, source, slot_index].set(rows_out)
    buffer = low_back(buffer)
    produced = lax.map(jax.checkpoint(expert_apply), (buffer.reshape(EXPERTS, N_SEQ * CAP, D), w_in, w_out))
    returned = produced.reshape(EXPERTS, N_SEQ, CAP, D)[flat_ids, source, slot_index].reshape(SEQLEN, TOP, D)
    return residual + lax.optimization_barrier(jnp.sum(gate_probs[:, :, None] * returned, axis=1))

def add_trees(left, right):
    return left + right

def reference(tokens, cotangent, gain_attn, gain_mlp, w_qkv, w_attn_out, router, rel_table, w_in, w_out, segment_ids, expert_ids, rel_bucket):
    params = (gain_attn, gain_mlp, w_qkv, w_attn_out, router, rel_table, w_in.astype(jnp.float32), w_out.astype(jnp.float32))

    def one_sequence(totals, pieces):
        inputs, upstream, seg_ids, chosen_ids = pieces

        def forward(values, weights):
            return layer(values, weights, seg_ids, chosen_ids, rel_bucket)
        result, pullback = jax.vjp(forward, inputs, params)
        input_grad, param_grads = pullback(upstream)
        totals = jax.tree.map(add_trees, totals, param_grads)
        return (totals, (result, input_grad))
    zeros = jax.tree.map(jnp.zeros_like, params)
    totals, (results, input_grads) = lax.scan(one_sequence, zeros, (tokens, cotangent, segment_ids, expert_ids))
    return (results, input_grads, totals[0], totals[1], totals[2], totals[3], totals[4], totals[5], totals[6], totals[7])
```

```python
from functools import partial
import math

import jax
import jax.numpy as jnp
from jax import lax
from jax.experimental import pallas as pl
from jax.experimental.pallas import tpu as pltpu
from jax.sharding import Mesh, PartitionSpec as P

D = 768
HEADS = 12
HEAD = 64
BUCKETS = 32
FF = 3072
GROUPS = 4
GHEADS = HEADS // GROUPS
GW = GHEADS * HEAD
EPS = 1e-06
HIGHEST = lax.Precision.HIGHEST
BF = jnp.bfloat16
F32 = jnp.float32
NT = (((1,), (1,)), ((), ()))
TN = (((0,), (0,)), ((), ()))
SEQ = ("g", "i")
REP = ("y", "c")


def dotf(a, b, dims=(((1,), (0,)), ((), ()))):
    return lax.dot_general(a, b, dims, preferred_element_type=F32)


def loop(count, body, init):
    if count <= 2:
        for step in range(count):
            init = body(step, init)
        return init
    return lax.fori_loop(0, count, body, init)


def head_mask(value, head):
    lane = lax.broadcasted_iota(jnp.int32, value.shape, value.ndim - 1)
    return jnp.where(lane // HEAD == head, value, jnp.zeros_like(value))


def bias_kernel(rows_ref, tiles_ref):
    heads, count, size, _ = tiles_ref.shape

    def head_step(head, carry):
        for step in range(count):
            pair = jnp.concatenate(
                (rows_ref[head, step : step + 1, :], rows_ref[head, step + 1 : step + 2, :]), axis=1
            )
            spread = jnp.broadcast_to(pair, (size, 2 * size))
            tiles_ref[head, step] = pltpu.roll(spread, 0, 1, stride=1, stride_axis=0)[:, :size]
        return carry

    lax.fori_loop(0, heads, head_step, 0)


def bias_tiles(rows):
    heads, count, size = rows.shape
    return pl.pallas_call(
        bias_kernel,
        out_shape=jax.ShapeDtypeStruct((heads, count - 1, size, size), F32),
        name="bias_tiles",
    )(rows)


def tile_allowed(start, query_block, key_block, size):
    lane = lax.broadcasted_iota(jnp.int32, (size, size), 1)
    row = lax.broadcasted_iota(jnp.int32, (size, size), 0)
    first = key_block * size
    return (lane >= start - first) & (lane - row <= (query_block - key_block) * size)


def forward_kernel(
    place_ref, q_ref, k_ref, v_ref, start_ref, bias_ref, att_ref, full_ref, lse_ref, s_ref
):
    groups, size, _ = q_ref.shape
    slots = k_ref.shape[0]
    inner = place_ref[0]
    stride = place_ref[1]
    full_ref[...] = jnp.zeros_like(full_ref)
    lse_ref[...] = jnp.zeros_like(lse_ref)

    def head_step(head, carry):
        for qb in range(groups):
            q_head = head_mask(q_ref[qb], head)
            start = start_ref[qb]
            query_block = qb * stride + inner

            def score_step(slot, top):
                for kb in range(qb + 1):
                    key_block = kb * stride + place_ref[2 + slot]
                    raw = dotf(q_head, k_ref[slot, kb], NT)
                    bias = bias_ref[head, jnp.maximum(query_block - key_block, 0)]
                    allowed = tile_allowed(start, query_block, key_block, size)
                    score = jnp.where(allowed, raw * 0.125 + bias, -1e30)
                    s_ref[slot, kb] = score
                    top = jnp.maximum(top, score)
                return top

            top = loop(slots, score_step, jnp.full((size, size), -1e30, F32))
            top = jnp.max(top, axis=1, keepdims=True)

            def exp_step(slot, total):
                for kb in range(qb + 1):
                    value = jnp.exp(s_ref[slot, kb] - top)
                    s_ref[slot, kb] = value
                    total = total + value
                return total

            total = loop(slots, exp_step, jnp.zeros((size, size), F32))
            total = jnp.sum(total, axis=1, keepdims=True)
            scale = 1.0 / total

            def out_step(slot, sums):
                low_sum, rest_sum = sums
                for kb in range(qb + 1):
                    prob = s_ref[slot, kb] * scale
                    prob_low = prob.astype(BF)
                    rest = (prob - prob_low.astype(F32)).astype(BF)
                    low_sum = low_sum + dotf(prob_low, v_ref[slot, kb])
                    rest_sum = rest_sum + dotf(rest, v_ref[slot, kb])
                return (low_sum, rest_sum)

            zero = jnp.zeros((size, GW), F32)
            low_sum, rest_sum = loop(slots, out_step, (zero, zero))
            low_sum = head_mask(low_sum, head)
            att_ref[qb] = jnp.where(head == 0, low_sum, att_ref[qb] + low_sum)
            full_ref[qb] += head_mask(rest_sum, head)
            lane = lax.broadcasted_iota(jnp.int32, (size, 128), 1)
            lse_ref[qb] = jnp.where(lane == head, top + jnp.log(total), lse_ref[qb])
        return carry

    lax.fori_loop(0, GHEADS, head_step, 0)
    full_ref[...] += att_ref[...]


VM = pl.BlockSpec(memory_space=pltpu.VMEM)
SM = pl.BlockSpec(memory_space=pltpu.SMEM)


def attention_forward(place, q, k, v, start, bias):
    groups, size, _ = q.shape
    slots = k.shape[0]
    return pl.pallas_call(
        forward_kernel,
        in_specs=[SM] + [VM] * 5,
        out_specs=[VM] * 3,
        out_shape=(
            jax.ShapeDtypeStruct((groups, size, GW), F32),
            jax.ShapeDtypeStruct((groups, size, GW), F32),
            jax.ShapeDtypeStruct((groups, size, 128), F32),
        ),
        scratch_shapes=[pltpu.VMEM((slots, groups, size, size), F32)],
        name="attention_forward",
    )(place, q, k, v, start, bias)


def backward_kernel(
    place_ref,
    q_ref,
    k_ref,
    v_ref,
    start_ref,
    bias_ref,
    lse_ref,
    out_grad_ref,
    delta_ref,
    dq_ref,
    dk_ref,
    dv_ref,
    dist_ref,
    dacc_ref,
):
    groups, size, _ = q_ref.shape
    slots = k_ref.shape[0]
    blocks = dacc_ref.shape[0]
    inner = place_ref[0]
    stride = place_ref[1]
    dq_ref[...] = jnp.zeros_like(dq_ref)
    dk_ref[...] = jnp.zeros_like(dk_ref)
    dv_ref[...] = jnp.zeros_like(dv_ref)

    def head_step(head, carry):
        dacc_ref[...] = jnp.zeros_like(dacc_ref)
        lane = lax.broadcasted_iota(jnp.int32, (size, 128), 1)

        def pick(ref, qb):
            return jnp.sum(jnp.where(lane == head, ref[qb], 0.0), axis=1, keepdims=True)

        log_total = [pick(lse_ref, qb) for qb in range(groups)]
        delta = [pick(delta_ref, qb) for qb in range(groups)]
        q_head = [head_mask(q_ref[qb], head) for qb in range(groups)]
        g_head = [head_mask(out_grad_ref[qb], head) for qb in range(groups)]

        def slot_step(slot, carry):
            for kb in range(groups):
                key_block = kb * stride + place_ref[2 + slot]
                key = k_ref[slot, kb]
                value = v_ref[slot, kb]
                dk = jnp.zeros((size, GW), F32)
                dv = jnp.zeros((size, GW), F32)
                for qb in range(kb, groups):
                    query_block = qb * stride + inner
                    gap = jnp.maximum(query_block - key_block, 0)
                    raw = dotf(q_head[qb], key, NT)
                    allowed = tile_allowed(start_ref[qb], query_block, key_block, size)
                    score = raw * 0.125 + bias_ref[head, gap] - log_total[qb]
                    prob = jnp.exp(jnp.where(allowed, score, -1e30))
                    prob_grad = dotf(g_head[qb], value, NT)
                    score_grad = (prob * (prob_grad - delta[qb])).astype(BF)
                    dacc_ref[gap] += score_grad.astype(F32)
                    dq_ref[qb] += head_mask(dotf(score_grad, key), head)
                    dk = dk + dotf(score_grad, q_head[qb], TN)
                    dv = dv + dotf(prob.astype(BF), g_head[qb], TN)
                dk_ref[slot, kb] += dk
                dv_ref[slot, kb] += dv
            return carry

        loop(slots, slot_step, 0)

        def dist_step(gap, carry):
            row = lax.broadcasted_iota(jnp.int32, (size, size), 0)
            lane = lax.broadcasted_iota(jnp.int32, (size, size), 1)
            flip = (row + lane == size - 1).astype(F32)
            tile = jnp.dot(flip, dacc_ref[gap], precision=HIGHEST)
            wide = jnp.concatenate((tile, jnp.zeros_like(tile)), axis=1)
            wide = pltpu.roll(wide, 1, 1, stride=1, stride_axis=0)
            dist_ref[head, pl.ds(gap, 1), :] = jnp.sum(wide, axis=0, keepdims=True)
            return carry

        lax.fori_loop(0, blocks, dist_step, 0)
        return carry

    lax.fori_loop(0, GHEADS, head_step, 0)


def attention_backward(place, q, k, v, start, bias, lse, out_grad, delta):
    groups, size, _ = q.shape
    slots = k.shape[0]
    blocks = bias.shape[1]
    return pl.pallas_call(
        backward_kernel,
        in_specs=[SM] + [VM] * 8,
        out_specs=[VM] * 4,
        out_shape=(
            jax.ShapeDtypeStruct((groups, size, GW), F32),
            jax.ShapeDtypeStruct((slots, groups, size, GW), F32),
            jax.ShapeDtypeStruct((slots, groups, size, GW), F32),
            jax.ShapeDtypeStruct((GHEADS, blocks, 2 * size), F32),
        ),
        scratch_shapes=[pltpu.VMEM((blocks, size, size), F32)],
        name="attention_backward",
    )(place, q, k, v, start, bias, lse, out_grad, delta)


def swap(value, axis):
    return lax.ppermute(value, axis, [(0, 1), (1, 0)])


def in_order(own, other, index):
    return jnp.where(
        index == 0, jnp.stack((own, other)), jnp.stack((other, own))
    )


def exchange(value, axes):
    return lax.all_to_all(value, axes, split_axis=0, concat_axis=0, tiled=True)


def rep_gather(value, y, c):
    pair = in_order(value, swap(value, "y"), y)
    both = in_order(pair, swap(pair, "c"), c)
    return jnp.swapaxes(both, 0, 1)


def rep_reduce(value, y, c):
    own = lax.dynamic_index_in_dim(value, c, -3, keepdims=False)
    theirs = lax.dynamic_index_in_dim(value, 1 - c, -3, keepdims=False)
    own = own + swap(theirs.astype(BF), "c").astype(F32)
    mine = lax.dynamic_index_in_dim(own, y, -3, keepdims=False)
    away = lax.dynamic_index_in_dim(own, 1 - y, -3, keepdims=False)
    return mine + swap(away.astype(BF), "y").astype(F32)


def norm_forward(value, gain):
    rate = lax.rsqrt(jnp.mean(value * value, axis=-1, keepdims=True) + EPS)
    unit = value * rate
    return unit * gain, unit, rate


def norm_backward(grad, gain, unit, rate):
    scaled = grad * gain
    inner = jnp.mean(scaled * unit, axis=-1, keepdims=True)
    return rate * (scaled - unit * inner)


def gelu_parts(hidden):
    inner = math.sqrt(2.0 / math.pi) * (hidden + 0.044715 * hidden * hidden * hidden)
    slope = math.sqrt(2.0 / math.pi) * (1.0 + 3 * 0.044715 * hidden * hidden)
    bend = jnp.tanh(inner)
    value = 0.5 * hidden * (1.0 + bend)
    grad = 0.5 * (1.0 + bend) + 0.5 * hidden * (1.0 - bend * bend) * slope
    return value, grad


def local(
    tokens,
    cotangent,
    gain_attn,
    gain_mlp,
    w_qkv,
    w_attn_out,
    router,
    rel_table,
    w_in,
    w_out,
    segment_ids,
    expert_ids,
    rel_bucket,
):
    groups, inner = lax.axis_size("g"), lax.axis_size("i")
    g, i = lax.axis_index("g"), lax.axis_index("i")
    y, c = lax.axis_index("y"), lax.axis_index("c")
    ranks = groups * inner
    copies = 4
    size = tokens.shape[1]
    length = size * ranks
    experts = ranks
    capacity = max(2, 4 * size // experts)
    inputs = tokens[0]
    upstream = cotangent[0]
    seg_all = segment_ids[0]
    chosen_ids = expert_ids[0]
    rows = w_qkv.shape[0] // copies
    me = g * inner + i

    normed_one, unit_one, rate_one = norm_forward(inputs, gain_attn)
    h_attn = normed_one.astype(BF)
    h_col = exchange(jnp.broadcast_to(h_attn[None], (groups, size, D)), "g")

    first = (y * 2 + c) * rows
    part = lax.dynamic_slice_in_dim(w_qkv, first, rows, 0).astype(BF)
    part = part.reshape(rows, 3, groups, GW).transpose(2, 1, 0, 3)
    part = jnp.broadcast_to(part[:, None], (groups, inner, 3, rows, GW))
    part = exchange(part.reshape(ranks, 3, rows, GW), SEQ)
    part = rep_gather(part, y, c)
    w_cols = part.transpose(3, 2, 0, 1, 4, 5).reshape(3, D, GW)

    q = dotf(h_col.reshape(groups * size, D), w_cols[0]).astype(BF)
    k = dotf(h_col.reshape(groups * size, D), w_cols[1]).astype(BF)
    v = dotf(h_col.reshape(groups * size, D), w_cols[2]).astype(BF)
    q = q.reshape(groups, size, GW)
    kv = jnp.stack((k, v)).reshape(2, groups, size, GW)
    if inner == 2:
        kv_all = jnp.stack((kv, swap(kv, "i")))
        slot_places = jnp.stack((i, 1 - i))
    else:
        kv_all = lax.all_gather(kv, "i")
        slot_places = jnp.arange(inner, dtype=jnp.int32)
    k_all, v_all = kv_all[:, 0], kv_all[:, 1]
    place = jnp.concatenate(
        (jnp.stack((i, jnp.int32(inner))), slot_places)
    ).astype(jnp.int32)

    seg_col = lax.dynamic_index_in_dim(
        seg_all.reshape(groups, inner, size), i, 1, keepdims=False
    )
    start = jnp.sum(
        (seg_all[None, None, :] < seg_col[:, :, None]).astype(jnp.int32), axis=-1, keepdims=True
    )
    padded = jnp.concatenate(
        (jnp.full((size - 1,), -1, jnp.int32), rel_bucket, jnp.full((1,), -1, jnp.int32))
    )
    reversed_bucket = padded.reshape(ranks + 1, size)[:, ::-1].reshape(-1)
    bucket_hot = (
        jnp.arange(BUCKETS, dtype=jnp.int32)[:, None] == reversed_bucket[None, :]
    ).astype(F32)
    table = lax.dynamic_slice_in_dim(rel_table, g * GHEADS, GHEADS, 0)
    bias_rows = jnp.dot(table, bucket_hot, precision=HIGHEST).reshape(GHEADS, ranks + 1, size)
    bias = bias_tiles(bias_rows)

    mixed, rest, lse = attention_forward(place, q, k_all, v_all, start, bias)
    mixed_full = rest
    attended = exchange(mixed.astype(BF), "g")

    both = jnp.concatenate((w_attn_out, jnp.pad(router, ((0, 0), (0, 128 - experts)))), axis=1)
    both = lax.dynamic_slice_in_dim(both, first, rows, 0).astype(BF)
    both = exchange(jnp.broadcast_to(both[None], (ranks, rows, D + 128)), SEQ)
    both = rep_gather(both, y, c)
    both = both.transpose(2, 0, 1, 3, 4).reshape(D, D + 128)
    w_attn_low = both[:, :D].reshape(groups, GW, D)
    router_low = both[:, D : D + experts]

    residual = inputs + jnp.einsum(
        "gtd,gde->te", attended, w_attn_low, preferred_element_type=F32
    )
    normed_two, unit_two, rate_two = norm_forward(residual, gain_mlp)
    h_mlp = normed_two.astype(BF)

    expert_iota = jnp.arange(experts, dtype=jnp.int32)
    flat_ids = chosen_ids.reshape(size * 2)
    flat_hot = (flat_ids[:, None] == expert_iota[None, :]).astype(jnp.int32)
    earlier = jnp.dot(
        (jnp.arange(2 * size)[:, None] > jnp.arange(2 * size)[None, :]).astype(BF),
        flat_hot.astype(BF),
        preferred_element_type=F32,
    ).astype(jnp.int32)
    slot_index = jnp.sum(earlier * flat_hot, axis=1)
    target_slot = flat_ids * capacity + slot_index
    route_hot = (
        target_slot[:, None] == jnp.arange(experts * capacity, dtype=jnp.int32)[None, :]
    ).astype(BF)
    route_hot = route_hot.reshape(size, 2, experts * capacity)
    other_hot = flat_hot.reshape(size, 2, experts)[:, ::-1].astype(BF)
    other_hot = jnp.pad(other_hot, ((0, 0), (0, 0), (0, 128 - experts)))
    early = jnp.concatenate(
        (jnp.broadcast_to(upstream.astype(BF)[:, None], (size, 2, D)), other_hot), axis=2
    )
    sent_early = jnp.einsum("tke,tkd->ed", route_hot, early, preferred_element_type=F32).astype(BF)
    came = exchange(sent_early.reshape(ranks, capacity, D + 128), SEQ)
    came = came.reshape(ranks * capacity, D + 128)
    up_rows = came[:, :D]
    other_rows = came[:, D : D + experts]

    outgoing = jnp.einsum("tke,td->ed", route_hot, h_mlp, preferred_element_type=F32).astype(BF)
    arrived = exchange(outgoing.reshape(ranks, capacity, D), SEQ).reshape(ranks * capacity, D)

    row_logits = jnp.dot(arrived, router_low, preferred_element_type=F32)
    own_hot = (expert_iota[None, :] == me).astype(F32)
    other_f = other_rows.astype(F32)
    own_logit = jnp.sum(row_logits * own_hot, axis=1, keepdims=True)
    other_logit = jnp.sum(row_logits * other_f, axis=1, keepdims=True)
    peak = jnp.maximum(own_logit, other_logit)
    own_e, other_e = jnp.exp(own_logit - peak), jnp.exp(other_logit - peak)
    own_gate = own_e / (own_e + other_e)
    other_gate = other_e / (own_e + other_e)

    hidden = jnp.dot(arrived, w_in[0], preferred_element_type=F32)
    active, slope = gelu_parts(hidden)
    active = active.astype(BF)
    produced = jnp.dot(active, w_out[0], preferred_element_type=F32).astype(BF)
    up_f = up_rows.astype(F32)
    produced_grad = (own_gate * up_f).astype(BF)
    gate_grad = jnp.sum(up_f * produced.astype(F32), axis=1, keepdims=True)
    active_grad = dotf(produced_grad, w_out[0], NT)
    hidden_grad = (slope * active_grad).astype(BF)
    row_grad = dotf(hidden_grad, w_in[0], NT).astype(BF).astype(F32)
    pull = own_gate * other_gate * gate_grad
    logit_rows = pull * (own_hot - other_f)
    row_grad = row_grad + dotf(logit_rows.astype(BF), router_low, NT)
    logit_rest = logit_rows - logit_rows.astype(BF).astype(F32)
    row_grad = row_grad + dotf(logit_rest.astype(BF), router_low, NT)
    back_rows = exchange(row_grad.astype(BF).reshape(ranks, capacity, D), SEQ)
    back_rows = back_rows.reshape(ranks * capacity, D)
    returned = exchange(produced.reshape(ranks, capacity, D), SEQ).reshape(ranks * capacity, D)

    w_in_grad = dotf(arrived, hidden_grad, TN)
    w_out_grad = dotf(active, produced_grad, TN)
    w_in_shard = rep_reduce(w_in_grad.reshape(D, 2, 2, FF // 4).transpose(1, 2, 0, 3), y, c)
    w_out_shard = rep_reduce(w_out_grad.reshape(2, 2, FF // 4, D), y, c)
    router_grad = dotf(arrived, logit_rows.astype(BF), TN) + dotf(
        arrived, logit_rest.astype(BF), TN
    )

    logits = jnp.dot(h_mlp, router_low, preferred_element_type=F32)
    picked = flat_hot.reshape(size, 2, experts).astype(F32)
    gates = jax.nn.softmax(jnp.sum(logits[:, None, :] * picked, axis=-1), axis=-1)
    expert_rows = jnp.einsum("tke,ed->tkd", route_hot, returned, preferred_element_type=F32)
    result = residual + jnp.sum(gates[:, :, None] * expert_rows, axis=1)

    mlp_grad = jnp.einsum("tke,ed->td", route_hot, back_rows, preferred_element_type=F32)
    gain_two = jnp.sum(mlp_grad * unit_two, axis=0)
    resid_grad = upstream + norm_backward(mlp_grad, gain_mlp, unit_two, rate_two)
    attn_grad = resid_grad.astype(BF)
    out_grad = jnp.einsum("te,gde->gtd", attn_grad, w_attn_low, preferred_element_type=F32)
    out_grad = exchange(out_grad.astype(BF), "g")
    attn_out_grad = jnp.einsum("gtd,te->gde", attended, attn_grad, preferred_element_type=F32)

    delta = out_grad.astype(F32) * mixed_full
    delta = jnp.sum(delta.reshape(groups, size, GHEADS, HEAD), axis=-1)
    delta = jnp.pad(delta, ((0, 0), (0, 0), (0, 128 - GHEADS)))
    dq, dk, dv, dist = attention_backward(
        place, q, k_all, v_all, start, bias, lse, out_grad, delta
    )
    dkv = jnp.stack((dk, dv), axis=1)
    if inner == 2:
        dkv = dkv[0] + swap(dkv[1].astype(BF), "i").astype(F32)
    else:
        dkv = lax.psum_scatter(dkv, "i")
    grads = jnp.concatenate((dq[None], dkv))
    dproj = (grads * jnp.array([0.125, 0.125, 1.0], F32)[:, None, None, None]).astype(BF)
    dproj = dproj.reshape(3, groups * size, GW)
    half = jnp.einsum("pte,pde->td", dproj, w_cols, preferred_element_type=F32)
    ratio = h_col.reshape(groups * size, D).astype(F32) / gain_attn
    gain_one = jnp.sum(half * ratio, axis=0)
    pieces = exchange(half.astype(BF).reshape(groups, size, D), "g")
    norm_in_grad = jnp.sum(pieces.astype(F32), axis=0)
    input_grad = resid_grad + norm_backward(norm_in_grad, gain_attn, unit_one, rate_one)

    qkv_grad = jnp.einsum(
        "td,pte->dpe", h_col.reshape(groups * size, D), dproj, preferred_element_type=F32
    ).reshape(ranks, 2, 2, rows, 3 * GW)
    qkv_part = rep_reduce(qkv_grad, y, c)
    qkv_part = exchange(qkv_part.astype(BF), SEQ).reshape(groups, inner, rows, 3, GW)
    qkv_part = jnp.sum(qkv_part.astype(F32), axis=1)
    qkv_part = qkv_part.transpose(1, 2, 0, 3).reshape(rows, 3 * D)
    qkv_shard = rep_gather(qkv_part.astype(BF), y, c).reshape(copies * rows, 3 * D).astype(F32)

    side_grad = jnp.concatenate(
        (
            attn_out_grad.reshape(D, D),
            jnp.pad(router_grad, ((0, 0), (0, 128 - experts))),
        ),
        axis=1,
    ).reshape(ranks, 2, 2, rows, D + 128)
    side_part = rep_reduce(side_grad, y, c)
    side_part = exchange(side_part.astype(BF), SEQ)
    side_part = jnp.sum(side_part.astype(F32), axis=0)
    side_shard = rep_gather(side_part.astype(BF), y, c).reshape(copies * rows, D + 128)
    side_shard = side_shard.astype(F32)
    attn_shard, router_shard = side_shard[:, :D], side_shard[:, D : D + experts]

    dist_rows = jnp.pad(dist[:, :, size:], ((0, 0), (0, 1), (0, 0))) + jnp.pad(
        dist[:, :, :size], ((0, 0), (1, 0), (0, 0))
    )
    table_grad = jnp.dot(dist_rows.reshape(GHEADS, -1), bucket_hot.T, precision=HIGHEST)
    table_all = lax.dynamic_update_slice(
        jnp.zeros((HEADS, BUCKETS), F32), table_grad, (g * GHEADS, 0)
    )
    small = jnp.concatenate((gain_one, gain_two, table_all.reshape(-1)))
    small = jnp.pad(small, (0, 2048 - small.shape[0])).reshape(1, 16, 128)
    small = exchange(
        jnp.broadcast_to(small, (copies * ranks, 16, 128)), REP + SEQ
    )
    small = jnp.sum(small, axis=0).reshape(-1)
    return (
        result[None],
        input_grad[None],
        small[:D],
        small[D : 2 * D],
        qkv_shard,
        attn_shard,
        router_shard,
        small[2 * D : 2 * D + HEADS * BUCKETS].reshape(HEADS, BUCKETS),
        w_in_shard[None],
        w_out_shard[None],
    )


def solution(mesh):
    ranks = mesh.shape["seq"]
    split = Mesh(
        mesh.devices.reshape(2, mesh.shape["rep"] // 2, GROUPS, ranks // GROUPS),
        ("y", "c", "g", "i"),
    )
    placed = (
        P(REP, SEQ, None),
        P(REP, SEQ, None),
        P(),
        P(),
        P(SEQ, None),
        P(SEQ, None),
        P(SEQ, None),
        P(),
        P(SEQ, None, None),
        P(SEQ, None, None),
        P(REP, None),
        P(REP, SEQ, None),
        P(),
    )
    return jax.shard_map(
        local,
        mesh=split,
        in_specs=placed,
        out_specs=(
            P(REP, SEQ, None),
            P(REP, SEQ, None),
            P(),
            P(),
            P(SEQ, None),
            P(SEQ, None),
            P(SEQ, None),
            P(),
            P(SEQ, None, REP),
            P(SEQ, REP, None),
        ),
        check_vma=False,
    )
```

```python
from functools import partial
import math

import jax
import jax.numpy as jnp
from jax import lax
from jax.experimental import pallas as pl
from jax.experimental.pallas import tpu as pltpu
from jax.sharding import Mesh, PartitionSpec as P

D = 768
HEADS = 12
HEAD = 64
BUCKETS = 32
FF = 3072
GROUPS = 4
GHEADS = HEADS // GROUPS
GW = GHEADS * HEAD
EPS = 1e-06
HIGHEST = lax.Precision.HIGHEST
BF = jnp.bfloat16
F32 = jnp.float32
NT = (((1,), (1,)), ((), ()))
TN = (((0,), (0,)), ((), ()))
SEQ = ("g", "i")
REP = ("y", "c")


def dotf(a, b, dims=(((1,), (0,)), ((), ()))):
    return lax.dot_general(a, b, dims, preferred_element_type=F32)


def loop(count, body, init):
    if count <= 2:
        for step in range(count):
            init = body(step, init)
        return init
    return lax.fori_loop(0, count, body, init)


def ahead(block, own, count):
    return lax.rem(block + count - own, count)


def behind(step, own, count):
    return lax.rem(own + count - step, count)


def heads_apart(value, scale):
    lane = lax.broadcasted_iota(jnp.int32, value.shape, 1)
    value = value * jnp.asarray(scale, value.dtype)
    return jnp.concatenate(
        [jnp.where(lane // HEAD == head, value, jnp.zeros_like(value)) for head in range(GHEADS)],
        axis=0,
    )


def heads_beside(value, size):
    return jnp.concatenate(
        [value[head * size : (head + 1) * size] for head in range(GHEADS)], axis=1
    )


def tile_mask(start, query_block, key_block, size):
    lane = lax.broadcasted_iota(jnp.int32, (size, size), 1)
    row = lax.broadcasted_iota(jnp.int32, (size, size), 0)
    allowed = (lane >= start - key_block * size) & (
        lane - row <= (query_block - key_block) * size
    )
    return jnp.where(allowed, 0.0, -1e30)


def bias_kernel(rows_ref, tiles_ref):
    heads, inner, count, size, _ = tiles_ref.shape

    def head_step(head, carry):
        for part in range(inner):
            tiles_ref[head, part, 0] = jnp.zeros((size, size), F32)
            for step in range(count - 1):
                gap = step * inner + part
                pair = jnp.concatenate(
                    (rows_ref[head, gap : gap + 1, :], rows_ref[head, gap + 1 : gap + 2, :]),
                    axis=1,
                )
                spread = jnp.broadcast_to(pair, (size, 2 * size))
                spread = pltpu.roll(spread, 0, 1, stride=1, stride_axis=0)
                tiles_ref[head, part, step + 1] = spread[:, :size]
        return carry

    lax.fori_loop(0, heads, head_step, 0)


def cost(us):
    return pl.CostEstimate(flops=0, bytes_accessed=int(us * 3.4e6), transcendentals=0)


def bias_tiles(rows, inner):
    heads, count, size = rows.shape
    return pl.pallas_call(
        bias_kernel,
        out_shape=jax.ShapeDtypeStruct((heads, inner, (count - 1) // inner + 1, size, size), F32),
        cost_estimate=cost(0.05),
        name="bias_tiles",
    )(rows)


def block_of(kv_refs, slot, kb):
    if len(kv_refs) == 1:
        return kv_refs[0][slot, kb]
    return kv_refs[slot][kb]


def bias_place(place_ref, slot):
    shift = place_ref[0] - place_ref[2 + slot]
    below = (shift < 0).astype(jnp.int32)
    return shift + below * place_ref[1], 1 - below


def forward_kernel(
    place_ref,
    q_ref,
    *refs,
):
    groups, size, _ = q_ref.shape
    kv_refs, (start_ref, bias_ref, out_ref, full_ref, lse_ref, s_ref, vs_ref) = refs[:-7], refs[-7:]
    slots = s_ref.shape[0]
    tall = GHEADS * size

    def spread_step(slot, carry):
        for kb in range(groups):
            vs_ref[slot, kb] = heads_apart(block_of(kv_refs, slot, kb)[:, GW:], 1)
        return carry

    loop(slots, spread_step, 0)
    for qb in range(groups):
        queries = heads_apart(q_ref[qb], 0.125)
        start = start_ref[qb]
        query_block = qb * place_ref[1] + place_ref[0]

        def score_step(slot, top):
            part, tile = bias_place(place_ref, slot)
            for kb in range(qb + 1):
                key_block = kb * place_ref[1] + place_ref[2 + slot]
                mask = tile_mask(start, query_block, key_block, size)
                raw = dotf(queries, block_of(kv_refs, slot, kb)[:, :GW], NT)
                bias = [bias_ref[head, part, tile + qb - kb] + mask for head in range(GHEADS)]
                score = raw + jnp.concatenate(bias, axis=0)
                s_ref[slot, kb] = score
                top = jnp.maximum(top, score)
            return top

        top = loop(slots, score_step, jnp.full((tall, size), -1e30, F32))
        top = jnp.broadcast_to(jnp.max(top, axis=1, keepdims=True), (tall, size))

        def exp_step(slot, total):
            for kb in range(qb + 1):
                value = jnp.exp(s_ref[slot, kb] - top)
                s_ref[slot, kb] = value
                total = total + value
            return total

        total = loop(slots, exp_step, jnp.zeros((tall, size), F32))
        total = jnp.broadcast_to(jnp.sum(total, axis=1, keepdims=True), (tall, size))
        scale = 1.0 / total
        lse_ref[qb] = top + jnp.log(total)

        def out_step(slot, sums):
            low_sum, rest_sum = sums
            for kb in range(qb + 1):
                prob = s_ref[slot, kb] * scale
                prob_low = prob.astype(BF)
                rest = (prob - prob_low.astype(F32)).astype(BF)
                values = vs_ref[slot, kb]
                low_sum = low_sum + dotf(heads_beside(prob_low, size), values)
                rest_sum = rest_sum + dotf(heads_beside(rest, size), values)
            return (low_sum, rest_sum)

        zero = jnp.zeros((size, GW), F32)
        low_sum, rest_sum = loop(slots, out_step, (zero, zero))
        full_ref[qb] = low_sum + rest_sum
        out_ref[qb] = low_sum.astype(BF)


VM = pl.BlockSpec(memory_space=pltpu.VMEM)
SM = pl.BlockSpec(memory_space=pltpu.SMEM)


def attention_forward(place, q, kv, start, bias):
    groups, size, _ = q.shape
    slots = kv[0].shape[0] if len(kv) == 1 else len(kv)
    return pl.pallas_call(
        forward_kernel,
        in_specs=[SM] + [VM] * (3 + len(kv)),
        out_specs=[VM] * 3,
        out_shape=(
            jax.ShapeDtypeStruct((groups, size, GW), BF),
            jax.ShapeDtypeStruct((groups, size, GW), F32),
            jax.ShapeDtypeStruct((groups, GHEADS * size, size), F32),
        ),
        scratch_shapes=[
            pltpu.VMEM((slots, groups, GHEADS * size, size), F32),
            pltpu.VMEM((slots, groups, GHEADS * size, GW), BF),
        ],
        cost_estimate=cost(0.05),
        name="attention_forward",
    )(place, q, *kv, start, bias)


def backward_kernel(
    place_ref,
    q_ref,
    kv_ref,
    start_ref,
    bias_ref,
    lse_ref,
    full_ref,
    out_grad_ref,
    dq_ref,
    dkv_ref,
    dist_ref,
    dist_acc,
    qs_ref,
    gs_ref,
    delta_ref,
    p_ref,
    ds_ref,
):
    groups, size, _ = q_ref.shape
    slots = kv_ref.shape[0]
    tall = GHEADS * size
    for block in range(groups):
        spread = heads_apart(out_grad_ref[block], 1)
        gs_ref[block] = spread
        full = full_ref[block]
        product = spread.astype(F32) * jnp.concatenate([full] * GHEADS, axis=0)
        delta = jnp.sum(product, axis=1, keepdims=True)
        delta_ref[block] = jnp.broadcast_to(delta, (tall, size))
    for qb in range(groups):
        qs_ref[qb] = heads_apart(q_ref[qb], 0.125)
    dq_ref[...] = jnp.zeros_like(dq_ref)

    def slot_step(slot, carry):
        dist_acc[...] = jnp.zeros_like(dist_acc)
        part, tile = bias_place(place_ref, slot)
        for kb in range(groups):
            key_block = kb * place_ref[1] + place_ref[2 + slot]
            key, value = kv_ref[slot, kb][:, :GW], kv_ref[slot, kb][:, GW:]
            keys = heads_apart(key, 0.125)
            for qb in range(kb, groups):
                query_block = qb * place_ref[1] + place_ref[0]
                mask = tile_mask(start_ref[qb], query_block, key_block, size)
                at = tile + qb - kb
                bias = [bias_ref[head, part, at] + mask for head in range(GHEADS)]
                raw = dotf(qs_ref[qb], key, NT)
                prob_grad = dotf(gs_ref[qb], value, NT)
                prob = jnp.exp(raw + (jnp.concatenate(bias, axis=0) - lse_ref[qb]))
                score_grad = (prob * (prob_grad - delta_ref[qb])).astype(BF)
                p_ref[qb] = prob.astype(BF)
                ds_ref[qb] = score_grad
                for head in range(GHEADS):
                    dist_acc[head, at] += score_grad[
                        head * size : (head + 1) * size
                    ].astype(F32)
                dq_ref[qb] += dotf(heads_beside(score_grad, size), keys)
            count = (groups - kb) * tall
            dk = dotf(ds_ref[kb:].reshape(count, size), qs_ref[kb:].reshape(count, GW), TN)
            dv = dotf(p_ref[kb:].reshape(count, size), gs_ref[kb:].reshape(count, GW), TN)
            dkv_ref[slot, kb] = jnp.concatenate((dk, dv), axis=1).astype(dkv_ref.dtype)
        row = lax.broadcasted_iota(jnp.int32, (size, size), 0)
        lane = lax.broadcasted_iota(jnp.int32, (size, size), 1)
        flip = (row + lane == size - 1).astype(F32)
        for head in range(GHEADS):
            tiles = jnp.concatenate(
                [dist_acc[head, step] for step in range(groups + 1)], axis=1
            )
            tiles = jnp.dot(flip, tiles, precision=HIGHEST)
            for step in range(groups + 1):
                tile_rows = tiles[:, step * size : (step + 1) * size]
                wide = jnp.concatenate((tile_rows, jnp.zeros_like(tile_rows)), axis=1)
                wide = pltpu.roll(wide, 1, 1, stride=1, stride_axis=0)
                dist_ref[slot, head, step : step + 1, :] = jnp.sum(wide, axis=0, keepdims=True)
        return carry

    loop(slots, slot_step, 0)


def attention_backward(place, q, kv, start, bias, lse, full, out_grad, dtype):
    groups, size, _ = q.shape
    slots = kv.shape[0]
    tall = GHEADS * size
    return pl.pallas_call(
        backward_kernel,
        in_specs=[SM] + [VM] * 7,
        out_specs=[VM] * 3,
        out_shape=(
            jax.ShapeDtypeStruct((groups, size, GW), F32),
            jax.ShapeDtypeStruct((slots, groups, size, 2 * GW), dtype),
            jax.ShapeDtypeStruct((slots, GHEADS, groups + 1, 2 * size), F32),
        ),
        scratch_shapes=[
            pltpu.VMEM((GHEADS, groups + 1, size, size), F32),
            pltpu.VMEM((groups, tall, GW), BF),
            pltpu.VMEM((groups, tall, GW), BF),
            pltpu.VMEM((groups, tall, size), F32),
            pltpu.VMEM((groups, tall, size), BF),
            pltpu.VMEM((groups, tall, size), BF),
        ],
        cost_estimate=cost(0.05),
        name="attention_backward",
    )(place, q, kv, start, bias, lse, full, out_grad)


def project_kernel(own_ref, h0_ref, h1_ref, h2_ref, h3_ref, w_ref, q_ref, kv_ref, h_ref):
    groups, size, _ = h_ref.shape
    for step, piece_ref in enumerate((h0_ref, h1_ref, h2_ref, h3_ref)):
        h_ref[behind(step, own_ref[0], groups)] = piece_ref[...]
    rows = dotf(h_ref[...].reshape(groups * size, D), w_ref[...]).astype(BF)
    q_ref[...] = rows[:, :GW].reshape(groups, size, GW)
    kv_ref[...] = rows[:, GW:].reshape(groups, size, 2 * GW)


def project(own, pieces, w_cols):
    size = pieces[0].shape[0]
    return pl.pallas_call(
        project_kernel,
        in_specs=[SM] + [VM] * 5,
        out_specs=[VM] * 3,
        out_shape=(
            jax.ShapeDtypeStruct((GROUPS, size, GW), BF),
            jax.ShapeDtypeStruct((GROUPS, size, 2 * GW), BF),
            jax.ShapeDtypeStruct((GROUPS, size, D), BF),
        ),
        cost_estimate=cost(0.05),
        name="project",
    )(own, *pieces, w_cols)


def mlp_in_kernel(
    att_ref, w_ref, x_ref, gain_ref, disp_ref, resid_ref, sent_ref
):
    total = x_ref[...]
    for group in range(GROUPS):
        total = total + dotf(att_ref[group], w_ref[group])
    resid_ref[...] = total
    rate = lax.rsqrt(jnp.mean(total * total, axis=-1, keepdims=True) + EPS)
    low = (total * rate * gain_ref[...]).astype(BF)
    sent_ref[...] = dotf(disp_ref[...], low).astype(BF)


def mlp_in(att, w_attn, x, gain, disp):
    return pl.pallas_call(
        mlp_in_kernel,
        in_specs=[VM] * 5,
        out_specs=[VM] * 2,
        out_shape=(
            jax.ShapeDtypeStruct(x.shape, F32),
            jax.ShapeDtypeStruct((disp.shape[0], D), BF),
        ),
        cost_estimate=cost(0.05),
        name="mlp_in",
    )(att, w_attn, x, gain, disp)


def expert_kernel(
    own_ref,
    x_ref,
    came_ref,
    w_in_ref,
    w_out_ref,
    router_ref,
    active_ref,
    hidden_grad_ref,
    out_grad_ref,
    back_ref,
    out_ref,
    router_grad_ref,
    out_acc,
    back_acc,
    gate_ref,
):
    step = pl.program_id(0)
    rows = x_ref[...]
    lane = lax.broadcasted_iota(jnp.int32, (rows.shape[0], 128), 1)

    @pl.when(step == 0)
    def _():
        logits = dotf(rows, router_ref[...])
        pair = came_ref[:, D:].astype(F32)
        own = jnp.sum(jnp.where(lane == own_ref[0], logits, 0.0), axis=1, keepdims=True)
        other = jnp.where(lane == own_ref[0], 0.0, pair)
        other = jnp.sum(other * logits, axis=1, keepdims=True)
        peak = jnp.maximum(own, other)
        own_e, other_e = jnp.exp(own - peak), jnp.exp(other - peak)
        total = own_e + other_e
        own_gate = own_e / total
        gate_ref[0] = jnp.broadcast_to(own_gate, lane.shape)
        gate_ref[1] = jnp.broadcast_to(other_e / total, lane.shape)
        out_grad_ref[...] = (own_gate * came_ref[:, :D].astype(F32)).astype(BF)
        out_acc[...] = jnp.zeros_like(out_acc)
        back_acc[...] = jnp.zeros_like(back_acc)

    hidden = dotf(rows, w_in_ref[...])
    active_grad = dotf(out_grad_ref[...], w_out_ref[...], NT)
    value, slope = gelu_parts(hidden)
    active = value.astype(BF)
    hidden_grad = (slope * active_grad).astype(BF)
    active_ref[...] = active
    hidden_grad_ref[...] = hidden_grad
    out_acc[...] += dotf(active, w_out_ref[...])
    back_acc[...] += dotf(hidden_grad, w_in_ref[...], NT)

    @pl.when(step == pl.num_programs(0) - 1)
    def _():
        produced = out_acc[...].astype(BF).astype(F32)
        own_gate, other_gate = gate_ref[0][:, :1], gate_ref[1][:, :1]
        out_ref[...] = (own_gate * produced).astype(BF)
        gate_grad = jnp.sum(came_ref[:, :D].astype(F32) * produced, axis=1, keepdims=True)
        pull = own_gate * other_gate * gate_grad
        pair = came_ref[:, D:].astype(F32)
        logit_rows = pull * jnp.where(lane == own_ref[0], 1.0, -pair)
        high = logit_rows.astype(BF)
        rest = (logit_rows - high.astype(F32)).astype(BF)
        router = router_ref[...]
        back = back_acc[...].astype(BF).astype(F32)
        back = back + dotf(high, router, NT) + dotf(rest, router, NT)
        back_ref[...] = back.astype(BF)
        router_grad_ref[...] = dotf(rows, high, TN) + dotf(rows, rest, TN)


def expert_layer(own, x, came, w_in, w_out, router):
    count = x.shape[0]
    steps = 4
    part = FF // steps
    whole = lambda *shape: pl.BlockSpec(shape, lambda f, own: (0,) * len(shape))
    piece = pl.BlockSpec((count, part), lambda f, own: (0, own[1 + f]))
    return pl.pallas_call(
        expert_kernel,
        grid_spec=pltpu.PrefetchScalarGridSpec(
            num_scalar_prefetch=1,
            grid=(steps,),
            in_specs=[
                whole(count, D),
                whole(count, D + 128),
                pl.BlockSpec((D, part), lambda f, own: (0, f)),
                pl.BlockSpec((part, D), lambda f, own: (f, 0)),
                whole(D, 128),
            ],
            out_specs=[
                piece,
                piece,
                whole(count, D),
                whole(count, D),
                whole(count, D),
                whole(D, 128),
            ],
            scratch_shapes=[
                pltpu.VMEM((count, D), F32),
                pltpu.VMEM((count, D), F32),
                pltpu.VMEM((2, count, 128), F32),
            ],
        ),
        out_shape=(
            jax.ShapeDtypeStruct((count, FF), BF),
            jax.ShapeDtypeStruct((count, FF), BF),
            jax.ShapeDtypeStruct((count, D), BF),
            jax.ShapeDtypeStruct((count, D), BF),
            jax.ShapeDtypeStruct((count, D), BF),
            jax.ShapeDtypeStruct((D, 128), F32),
        ),
        cost_estimate=cost(0.05),
        name="expert_layer",
    )(own, x, came, w_in, w_out, router)


def mlp_back_kernel(
    back_ref, disp_ref, resid_ref, up_ref, gain_ref, w_ref, grad_ref, low_ref, gain_grad_ref, out_ref
):
    grad = dotf(disp_ref[...], back_ref[...], TN)
    resid = resid_ref[...]
    rate = lax.rsqrt(jnp.mean(resid * resid, axis=-1, keepdims=True) + EPS)
    unit = resid * rate
    gain_grad_ref[...] = jnp.sum(grad * unit, axis=0, keepdims=True)
    scaled = grad * gain_ref[...]
    total = up_ref[...] + rate * (
        scaled - unit * jnp.mean(scaled * unit, axis=-1, keepdims=True)
    )
    grad_ref[...] = total
    low = total.astype(BF)
    low_ref[...] = low
    for group in range(GROUPS):
        out_ref[group] = dotf(low, w_ref[group], NT).astype(BF)


def mlp_back(back, disp, resid, up, gain, w_attn):
    size = resid.shape[0]
    return pl.pallas_call(
        mlp_back_kernel,
        in_specs=[VM] * 6,
        out_specs=[VM] * 4,
        out_shape=(
            jax.ShapeDtypeStruct((size, D), F32),
            jax.ShapeDtypeStruct((size, D), BF),
            jax.ShapeDtypeStruct((1, D), F32),
            jax.ShapeDtypeStruct((GROUPS, size, GW), BF),
        ),
        cost_estimate=cost(0.05),
        name="mlp_back",
    )(back, disp, resid, up, gain, w_attn)


def project_back_kernel(
    dq_ref,
    dq_other_ref,
    dkv_ref,
    came_ref,
    w_ref,
    h_ref,
    gain_ref,
    dproj_ref,
    gain_grad_ref,
    half_ref,
):
    groups, size, _ = dq_ref.shape
    dq = (dq_ref[...] + dq_other_ref[...]).astype(BF).reshape(groups * size, GW)
    dkv = (dkv_ref[...] + came_ref[...].astype(F32)).astype(BF)
    dkv = dkv.reshape(groups * size, 2 * GW)
    dproj_ref[...] = jnp.concatenate((dq, dkv), axis=1)
    total = jnp.zeros((1, D), F32)
    for block in range(groups):
        half = dotf(dproj_ref[block * size : (block + 1) * size], w_ref[...], NT)
        half_ref[block] = half.astype(BF)
        total = total + jnp.sum(half * h_ref[block].astype(F32), axis=0, keepdims=True)
    gain_grad_ref[...] = total / gain_ref[...]


def project_back(dq, dq_other, dkv, came, w_cols, h_col, gain):
    groups, size, _ = dq.shape
    return pl.pallas_call(
        project_back_kernel,
        in_specs=[VM] * 7,
        out_specs=[VM] * 3,
        out_shape=(
            jax.ShapeDtypeStruct((groups * size, 3 * GW), BF),
            jax.ShapeDtypeStruct((1, D), F32),
            jax.ShapeDtypeStruct((groups, size, D), BF),
        ),
        cost_estimate=cost(0.05),
        name="project_back",
    )(dq, dq_other, dkv, came, w_cols, h_col, gain)


def qkv_grad_kernel(h_ref, dproj_ref, grad_ref):
    ranks, rows, _ = grad_ref.shape
    groups, size, _ = h_ref.shape
    total = dotf(h_ref[...].reshape(groups * size, D), dproj_ref[...], TN)
    for rank in range(ranks):
        grad_ref[rank] = total[rank * rows : (rank + 1) * rows]


def qkv_grad_of(h_col, dproj, ranks):
    return pl.pallas_call(
        qkv_grad_kernel,
        in_specs=[VM] * 2,
        out_specs=VM,
        out_shape=jax.ShapeDtypeStruct((ranks, D // ranks, 3 * GW), F32),
        cost_estimate=cost(0.05),
        name="qkv_grad",
    )(h_col, dproj)


def side_grad_kernel(att_ref, grad_ref, router_ref, out_ref):
    ranks, rows, _ = out_ref.shape
    inner = ranks // GROUPS
    for block in range(GROUPS):
        total = dotf(att_ref[block], grad_ref[...], TN)
        for part in range(inner):
            out_ref[block * inner + part, :, :D] = total[part * rows : (part + 1) * rows]
    for rank in range(ranks):
        out_ref[rank, :, D:] = router_ref[rank * rows : (rank + 1) * rows]


def side_grad_of(att, grad, router_grad, ranks):
    return pl.pallas_call(
        side_grad_kernel,
        in_specs=[VM] * 3,
        out_specs=VM,
        out_shape=jax.ShapeDtypeStruct((ranks, D // ranks, D + 128), F32),
        cost_estimate=cost(0.05),
        name="side_grad",
    )(att, grad, router_grad)


def gelu_parts(hidden):
    scale = math.sqrt(2.0 / math.pi)
    square = hidden * hidden
    bend = jnp.tanh(hidden * (scale + (scale * 0.044715) * square))
    half = 0.5 + 0.5 * bend
    slope = scale + (3 * scale * 0.044715) * square
    return hidden * half, half + (0.5 * hidden) * (1.0 - bend * bend) * slope


def swap(value, axis):
    return lax.ppermute(value, axis, [(0, 1), (1, 0)])


def after(value, *others):
    return lax.optimization_barrier((value,) + others)[0]


def turn(value, step):
    return lax.ppermute(value, "g", [(j, (j + step) % GROUPS) for j in range(GROUPS)])


def exchange(value, axes):
    return lax.all_to_all(value, axes, split_axis=0, concat_axis=0, tiled=True)


def rep_gather(value, y, c):
    pair = jnp.stack((value, swap(value, "y")))
    both = jnp.stack((pair, swap(pair, "c")), axis=1)
    both = jnp.where(y == 0, both, both[::-1])
    return jnp.where(c == 0, both, both[:, ::-1])


def pick(value, index, axis):
    return lax.dynamic_index_in_dim(value, index, axis, keepdims=False)


def norm_backward(grad, gain, value):
    rate = lax.rsqrt(jnp.mean(value * value, axis=-1, keepdims=True) + EPS)
    unit = value * rate
    scaled = grad * gain
    return rate * (scaled - unit * jnp.mean(scaled * unit, axis=-1, keepdims=True))


def local(
    tokens,
    cotangent,
    gain_attn,
    gain_mlp,
    w_qkv,
    w_attn_out,
    router,
    rel_table,
    w_in,
    w_out,
    segment_ids,
    expert_ids,
    rel_bucket,
):
    groups, inner = lax.axis_size("g"), lax.axis_size("i")
    g, i = lax.axis_index("g"), lax.axis_index("i")
    y, c = lax.axis_index("y"), lax.axis_index("c")
    ranks = groups * inner
    copies = 4
    size = tokens.shape[1]
    experts = ranks
    capacity = max(2, 4 * size // experts)
    inputs = tokens[0]
    upstream = cotangent[0]
    seg_all = segment_ids[0]
    chosen_ids = expert_ids[0]
    rows = w_qkv.shape[0] // copies
    me = g * inner + i
    own_g = g[None].astype(jnp.int32)

    rate = lax.rsqrt(jnp.mean(inputs * inputs, axis=-1, keepdims=True) + EPS)
    h_attn = (inputs * rate * gain_attn).astype(BF)
    h_pieces = [h_attn] + [turn(h_attn, step) for step in range(1, groups)]

    first = (y * 2 + c) * rows
    part = lax.dynamic_slice_in_dim(w_qkv, first, rows, 0).astype(BF)
    part = part.reshape(rows, 3, groups, GW).transpose(2, 0, 1, 3)
    part = jnp.broadcast_to(part[:, None], (groups, inner, rows, 3, GW))
    both = jnp.concatenate((w_attn_out, jnp.pad(router, ((0, 0), (0, 128 - experts)))), axis=1)
    both = lax.dynamic_slice_in_dim(both, first, rows, 0).astype(BF)
    both = jnp.broadcast_to(both[None], (ranks, rows, D + 128))
    weights = jnp.concatenate((both, part.reshape(ranks, rows, 3 * GW)), axis=2)
    weights = exchange(weights, SEQ)
    weights, *h_pieces = lax.optimization_barrier((weights, *h_pieces))
    chosen_ids, seg_all, table_rows = lax.optimization_barrier(
        (chosen_ids, seg_all, rel_table, h_pieces[1], h_pieces[2], h_pieces[3])
    )[:3]
    w_cols = rep_gather(weights[:, :, D + 128 :], y, c)
    w_cols = w_cols.transpose(2, 0, 1, 3, 4).reshape(D, 3 * GW)
    both = rep_gather(weights[:, :, : D + 128], y, c)
    both = both.transpose(2, 0, 1, 3, 4).reshape(D, D + 128)
    w_attn_low = both[:, :D].reshape(groups, GW, D)
    router_low = both[:, D:]

    expert_iota = jnp.arange(experts, dtype=jnp.int32)
    token_iota = jnp.arange(size, dtype=jnp.int32)
    pair_hot = jnp.any(chosen_ids[:, :, None] == expert_iota[None, None, :], axis=1)
    rank = jnp.dot(
        (token_iota[:, None] > token_iota[None, :]).astype(BF),
        pair_hot.astype(BF),
        preferred_element_type=F32,
    ).astype(jnp.int32)
    disp = (rank.T[:, None, :] == jnp.arange(capacity, dtype=jnp.int32)[None, :, None]) & (
        pair_hot.T[:, None, :]
    )
    disp = disp.astype(BF).reshape(experts * capacity, size)
    early = jnp.concatenate(
        (upstream.astype(BF), jnp.pad(pair_hot.astype(BF), ((0, 0), (0, 128 - experts)))), axis=1
    )
    early = jnp.dot(disp, early, preferred_element_type=F32).astype(BF)
    seg_col = pick(seg_all.reshape(groups, inner, size), i, 1)
    start = jnp.sum(
        (seg_all[None, None, :] < seg_col[:, :, None]).astype(jnp.int32), axis=-1, keepdims=True
    )
    padded = jnp.concatenate(
        (jnp.full((size - 1,), -1, jnp.int32), rel_bucket, jnp.full((1,), -1, jnp.int32))
    )
    reversed_bucket = padded.reshape(ranks + 1, size)[:, ::-1].reshape(-1)
    bucket_hot = (
        jnp.arange(BUCKETS, dtype=jnp.int32)[:, None] == reversed_bucket[None, :]
    ).astype(F32)
    table = lax.dynamic_slice_in_dim(table_rows, g * GHEADS, GHEADS, 0)
    bias_rows = jnp.dot(table, bucket_hot, precision=HIGHEST).reshape(GHEADS, ranks + 1, size)
    bias = bias_tiles(bias_rows, inner)

    q, kv, h_col = project(own_g, h_pieces, w_cols)
    came = exchange(after(early, weights).reshape(ranks, capacity, D + 128), SEQ)
    came = came.reshape(ranks * capacity, D + 128)
    head_place = jnp.stack((i, jnp.int32(inner)))

    def place_of(columns):
        return jnp.concatenate((head_place, columns, own_g)).astype(jnp.int32)

    if inner == 2:
        kv_came = swap(kv, "i")
        kv_all = (kv, kv_came)
        columns = jnp.stack((i, 1 - i))
    else:
        kv_all = (lax.all_gather(kv, "i"),)
        columns = jnp.arange(inner, dtype=jnp.int32)
    place = place_of(columns)
    mixed, mixed_full, lse = attention_forward(place, after(q, came), kv_all, start, bias)
    att = exchange(mixed, "g")
    residual, outgoing = mlp_in(att, w_attn_low, inputs, gain_mlp[None], disp)

    arrived = exchange(outgoing.reshape(ranks, capacity, D), SEQ).reshape(ranks * capacity, D)
    active, hidden_grad, produced_grad, back, produced, router_grad = expert_layer(
        jnp.stack([me] + [2 * (c == f % 2) + (y == f // 2) for f in range(4)]).astype(jnp.int32),
        arrived,
        came, w_in[0], w_out[0], router_low
    )
    back_rows = exchange(back.reshape(ranks, capacity, D), SEQ).reshape(ranks * capacity, D)

    part_ff = FF // 4
    parts = [slice(f * part_ff, (f + 1) * part_ff) for f in range(4)]

    def part_grads(f):
        return (
            dotf(active[:, parts[f]], produced_grad, TN),
            dotf(arrived, hidden_grad[:, parts[f]], TN),
        )

    core_far = [swap(grad.astype(BF), "c") for grad in part_grads(0)]
    core_near = [swap(grad.astype(BF), "c") for grad in part_grads(1)]
    away = [
        (grad + core.astype(F32)).astype(BF) for grad, core in zip(part_grads(2), core_far)
    ]
    far_out, far_in = [swap(grad, "y") for grad in away]
    mine_out, mine_in = [
        grad + core.astype(F32) for grad, core in zip(part_grads(3), core_near)
    ]

    resid_grad, attn_grad, gain_two, out_grad = mlp_back(
        back_rows, disp, residual, upstream, gain_mlp[None], w_attn_low
    )
    out_grad = exchange(out_grad, "g")
    returned = exchange(after(produced, out_grad).reshape(ranks, capacity, D), SEQ)
    returned = returned.reshape(ranks * capacity, D)
    out_grad = after(out_grad, *away)

    def core_reduce(value):
        value = value.reshape(ranks, 2, 2 * rows, value.shape[-1])
        return pick(value, c, 1) + swap(pick(value, 1 - c, 1).astype(BF), "c").astype(F32)

    def inner_reduce(value):
        value = value.reshape(groups, inner, *value.shape[1:])
        if inner > 2:
            return lax.psum_scatter(value, "i", scatter_dimension=1).astype(BF)
        own = pick(value, i, 1) + swap(pick(value, 1 - i, 1).astype(BF), "i").astype(F32)
        return own.astype(BF)

    def share(value):
        value = value.astype(BF)
        value = (value.astype(F32) + swap(value, "y").astype(F32)).astype(BF)
        other = swap(value, "c")
        return jnp.where(c == 0, jnp.stack((value, other)), jnp.stack((other, value)))

    side_grad = side_grad_of(att, attn_grad, router_grad, ranks)
    side_part = inner_reduce(core_reduce(side_grad))

    if inner == 2:
        dq_other, dkv_other, dist_other = attention_backward(
            place_of(1 - i[None]),
            q,
            kv_came[None],
            start,
            bias,
            lse,
            mixed_full,
            out_grad,
            BF,
        )
        dkv_came = swap(dkv_other[0], "i")
        dq, dkv_own, dist = attention_backward(
            place_of(i[None]),
            q,
            kv[None],
            start,
            bias,
            lse,
            mixed_full,
            after(out_grad, dq_other),
            F32,
        )
        dkv_own = dkv_own[0]
        dist = jnp.concatenate((dist, dist_other))
    else:
        dq, dkv_all, dist = attention_backward(
            place, q, kv_all[0], start, bias, lse, mixed_full, out_grad, F32
        )
        dkv_own = lax.psum_scatter(dkv_all, "i")
        dkv_came = jnp.zeros(dkv_own.shape, BF)
        dq_other = jnp.zeros_like(dq)
        dist = jnp.take(dist, (i - jnp.arange(inner)) % inner, axis=0)
    dproj, gain_one, half = project_back(
        dq,
        dq_other,
        after(dkv_own, far_out, returned),
        dkv_came,
        w_cols,
        h_col,
        gain_attn[None],
    )
    dist = dist[:, :, 1:].transpose(1, 2, 0, 3).reshape(GHEADS, ranks, 2 * size)
    dist_rows = jnp.pad(dist[:, :, size:], ((0, 0), (0, 1), (0, 0))) + jnp.pad(
        dist[:, :, :size], ((0, 0), (1, 0), (0, 0))
    )
    table_grad = jnp.dot(dist_rows.reshape(GHEADS, -1), bucket_hot.T, precision=HIGHEST)
    table_all = lax.dynamic_update_slice(
        jnp.zeros((HEADS, BUCKETS), F32), table_grad, (g * GHEADS, 0)
    )
    half = exchange(half, "g")
    norm_in_grad = jnp.sum(half.astype(F32), axis=0)
    input_grad = resid_grad + norm_backward(norm_in_grad, gain_attn, inputs)
    result = residual + dotf(disp, returned, TN)

    qkv_part = inner_reduce(core_reduce(qkv_grad_of(h_col, dproj, ranks)))
    parts = jnp.concatenate((side_part, qkv_part), axis=2)
    parts = exchange(after(parts, half, far_in), "g")
    side_sum = jnp.sum(parts[:, :, : D + 128].astype(F32), axis=0).astype(BF)
    qkv_rows = parts[:, :, D + 128 :].swapaxes(0, 1).reshape(2 * rows, 3 * D)
    shards = share(jnp.concatenate((side_sum, qkv_rows), axis=1))
    shards = shards.reshape(copies * rows, -1).astype(F32)
    attn_shard, router_shard = shards[:, :D], shards[:, D : D + experts]
    qkv_shard = shards[:, D + 128 :].reshape(copies * rows, groups, 3, GW)
    qkv_shard = qkv_shard.swapaxes(1, 2).reshape(copies * rows, 3 * D)

    small = jnp.concatenate((gain_one[0], gain_two[0], table_all.reshape(-1)))
    small = jnp.pad(small, (0, 2048 - small.shape[0])).reshape(1, 16, 128)
    small = jnp.broadcast_to(small, (copies * ranks, 16, 128))
    small = exchange(after(small, parts), REP + SEQ)
    small = jnp.sum(small, axis=0).reshape(-1)
    w_in_shard = mine_in + far_in.astype(F32)
    w_out_shard = mine_out + far_out.astype(F32)
    return (
        result[None],
        input_grad[None],
        small[:D],
        small[D : 2 * D],
        qkv_shard,
        attn_shard,
        router_shard,
        small[2 * D : 2 * D + HEADS * BUCKETS].reshape(HEADS, BUCKETS),
        w_in_shard[None],
        w_out_shard[None],
    )


def solution(mesh):
    ranks = mesh.shape["seq"]
    split = Mesh(
        mesh.devices.reshape(2, mesh.shape["rep"] // 2, GROUPS, ranks // GROUPS),
        ("y", "c", "g", "i"),
    )
    placed = (
        P(REP, SEQ, None),
        P(REP, SEQ, None),
        P(),
        P(),
        P(SEQ, None),
        P(SEQ, None),
        P(SEQ, None),
        P(),
        P(SEQ, None, None),
        P(SEQ, None, None),
        P(REP, None),
        P(REP, SEQ, None),
        P(),
    )
    return jax.shard_map(
        local,
        mesh=split,
        in_specs=placed,
        out_specs=(
            P(REP, SEQ, None),
            P(REP, SEQ, None),
            P(),
            P(),
            P(SEQ, None),
            P(SEQ, None),
            P(SEQ, None),
            P(),
            P(SEQ, None, REP),
            P(SEQ, REP, None),
        ),
        check_vma=False,
    )
```

```python
from functools import partial
import math

import jax
import jax.numpy as jnp
from jax import lax
from jax.experimental import pallas as pl
from jax.experimental.pallas import tpu as pltpu
from jax.sharding import Mesh, PartitionSpec as P

D = 768
HEADS = 12
HEAD = 64
BUCKETS = 32
FF = 3072
GROUPS = 4
GHEADS = HEADS // GROUPS
GW = GHEADS * HEAD
EPS = 1e-06
HIGHEST = lax.Precision.HIGHEST
BF = jnp.bfloat16
F32 = jnp.float32
NT = (((1,), (1,)), ((), ()))
TN = (((0,), (0,)), ((), ()))
SEQ = ("g", "i")
REP = ("y", "c")


def dotf(a, b, dims=(((1,), (0,)), ((), ()))):
    return lax.dot_general(a, b, dims, preferred_element_type=F32)


def loop(count, body, init):
    if count <= 2:
        for step in range(count):
            init = body(step, init)
        return init
    return lax.fori_loop(0, count, body, init)


def ahead(block, own, count):
    return lax.rem(block + count - own, count)


def behind(step, own, count):
    return lax.rem(own + count - step, count)


def heads_apart(value, scale):
    lane = lax.broadcasted_iota(jnp.int32, value.shape, 1)
    value = value * jnp.asarray(scale, value.dtype)
    return jnp.concatenate(
        [jnp.where(lane // HEAD == head, value, jnp.zeros_like(value)) for head in range(GHEADS)],
        axis=0,
    )


def heads_beside(value, size):
    return jnp.concatenate(
        [value[head * size : (head + 1) * size] for head in range(GHEADS)], axis=1
    )


def tile_mask(start, query_block, key_block, size):
    lane = lax.broadcasted_iota(jnp.int32, (size, size), 1)
    row = lax.broadcasted_iota(jnp.int32, (size, size), 0)
    allowed = (lane >= start - key_block * size) & (
        lane - row <= (query_block - key_block) * size
    )
    return jnp.where(allowed, 0.0, -1e30)


def bias_kernel(rows_ref, tiles_ref):
    heads, inner, count, size, _ = tiles_ref.shape

    def head_step(head, carry):
        for part in range(inner):
            tiles_ref[head, part, 0] = jnp.zeros((size, size), F32)
            for step in range(count - 1):
                gap = step * inner + part
                pair = jnp.concatenate(
                    (rows_ref[head, gap : gap + 1, :], rows_ref[head, gap + 1 : gap + 2, :]),
                    axis=1,
                )
                spread = jnp.broadcast_to(pair, (size, 2 * size))
                spread = pltpu.roll(spread, 0, 1, stride=1, stride_axis=0)
                tiles_ref[head, part, step + 1] = spread[:, :size]
        return carry

    lax.fori_loop(0, heads, head_step, 0)


def cost(us):
    return pl.CostEstimate(flops=0, bytes_accessed=int(us * 3.4e6), transcendentals=0)


def bias_tiles(rows, inner):
    heads, count, size = rows.shape
    return pl.pallas_call(
        bias_kernel,
        out_shape=jax.ShapeDtypeStruct((heads, inner, (count - 1) // inner + 1, size, size), F32),
        cost_estimate=cost(0.05),
        name="bias_tiles",
    )(rows)


def block_of(kv_refs, slot, kb):
    if len(kv_refs) == 1:
        return kv_refs[0][slot, kb]
    return kv_refs[slot][kb]


def bias_place(place_ref, slot):
    shift = place_ref[0] - place_ref[2 + slot]
    below = (shift < 0).astype(jnp.int32)
    return shift + below * place_ref[1], 1 - below


def forward_kernel(
    place_ref,
    q_ref,
    *refs,
):
    groups, size, _ = q_ref.shape
    kv_refs, (start_ref, bias_ref, out_ref, full_ref, lse_ref, s_ref, vs_ref) = refs[:-7], refs[-7:]
    slots = s_ref.shape[0]
    tall = GHEADS * size

    def spread_step(slot, carry):
        for kb in range(groups):
            vs_ref[slot, kb] = heads_apart(block_of(kv_refs, slot, kb)[:, GW:], 1)
        return carry

    loop(slots, spread_step, 0)
    for qb in range(groups):
        queries = heads_apart(q_ref[qb], 0.125)
        start = start_ref[qb]
        query_block = qb * place_ref[1] + place_ref[0]

        def score_step(slot, top):
            part, tile = bias_place(place_ref, slot)
            for kb in range(qb + 1):
                key_block = kb * place_ref[1] + place_ref[2 + slot]
                mask = tile_mask(start, query_block, key_block, size)
                raw = dotf(queries, block_of(kv_refs, slot, kb)[:, :GW], NT)
                bias = [bias_ref[head, part, tile + qb - kb] + mask for head in range(GHEADS)]
                score = raw + jnp.concatenate(bias, axis=0)
                s_ref[slot, kb] = score
                top = jnp.maximum(top, score)
            return top

        top = loop(slots, score_step, jnp.full((tall, size), -1e30, F32))
        top = jnp.broadcast_to(jnp.max(top, axis=1, keepdims=True), (tall, size))

        def exp_step(slot, total):
            for kb in range(qb + 1):
                value = jnp.exp(s_ref[slot, kb] - top)
                s_ref[slot, kb] = value
                total = total + value
            return total

        total = loop(slots, exp_step, jnp.zeros((tall, size), F32))
        total = jnp.broadcast_to(jnp.sum(total, axis=1, keepdims=True), (tall, size))
        scale = 1.0 / total
        lse_ref[qb] = top + jnp.log(total)

        def out_step(slot, sums):
            low_sum, rest_sum = sums
            for kb in range(qb + 1):
                prob = s_ref[slot, kb] * scale
                prob_low = prob.astype(BF)
                rest = (prob - prob_low.astype(F32)).astype(BF)
                values = vs_ref[slot, kb]
                low_sum = low_sum + dotf(heads_beside(prob_low, size), values)
                rest_sum = rest_sum + dotf(heads_beside(rest, size), values)
            return (low_sum, rest_sum)

        zero = jnp.zeros((size, GW), F32)
        low_sum, rest_sum = loop(slots, out_step, (zero, zero))
        full_ref[qb] = low_sum + rest_sum
        out_ref[qb] = low_sum.astype(BF)


VM = pl.BlockSpec(memory_space=pltpu.VMEM)
SM = pl.BlockSpec(memory_space=pltpu.SMEM)


def attention_forward(place, q, kv, start, bias):
    groups, size, _ = q.shape
    slots = kv[0].shape[0] if len(kv) == 1 else len(kv)
    return pl.pallas_call(
        forward_kernel,
        in_specs=[SM] + [VM] * (3 + len(kv)),
        out_specs=[VM] * 3,
        out_shape=(
            jax.ShapeDtypeStruct((groups, size, GW), BF),
            jax.ShapeDtypeStruct((groups, size, GW), F32),
            jax.ShapeDtypeStruct((groups, GHEADS * size, size), F32),
        ),
        scratch_shapes=[
            pltpu.VMEM((slots, groups, GHEADS * size, size), F32),
            pltpu.VMEM((slots, groups, GHEADS * size, GW), BF),
        ],
        cost_estimate=cost(7),
        name="attention_forward",
    )(place, q, *kv, start, bias)


def backward_kernel(
    place_ref,
    q_ref,
    kv_ref,
    start_ref,
    bias_ref,
    lse_ref,
    full_ref,
    out_grad_ref,
    dq_ref,
    dkv_ref,
    dist_ref,
    dist_acc,
    qs_ref,
    gs_ref,
    delta_ref,
    p_ref,
    ds_ref,
):
    groups, size, _ = q_ref.shape
    slots = kv_ref.shape[0]
    tall = GHEADS * size
    for block in range(groups):
        spread = heads_apart(out_grad_ref[block], 1)
        gs_ref[block] = spread
        full = full_ref[block]
        product = spread.astype(F32) * jnp.concatenate([full] * GHEADS, axis=0)
        delta = jnp.sum(product, axis=1, keepdims=True)
        delta_ref[block] = jnp.broadcast_to(delta, (tall, size))
    for qb in range(groups):
        qs_ref[qb] = heads_apart(q_ref[qb], 0.125)
    dq_ref[...] = jnp.zeros_like(dq_ref)

    def slot_step(slot, carry):
        dist_acc[...] = jnp.zeros_like(dist_acc)
        part, tile = bias_place(place_ref, slot)
        for kb in range(groups):
            key_block = kb * place_ref[1] + place_ref[2 + slot]
            key, value = kv_ref[slot, kb][:, :GW], kv_ref[slot, kb][:, GW:]
            keys = heads_apart(key, 0.125)
            for qb in range(kb, groups):
                query_block = qb * place_ref[1] + place_ref[0]
                mask = tile_mask(start_ref[qb], query_block, key_block, size)
                at = tile + qb - kb
                bias = [bias_ref[head, part, at] + mask for head in range(GHEADS)]
                raw = dotf(qs_ref[qb], key, NT)
                prob_grad = dotf(gs_ref[qb], value, NT)
                prob = jnp.exp(raw + (jnp.concatenate(bias, axis=0) - lse_ref[qb]))
                score_grad = (prob * (prob_grad - delta_ref[qb])).astype(BF)
                p_ref[qb] = prob.astype(BF)
                ds_ref[qb] = score_grad
                for head in range(GHEADS):
                    dist_acc[head, at] += score_grad[
                        head * size : (head + 1) * size
                    ].astype(F32)
                dq_ref[qb] += dotf(heads_beside(score_grad, size), keys)
            count = (groups - kb) * tall
            dk = dotf(ds_ref[kb:].reshape(count, size), qs_ref[kb:].reshape(count, GW), TN)
            dv = dotf(p_ref[kb:].reshape(count, size), gs_ref[kb:].reshape(count, GW), TN)
            dkv_ref[slot, kb] = jnp.concatenate((dk, dv), axis=1).astype(dkv_ref.dtype)
        row = lax.broadcasted_iota(jnp.int32, (size, size), 0)
        lane = lax.broadcasted_iota(jnp.int32, (size, size), 1)
        flip = (row + lane == size - 1).astype(F32)
        for head in range(GHEADS):
            tiles = jnp.concatenate(
                [dist_acc[head, step] for step in range(groups + 1)], axis=1
            )
            tiles = jnp.dot(flip, tiles, precision=HIGHEST)
            for step in range(groups + 1):
                tile_rows = tiles[:, step * size : (step + 1) * size]
                wide = jnp.concatenate((tile_rows, jnp.zeros_like(tile_rows)), axis=1)
                wide = pltpu.roll(wide, 1, 1, stride=1, stride_axis=0)
                dist_ref[slot, head, step : step + 1, :] = jnp.sum(wide, axis=0, keepdims=True)
        return carry

    loop(slots, slot_step, 0)


def attention_backward(place, q, kv, start, bias, lse, full, out_grad, dtype):
    groups, size, _ = q.shape
    slots = kv.shape[0]
    tall = GHEADS * size
    return pl.pallas_call(
        backward_kernel,
        in_specs=[SM] + [VM] * 7,
        out_specs=[VM] * 3,
        out_shape=(
            jax.ShapeDtypeStruct((groups, size, GW), F32),
            jax.ShapeDtypeStruct((slots, groups, size, 2 * GW), dtype),
            jax.ShapeDtypeStruct((slots, GHEADS, groups + 1, 2 * size), F32),
        ),
        scratch_shapes=[
            pltpu.VMEM((GHEADS, groups + 1, size, size), F32),
            pltpu.VMEM((groups, tall, GW), BF),
            pltpu.VMEM((groups, tall, GW), BF),
            pltpu.VMEM((groups, tall, size), F32),
            pltpu.VMEM((groups, tall, size), BF),
            pltpu.VMEM((groups, tall, size), BF),
        ],
        cost_estimate=cost(8),
        name="attention_backward",
    )(place, q, kv, start, bias, lse, full, out_grad)


def project_kernel(own_ref, h0_ref, h1_ref, h2_ref, h3_ref, w_ref, q_ref, kv_ref, h_ref):
    groups, size, _ = h_ref.shape
    for step, piece_ref in enumerate((h0_ref, h1_ref, h2_ref, h3_ref)):
        h_ref[behind(step, own_ref[0], groups)] = piece_ref[...]
    rows = dotf(h_ref[...].reshape(groups * size, D), w_ref[...]).astype(BF)
    q_ref[...] = rows[:, :GW].reshape(groups, size, GW)
    kv_ref[...] = rows[:, GW:].reshape(groups, size, 2 * GW)


def project(own, pieces, w_cols):
    size = pieces[0].shape[0]
    return pl.pallas_call(
        project_kernel,
        in_specs=[SM] + [VM] * 5,
        out_specs=[VM] * 3,
        out_shape=(
            jax.ShapeDtypeStruct((GROUPS, size, GW), BF),
            jax.ShapeDtypeStruct((GROUPS, size, 2 * GW), BF),
            jax.ShapeDtypeStruct((GROUPS, size, D), BF),
        ),
        cost_estimate=cost(0.05),
        name="project",
    )(own, *pieces, w_cols)


def mlp_in_kernel(
    att_ref, w_ref, x_ref, gain_ref, disp_ref, resid_ref, sent_ref
):
    total = x_ref[...]
    for group in range(GROUPS):
        total = total + dotf(att_ref[group], w_ref[group])
    resid_ref[...] = total
    rate = lax.rsqrt(jnp.mean(total * total, axis=-1, keepdims=True) + EPS)
    low = (total * rate * gain_ref[...]).astype(BF)
    sent_ref[...] = dotf(disp_ref[...], low).astype(BF)


def mlp_in(att, w_attn, x, gain, disp):
    return pl.pallas_call(
        mlp_in_kernel,
        in_specs=[VM] * 5,
        out_specs=[VM] * 2,
        out_shape=(
            jax.ShapeDtypeStruct(x.shape, F32),
            jax.ShapeDtypeStruct((disp.shape[0], D), BF),
        ),
        cost_estimate=cost(0.05),
        name="mlp_in",
    )(att, w_attn, x, gain, disp)


def expert_kernel(
    own_ref,
    x_ref,
    came_ref,
    w_in_ref,
    w_out_ref,
    router_ref,
    active_ref,
    hidden_grad_ref,
    out_grad_ref,
    back_ref,
    out_ref,
    router_grad_ref,
    out_acc,
    back_acc,
    gate_ref,
):
    step = pl.program_id(0)
    rows = x_ref[...]
    lane = lax.broadcasted_iota(jnp.int32, (rows.shape[0], 128), 1)

    @pl.when(step == 0)
    def _():
        logits = dotf(rows, router_ref[...])
        pair = came_ref[:, D:].astype(F32)
        own = jnp.sum(jnp.where(lane == own_ref[0], logits, 0.0), axis=1, keepdims=True)
        other = jnp.where(lane == own_ref[0], 0.0, pair)
        other = jnp.sum(other * logits, axis=1, keepdims=True)
        peak = jnp.maximum(own, other)
        own_e, other_e = jnp.exp(own - peak), jnp.exp(other - peak)
        total = own_e + other_e
        own_gate = own_e / total
        gate_ref[0] = jnp.broadcast_to(own_gate, lane.shape)
        gate_ref[1] = jnp.broadcast_to(other_e / total, lane.shape)
        out_grad_ref[...] = (own_gate * came_ref[:, :D].astype(F32)).astype(BF)
        out_acc[...] = jnp.zeros_like(out_acc)
        back_acc[...] = jnp.zeros_like(back_acc)

    hidden = dotf(rows, w_in_ref[...])
    active_grad = dotf(out_grad_ref[...], w_out_ref[...], NT)
    value, slope = gelu_parts(hidden)
    active = value.astype(BF)
    hidden_grad = (slope * active_grad).astype(BF)
    active_ref[...] = active
    hidden_grad_ref[...] = hidden_grad
    out_acc[...] += dotf(active, w_out_ref[...])
    back_acc[...] += dotf(hidden_grad, w_in_ref[...], NT)

    @pl.when(step == pl.num_programs(0) - 1)
    def _():
        produced = out_acc[...].astype(BF).astype(F32)
        own_gate, other_gate = gate_ref[0][:, :1], gate_ref[1][:, :1]
        out_ref[...] = (own_gate * produced).astype(BF)
        gate_grad = jnp.sum(came_ref[:, :D].astype(F32) * produced, axis=1, keepdims=True)
        pull = own_gate * other_gate * gate_grad
        pair = came_ref[:, D:].astype(F32)
        logit_rows = pull * jnp.where(lane == own_ref[0], 1.0, -pair)
        high = logit_rows.astype(BF)
        rest = (logit_rows - high.astype(F32)).astype(BF)
        router = router_ref[...]
        back = back_acc[...].astype(BF).astype(F32)
        back = back + dotf(high, router, NT) + dotf(rest, router, NT)
        back_ref[...] = back.astype(BF)
        router_grad_ref[...] = dotf(rows, high, TN) + dotf(rows, rest, TN)


def expert_layer(own, x, came, w_in, w_out, router):
    count = x.shape[0]
    steps = 4
    part = FF // steps
    whole = lambda *shape: pl.BlockSpec(shape, lambda f, own: (0,) * len(shape))
    piece = pl.BlockSpec((count, part), lambda f, own: (0, own[1 + f]))
    return pl.pallas_call(
        expert_kernel,
        grid_spec=pltpu.PrefetchScalarGridSpec(
            num_scalar_prefetch=1,
            grid=(steps,),
            in_specs=[
                whole(count, D),
                whole(count, D + 128),
                pl.BlockSpec((D, part), lambda f, own: (0, f)),
                pl.BlockSpec((part, D), lambda f, own: (f, 0)),
                whole(D, 128),
            ],
            out_specs=[
                piece,
                piece,
                whole(count, D),
                whole(count, D),
                whole(count, D),
                whole(D, 128),
            ],
            scratch_shapes=[
                pltpu.VMEM((count, D), F32),
                pltpu.VMEM((count, D), F32),
                pltpu.VMEM((2, count, 128), F32),
            ],
        ),
        out_shape=(
            jax.ShapeDtypeStruct((count, FF), BF),
            jax.ShapeDtypeStruct((count, FF), BF),
            jax.ShapeDtypeStruct((count, D), BF),
            jax.ShapeDtypeStruct((count, D), BF),
            jax.ShapeDtypeStruct((count, D), BF),
            jax.ShapeDtypeStruct((D, 128), F32),
        ),
        cost_estimate=cost(0.05),
        name="expert_layer",
    )(own, x, came, w_in, w_out, router)


def mlp_back_kernel(
    back_ref, disp_ref, resid_ref, up_ref, gain_ref, w_ref, grad_ref, low_ref, gain_grad_ref, out_ref
):
    grad = dotf(disp_ref[...], back_ref[...], TN)
    resid = resid_ref[...]
    rate = lax.rsqrt(jnp.mean(resid * resid, axis=-1, keepdims=True) + EPS)
    unit = resid * rate
    gain_grad_ref[...] = jnp.sum(grad * unit, axis=0, keepdims=True)
    scaled = grad * gain_ref[...]
    total = up_ref[...] + rate * (
        scaled - unit * jnp.mean(scaled * unit, axis=-1, keepdims=True)
    )
    grad_ref[...] = total
    low = total.astype(BF)
    low_ref[...] = low
    for group in range(GROUPS):
        out_ref[group] = dotf(low, w_ref[group], NT).astype(BF)


def mlp_back(back, disp, resid, up, gain, w_attn):
    size = resid.shape[0]
    return pl.pallas_call(
        mlp_back_kernel,
        in_specs=[VM] * 6,
        out_specs=[VM] * 4,
        out_shape=(
            jax.ShapeDtypeStruct((size, D), F32),
            jax.ShapeDtypeStruct((size, D), BF),
            jax.ShapeDtypeStruct((1, D), F32),
            jax.ShapeDtypeStruct((GROUPS, size, GW), BF),
        ),
        cost_estimate=cost(4),
        name="mlp_back",
    )(back, disp, resid, up, gain, w_attn)


def project_back_kernel(
    dq_ref,
    dq_other_ref,
    dkv_ref,
    came_ref,
    w_ref,
    h_ref,
    gain_ref,
    dproj_ref,
    gain_grad_ref,
    half_ref,
):
    groups, size, _ = dq_ref.shape
    dq = (dq_ref[...] + dq_other_ref[...]).astype(BF).reshape(groups * size, GW)
    dkv = (dkv_ref[...] + came_ref[...].astype(F32)).astype(BF)
    dkv = dkv.reshape(groups * size, 2 * GW)
    dproj_ref[...] = jnp.concatenate((dq, dkv), axis=1)
    total = jnp.zeros((1, D), F32)
    for block in range(groups):
        half = dotf(dproj_ref[block * size : (block + 1) * size], w_ref[...], NT)
        half_ref[block] = half.astype(BF)
        total = total + jnp.sum(half * h_ref[block].astype(F32), axis=0, keepdims=True)
    gain_grad_ref[...] = total / gain_ref[...]


def project_back(dq, dq_other, dkv, came, w_cols, h_col, gain):
    groups, size, _ = dq.shape
    return pl.pallas_call(
        project_back_kernel,
        in_specs=[VM] * 7,
        out_specs=[VM] * 3,
        out_shape=(
            jax.ShapeDtypeStruct((groups * size, 3 * GW), BF),
            jax.ShapeDtypeStruct((1, D), F32),
            jax.ShapeDtypeStruct((groups, size, D), BF),
        ),
        cost_estimate=cost(4),
        name="project_back",
    )(dq, dq_other, dkv, came, w_cols, h_col, gain)


def qkv_grad_kernel(h_ref, dproj_ref, grad_ref):
    ranks, rows, _ = grad_ref.shape
    groups, size, _ = h_ref.shape
    total = dotf(h_ref[...].reshape(groups * size, D), dproj_ref[...], TN)
    for rank in range(ranks):
        grad_ref[rank] = total[rank * rows : (rank + 1) * rows]


def qkv_grad_of(h_col, dproj, ranks):
    return pl.pallas_call(
        qkv_grad_kernel,
        in_specs=[VM] * 2,
        out_specs=VM,
        out_shape=jax.ShapeDtypeStruct((ranks, D // ranks, 3 * GW), F32),
        cost_estimate=cost(0.05),
        name="qkv_grad",
    )(h_col, dproj)


def side_grad_kernel(att_ref, grad_ref, router_ref, out_ref):
    ranks, rows, _ = out_ref.shape
    inner = ranks // GROUPS
    for block in range(GROUPS):
        total = dotf(att_ref[block], grad_ref[...], TN)
        for part in range(inner):
            out_ref[block * inner + part, :, :D] = total[part * rows : (part + 1) * rows]
    for rank in range(ranks):
        out_ref[rank, :, D:] = router_ref[rank * rows : (rank + 1) * rows]


def side_grad_of(att, grad, router_grad, ranks):
    return pl.pallas_call(
        side_grad_kernel,
        in_specs=[VM] * 3,
        out_specs=VM,
        out_shape=jax.ShapeDtypeStruct((ranks, D // ranks, D + 128), F32),
        cost_estimate=cost(0.05),
        name="side_grad",
    )(att, grad, router_grad)


def assemble_kernel(own_ref, p0_ref, p1_ref, p2_ref, p3_ref, rows_ref, scratch):
    side = D + 128
    wide = side + 3 * GW
    last = side + 3 * D
    width = (p0_ref.shape[1] - wide) // 2
    pieces = [ref[...].astype(F32) for ref in (p0_ref, p1_ref, p2_ref, p3_ref)]
    total = pieces[0] + pieces[1] + pieces[2] + pieces[3]
    rows_ref[:, :side] = total[:, :side].astype(BF)
    small = total[:, wide : wide + width] + total[:, wide + width :]
    high = small.astype(BF)
    rows_ref[:, last : last + width] = high
    rows_ref[:, last + width :] = (small - high.astype(F32)).astype(BF)
    for step, piece in enumerate(pieces):
        scratch[behind(step, own_ref[0], GROUPS)] = piece[:, side:wide]
    for group in range(GROUPS):
        for kind in range(3):
            at = side + (kind * GROUPS + group) * GW
            rows_ref[:, at : at + GW] = scratch[group, :, kind * GW : (kind + 1) * GW].astype(BF)


def assemble(own, parts):
    rows, width = parts[0].shape
    return pl.pallas_call(
        assemble_kernel,
        in_specs=[SM] + [VM] * 4,
        out_specs=VM,
        out_shape=jax.ShapeDtypeStruct((rows, width + 3 * D - 3 * GW), BF),
        scratch_shapes=[pltpu.VMEM((GROUPS, rows, 3 * GW), F32)],
        cost_estimate=cost(0.05),
        name="assemble",
    )(own, *parts)


def unpack_kernel(own_ref, pair_ref, came_ref, attn_ref, router_ref, qkv_ref, small_ref):
    experts = router_ref.shape[2]
    last = 4 * D + 128
    width = small_ref.shape[1]
    small = jnp.zeros(small_ref.shape, F32)
    for near, ref in ((own_ref[0], pair_ref), (1 - own_ref[0], came_ref)):
        for part in range(2):
            value = ref[part].astype(F32)
            attn_ref[near * 2 + part] = value[:, :D]
            router_ref[near * 2 + part] = value[:, D : D + experts]
            qkv_ref[near * 2 + part] = value[:, D + 128 : last]
            small = small + (value[:, last : last + width] + value[:, last + width :])
    small_ref[...] = small


def unpack(own, pair, came, experts):
    rows = pair.shape[1]
    width = (pair.shape[2] - 4 * D - 128) // 2
    outs = pl.pallas_call(
        unpack_kernel,
        in_specs=[SM] + [VM] * 2,
        out_specs=[VM] * 4,
        out_shape=[jax.ShapeDtypeStruct((4, rows, n), F32) for n in (D, experts, 3 * D)]
        + [jax.ShapeDtypeStruct((rows, width), F32)],
        cost_estimate=cost(0.05),
        name="unpack",
    )(own.astype(jnp.int32), pair, came)
    return [out.reshape(4 * rows, -1) for out in outs[:3]] + [outs[3]]


def gelu_parts(hidden):
    scale = math.sqrt(2.0 / math.pi)
    square = hidden * hidden
    bend = jnp.tanh(hidden * (scale + (scale * 0.044715) * square))
    half = 0.5 + 0.5 * bend
    slope = scale + (3 * scale * 0.044715) * square
    return hidden * half, half + (0.5 * hidden) * (1.0 - bend * bend) * slope


def swap(value, axis):
    return lax.ppermute(value, axis, [(0, 1), (1, 0)])


def tie(*values):
    return lax.optimization_barrier(values)


def turn(value, step):
    return lax.ppermute(value, "g", [(j, (j + step) % GROUPS) for j in range(GROUPS)])


def in_turn(pieces, g):
    pieces = jnp.stack(pieces[::-1] * 2)
    return lax.dynamic_slice_in_dim(pieces, GROUPS - 1 - g, GROUPS, 0)


def exchange(value, axes):
    return lax.all_to_all(value, axes, split_axis=0, concat_axis=0, tiled=True)


def in_order(own, came, index):
    return jnp.where(index == 0, jnp.stack((own, came)), jnp.stack((came, own)))


def rep_gather(value, y, c):
    pair = in_order(value, swap(value, "y"), y)
    return in_order(pair, swap(pair, "c"), c)


def halve(value, index, axis):
    count, rows, cols = value.shape
    value = value.reshape(count, 2, rows // 2, cols)
    away = swap(pick(value, 1 - index, 1).astype(BF), axis)
    return pick(value, index, 1) + away.astype(F32)


def pick(value, index, axis):
    return lax.dynamic_index_in_dim(value, index, axis, keepdims=False)


def norm_backward(grad, gain, value):
    rate = lax.rsqrt(jnp.mean(value * value, axis=-1, keepdims=True) + EPS)
    unit = value * rate
    scaled = grad * gain
    return rate * (scaled - unit * jnp.mean(scaled * unit, axis=-1, keepdims=True))


def local(
    tokens,
    cotangent,
    gain_attn,
    gain_mlp,
    w_qkv,
    w_attn_out,
    router,
    rel_table,
    w_in,
    w_out,
    segment_ids,
    expert_ids,
    rel_bucket,
):
    groups, inner = lax.axis_size("g"), lax.axis_size("i")
    g, i = lax.axis_index("g"), lax.axis_index("i")
    y, c = lax.axis_index("y"), lax.axis_index("c")
    ranks = groups * inner
    copies = 4
    size = tokens.shape[1]
    experts = ranks
    capacity = max(2, 4 * size // experts)
    inputs = tokens[0]
    upstream = cotangent[0]
    seg_all = segment_ids[0]
    chosen_ids = expert_ids[0]
    rows = w_qkv.shape[0] // copies
    me = g * inner + i
    own_g = g[None].astype(jnp.int32)

    rate = lax.rsqrt(jnp.mean(inputs * inputs, axis=-1, keepdims=True) + EPS)
    h_attn = (inputs * rate * gain_attn).astype(BF)
    h_pieces = [h_attn] + [turn(h_attn, step) for step in range(1, groups)]

    part = lax.dynamic_slice_in_dim(w_qkv, c * 2 * rows, 2 * rows, 0).astype(BF)
    part = part.reshape(2 * rows, 3, groups, GW).transpose(2, 0, 1, 3)
    part = jnp.broadcast_to(part[:, None], (groups, inner, 2 * rows, 3, GW))
    part = exchange(part.reshape(ranks, 2 * rows, 3 * GW), SEQ)
    both = jnp.concatenate((w_attn_out, jnp.pad(router, ((0, 0), (0, 128 - experts)))), axis=1)
    both = lax.dynamic_slice_in_dim(both, (c * 2 + y) * rows, rows, 0).astype(BF)
    both = jnp.broadcast_to(both[None], (ranks, rows, D + 128))
    w_cols = in_order(part, swap(part, "c"), c).swapaxes(0, 1).reshape(D, 3 * GW)

    expert_iota = jnp.arange(experts, dtype=jnp.int32)
    token_iota = jnp.arange(size, dtype=jnp.int32)
    pair_hot = jnp.any(chosen_ids[:, :, None] == expert_iota[None, None, :], axis=1)
    rank = jnp.dot(
        (token_iota[:, None] > token_iota[None, :]).astype(BF),
        pair_hot.astype(BF),
        preferred_element_type=F32,
    ).astype(jnp.int32)
    disp = (rank.T[:, None, :] == jnp.arange(capacity, dtype=jnp.int32)[None, :, None]) & (
        pair_hot.T[:, None, :]
    )
    disp = disp.astype(BF).reshape(experts * capacity, size)
    early = jnp.concatenate(
        (upstream.astype(BF), jnp.pad(pair_hot.astype(BF), ((0, 0), (0, 128 - experts)))), axis=1
    )
    early = jnp.dot(disp, early, preferred_element_type=F32).astype(BF)
    seg_col = pick(seg_all.reshape(groups, inner, size), i, 1)
    start = jnp.sum(
        (seg_all[None, None, :] < seg_col[:, :, None]).astype(jnp.int32), axis=-1, keepdims=True
    )
    padded = jnp.concatenate(
        (jnp.full((size - 1,), -1, jnp.int32), rel_bucket, jnp.full((1,), -1, jnp.int32))
    )
    reversed_bucket = padded.reshape(ranks + 1, size)[:, ::-1].reshape(-1)
    bucket_hot = (
        jnp.arange(BUCKETS, dtype=jnp.int32)[:, None] == reversed_bucket[None, :]
    ).astype(F32)
    table = lax.dynamic_slice_in_dim(rel_table, g * GHEADS, GHEADS, 0)
    bias_rows = jnp.dot(table, bucket_hot, precision=HIGHEST).reshape(GHEADS, ranks + 1, size)
    bias = bias_tiles(bias_rows, inner)
    bias, start, *h_pieces = tie(bias, start, *h_pieces)

    early = jnp.concatenate((early.reshape(ranks, capacity, D + 128), both), axis=1)
    early, *h_pieces = tie(early, *h_pieces)
    q, kv, h_col = project(own_g, h_pieces, w_cols)
    came_rows = exchange(early, SEQ)
    head_place = jnp.stack((i, jnp.int32(inner)))

    def place_of(columns):
        return jnp.concatenate((head_place, columns, own_g)).astype(jnp.int32)

    if inner == 2:
        kv_came = swap(kv, "i")
        kv_all = (kv, kv_came)
        columns = jnp.stack((i, 1 - i))
    else:
        kv_all = (lax.all_gather(kv, "i"),)
        columns = jnp.arange(inner, dtype=jnp.int32)
    place = place_of(columns)
    mixed, mixed_full, lse = attention_forward(place, q, kv_all, start, bias)
    mixed, came_rows = tie(mixed, came_rows)
    both = rep_gather(came_rows[:, capacity:], y, c)
    both = both.transpose(2, 0, 1, 3, 4).reshape(D, D + 128)
    w_attn_low = both[:, :D].reshape(groups, GW, D)
    router_low = both[:, D:]
    came_rows = came_rows[:, :capacity].reshape(ranks * capacity, D + 128)
    att = exchange(mixed, "g")
    residual, outgoing = mlp_in(att, w_attn_low, inputs, gain_mlp[None], disp)

    arrived = exchange(outgoing.reshape(ranks, capacity, D), SEQ).reshape(ranks * capacity, D)
    active, hidden_grad, produced_grad, back, produced, router_grad = expert_layer(
        jnp.stack([me] + [2 * (c == f % 2) + (y == f // 2) for f in range(4)]).astype(jnp.int32),
        arrived,
        came_rows, w_in[0], w_out[0], router_low
    )
    back_rows = exchange(back.reshape(ranks, capacity, D), SEQ).reshape(ranks * capacity, D)

    part_ff = FF // 4
    slices = [slice(f * part_ff, (f + 1) * part_ff) for f in range(4)]

    def part_grads(f, active=active, hidden_grad=hidden_grad):
        return (
            dotf(active[:, slices[f]], produced_grad, TN),
            dotf(arrived, hidden_grad[:, slices[f]], TN),
        )

    core_far = [swap(grad.astype(BF), "c") for grad in part_grads(0)]
    near = [grad.astype(BF) for grad in part_grads(1)]
    away = [
        (grad + core.astype(F32)).astype(BF) for grad, core in zip(part_grads(2), core_far)
    ]
    far_out = swap(away[0], "y")
    back_rows, *near = tie(back_rows, *near)

    resid_grad, attn_grad, gain_two, out_grad = mlp_back(
        back_rows, disp, residual, upstream, gain_mlp[None], w_attn_low
    )
    out_grad = exchange(out_grad, "g")
    side_grad = side_grad_of(att, attn_grad, router_grad, ranks)
    out_grad, produced, side_grad, away_in = tie(out_grad, produced, side_grad, away[1])
    far_in = swap(away_in, "y")
    near = [swap(grad, "c") for grad in near]
    returned = exchange(produced.reshape(ranks, capacity, D), SEQ)

    def inner_reduce(value):
        value = value.reshape(groups, inner, *value.shape[1:])
        if inner > 2:
            return lax.psum_scatter(value, "i", scatter_dimension=1).astype(BF)
        own = pick(value, i, 1) + swap(pick(value, 1 - i, 1).astype(BF), "i").astype(F32)
        return own.astype(BF)

    if inner == 2:
        dq_other, dkv_other, dist_other = attention_backward(
            place_of(1 - i[None]),
            q,
            kv_came[None],
            start,
            bias,
            lse,
            mixed_full,
            out_grad,
            BF,
        )
        out_grad, dq_other, dkv_other, far_out = tie(out_grad, dq_other, dkv_other, far_out)
        dkv_came = swap(dkv_other[0], "i")
        dq, dkv_own, dist = attention_backward(
            place_of(i[None]),
            q,
            kv[None],
            start,
            bias,
            lse,
            mixed_full,
            out_grad,
            F32,
        )
        dkv_own = dkv_own[0]
        dist = jnp.concatenate((dist, dist_other))
    else:
        dq, dkv_all, dist = attention_backward(
            place, q, kv_all[0], start, bias, lse, mixed_full, out_grad, F32
        )
        dkv_own = lax.psum_scatter(dkv_all, "i")
        dkv_came = jnp.zeros(dkv_own.shape, BF)
        dq_other = jnp.zeros_like(dq)
        dist = jnp.take(dist, (i - jnp.arange(inner)) % inner, axis=0)
    dkv_own, returned, far_in = tie(dkv_own, returned, far_in)
    returned = returned.reshape(ranks * capacity, D)
    dproj, gain_one, half = project_back(
        dq, dq_other, dkv_own, dkv_came, w_cols, h_col, gain_attn[None]
    )
    half = exchange(half, "g")
    dproj, side_grad = tie(dproj, side_grad)
    side_grad = halve(side_grad, c, "c")
    parts = halve(qkv_grad_of(h_col, dproj, ranks), c, "c")
    parts, gain_one, gain_two, dist = tie(
        jnp.concatenate((side_grad, parts), axis=2), gain_one, gain_two, dist
    )
    parts = halve(parts, y, "y")
    parts, half, active, hidden_grad, *near = tie(parts, half, active, hidden_grad, *near)
    mine_out, mine_in = [
        grad + core.astype(F32) for grad, core in zip(part_grads(3, active, hidden_grad), near)
    ]
    dist = dist[:, :, 1:].transpose(1, 2, 0, 3).reshape(GHEADS, ranks, 2 * size)
    dist_rows = jnp.pad(dist[:, :, size:], ((0, 0), (0, 1), (0, 0))) + jnp.pad(
        dist[:, :, :size], ((0, 0), (1, 0), (0, 0))
    )
    table_grad = jnp.dot(dist_rows.reshape(GHEADS, -1), bucket_hot.T, precision=HIGHEST)
    table_all = lax.dynamic_update_slice(
        jnp.zeros((HEADS, BUCKETS), F32), table_grad, (g * GHEADS, 0)
    )
    small = jnp.concatenate((gain_one[0], gain_two[0], table_all.reshape(-1)))
    count = small.shape[0]
    width = -(-count // (rows * 128)) * 128
    small = jnp.pad(small.reshape(-1, 128), ((0, (rows * width - count) // 128), (0, 0)))
    small = small.reshape(rows, width)
    small = small + (swap(small, "i") if inner == 2 else lax.psum(small, "i") - small)
    high = lax.reduce_precision(small, 8, 7)
    small = jnp.concatenate((high, small - high), axis=1).astype(BF)
    small = jnp.broadcast_to(small[None], (groups, rows, 2 * width))

    parts = jnp.concatenate((inner_reduce(parts), small), axis=2)
    parts = [pick(parts, g, 0)] + [
        turn(pick(parts, lax.rem(g + step, groups), 0), step) for step in range(1, groups)
    ]
    norm_in_grad = jnp.sum(half.astype(F32), axis=0)
    input_grad = resid_grad + norm_backward(norm_in_grad, gain_attn, inputs)
    result = residual + dotf(disp, returned, TN)
    shards = assemble(own_g, parts)
    pair = in_order(shards, swap(shards, "y"), y)
    attn_shard, router_shard, qkv_shard, small = unpack(c[None], pair, swap(pair, "c"), experts)
    small = small.reshape(-1)
    w_in_shard = mine_in + far_in.astype(F32)
    w_out_shard = mine_out + far_out.astype(F32)
    return (
        result[None],
        input_grad[None],
        small[:D],
        small[D : 2 * D],
        qkv_shard,
        attn_shard,
        router_shard,
        small[2 * D : 2 * D + HEADS * BUCKETS].reshape(HEADS, BUCKETS),
        w_in_shard[None],
        w_out_shard[None],
    )


def solution(mesh):
    ranks = mesh.shape["seq"]
    split = Mesh(
        mesh.devices.reshape(2, mesh.shape["rep"] // 2, GROUPS, ranks // GROUPS),
        ("y", "c", "g", "i"),
    )
    placed = (
        P(REP, SEQ, None),
        P(REP, SEQ, None),
        P(),
        P(),
        P(SEQ, None),
        P(SEQ, None),
        P(SEQ, None),
        P(),
        P(SEQ, None, None),
        P(SEQ, None, None),
        P(REP, None),
        P(REP, SEQ, None),
        P(),
    )
    return jax.shard_map(
        local,
        mesh=split,
        in_specs=placed,
        out_specs=(
            P(REP, SEQ, None),
            P(REP, SEQ, None),
            P(),
            P(),
            P(SEQ, None),
            P(SEQ, None),
            P(SEQ, None),
            P(),
            P(SEQ, None, REP),
            P(SEQ, REP, None),
        ),
        check_vma=False,
    )
```

```python
from functools import partial
import math

import jax
import jax.numpy as jnp
from jax import lax
from jax.experimental import pallas as pl
from jax.experimental.pallas import tpu as pltpu
from jax.sharding import Mesh, PartitionSpec as P

D = 768
HEADS = 12
HEAD = 64
BUCKETS = 32
FF = 3072
GROUPS = 4
GHEADS = HEADS // GROUPS
GW = GHEADS * HEAD
EPS = 1e-06
HIGHEST = lax.Precision.HIGHEST
BF = jnp.bfloat16
F32 = jnp.float32
NT = (((1,), (1,)), ((), ()))
TN = (((0,), (0,)), ((), ()))
SEQ = ("g", "i")
REP = ("y", "c")


def dotf(a, b, dims=(((1,), (0,)), ((), ()))):
    return lax.dot_general(a, b, dims, preferred_element_type=F32)


def loop(count, body, init):
    if count <= 2:
        for step in range(count):
            init = body(step, init)
        return init
    return lax.fori_loop(0, count, body, init)


def ahead(block, own, count):
    return lax.rem(block + count - own, count)


def behind(step, own, count):
    return lax.rem(own + count - step, count)


def heads_apart(value, scale):
    lane = lax.broadcasted_iota(jnp.int32, value.shape, 1)
    value = value * jnp.asarray(scale, value.dtype)
    return jnp.concatenate(
        [jnp.where(lane // HEAD == head, value, jnp.zeros_like(value)) for head in range(GHEADS)],
        axis=0,
    )


def heads_beside(value, size):
    return jnp.concatenate(
        [value[head * size : (head + 1) * size] for head in range(GHEADS)], axis=1
    )


def turned(value):
    wide = jnp.concatenate((value, jnp.zeros((value.shape[0], -GW % 128), F32)), axis=1)
    return wide.T[:GW]


def turned_back(value):
    tall = jnp.concatenate((value, jnp.zeros((-GW % 128, value.shape[1]), F32)), axis=0)
    return tall.T[:, :GW]


def tile_mask(start, query_block, key_block, size):
    lane = lax.broadcasted_iota(jnp.int32, (size, size), 1)
    row = lax.broadcasted_iota(jnp.int32, (size, size), 0)
    allowed = (lane >= start - key_block * size) & (
        lane - row <= (query_block - key_block) * size
    )
    return jnp.where(allowed, 0.0, -1e30)


def bias_kernel(rows_ref, tiles_ref):
    heads, inner, count, size, _ = tiles_ref.shape

    def head_step(head, carry):
        for part in range(inner):
            tiles_ref[head, part, 0] = jnp.zeros((size, size), F32)
            for step in range(count - 1):
                gap = step * inner + part
                pair = jnp.concatenate(
                    (rows_ref[head, gap : gap + 1, :], rows_ref[head, gap + 1 : gap + 2, :]),
                    axis=1,
                )
                spread = jnp.broadcast_to(pair, (size, 2 * size))
                spread = pltpu.roll(spread, 0, 1, stride=1, stride_axis=0)
                tiles_ref[head, part, step + 1] = spread[:, :size]
        return carry

    lax.fori_loop(0, heads, head_step, 0)


def cost(us):
    return pl.CostEstimate(flops=0, bytes_accessed=int(us * 3.4e6), transcendentals=0)


def bias_tiles(rows, inner):
    heads, count, size = rows.shape
    return pl.pallas_call(
        bias_kernel,
        out_shape=jax.ShapeDtypeStruct((heads, inner, (count - 1) // inner + 1, size, size), F32),
        cost_estimate=cost(0.05),
        name="bias_tiles",
    )(rows)


def block_of(kv_refs, slot, kb):
    if len(kv_refs) == 1:
        return kv_refs[0][slot, kb]
    return kv_refs[slot][kb]


def bias_place(place_ref, slot):
    shift = place_ref[0] - place_ref[2 + slot]
    below = (shift < 0).astype(jnp.int32)
    return shift + below * place_ref[1], 1 - below


def forward_kernel(
    place_ref,
    q_ref,
    *refs,
):
    groups, size, _ = q_ref.shape
    kv_refs, (start_ref, bias_ref, out_ref, full_ref, lse_ref, s_ref, vs_ref) = refs[:-7], refs[-7:]
    slots = s_ref.shape[0]
    tall = GHEADS * size

    def spread_step(slot, carry):
        for kb in range(groups):
            vs_ref[slot, kb] = heads_apart(block_of(kv_refs, slot, kb)[:, GW:], 1)
        return carry

    loop(slots, spread_step, 0)
    for qb in range(groups):
        queries = heads_apart(q_ref[qb], 0.125)
        start = start_ref[qb]
        query_block = qb * place_ref[1] + place_ref[0]

        def score_step(slot, top):
            part, tile = bias_place(place_ref, slot)
            for kb in range(qb + 1):
                key_block = kb * place_ref[1] + place_ref[2 + slot]
                mask = tile_mask(start, query_block, key_block, size)
                raw = dotf(queries, block_of(kv_refs, slot, kb)[:, :GW], NT)
                bias = [bias_ref[head, part, tile + qb - kb] + mask for head in range(GHEADS)]
                score = raw + jnp.concatenate(bias, axis=0)
                s_ref[slot, kb] = score
                top = jnp.maximum(top, score)
            return top

        top = loop(slots, score_step, jnp.full((tall, size), -1e30, F32))
        top = jnp.broadcast_to(jnp.max(top, axis=1, keepdims=True), (tall, size))

        def exp_step(slot, total):
            for kb in range(qb + 1):
                value = jnp.exp(s_ref[slot, kb] - top)
                s_ref[slot, kb] = value
                total = total + value
            return total

        total = loop(slots, exp_step, jnp.zeros((tall, size), F32))
        total = jnp.broadcast_to(jnp.sum(total, axis=1, keepdims=True), (tall, size))
        scale = 1.0 / total
        lse_ref[qb] = top + jnp.log(total)

        def out_step(slot, sums):
            low_sum, rest_sum = sums
            for kb in range(qb + 1):
                prob = s_ref[slot, kb] * scale
                prob_low = prob.astype(BF)
                rest = (prob - prob_low.astype(F32)).astype(BF)
                values = vs_ref[slot, kb]
                low_sum = low_sum + dotf(heads_beside(prob_low, size), values)
                rest_sum = rest_sum + dotf(heads_beside(rest, size), values)
            return (low_sum, rest_sum)

        zero = jnp.zeros((size, GW), F32)
        low_sum, rest_sum = loop(slots, out_step, (zero, zero))
        full_ref[qb] = low_sum + rest_sum
        out_ref[qb] = turned(low_sum).astype(BF)


VM = pl.BlockSpec(memory_space=pltpu.VMEM)
SM = pl.BlockSpec(memory_space=pltpu.SMEM)


def attention_forward(place, q, kv, start, bias):
    groups, size, _ = q.shape
    slots = kv[0].shape[0] if len(kv) == 1 else len(kv)
    return pl.pallas_call(
        forward_kernel,
        in_specs=[SM] + [VM] * (3 + len(kv)),
        out_specs=[VM] * 3,
        out_shape=(
            jax.ShapeDtypeStruct((groups, GW, size), BF),
            jax.ShapeDtypeStruct((groups, size, GW), F32),
            jax.ShapeDtypeStruct((groups, GHEADS * size, size), F32),
        ),
        scratch_shapes=[
            pltpu.VMEM((slots, groups, GHEADS * size, size), F32),
            pltpu.VMEM((slots, groups, GHEADS * size, GW), BF),
        ],
        cost_estimate=cost(7),
        name="attention_forward",
    )(place, q, *kv, start, bias)


def backward_kernel(
    place_ref,
    q_ref,
    kv_ref,
    start_ref,
    bias_ref,
    lse_ref,
    full_ref,
    out_grad_ref,
    dq_ref,
    dkv_ref,
    dist_ref,
    dist_acc,
    qs_ref,
    gs_ref,
    delta_ref,
    dkv_acc,
):
    groups, size, _ = q_ref.shape
    slots = kv_ref.shape[0]
    tall = GHEADS * size
    for block in range(groups):
        spread = heads_apart(turned_back(out_grad_ref[block].astype(F32)).astype(BF), 1)
        gs_ref[block] = spread
        full = full_ref[block]
        product = spread.astype(F32) * jnp.concatenate([full] * GHEADS, axis=0)
        delta = jnp.sum(product, axis=1, keepdims=True)
        delta_ref[block] = jnp.broadcast_to(delta, (tall, size))
    for qb in range(groups):
        qs_ref[qb] = heads_apart(q_ref[qb], 0.125)
    dq_ref[...] = jnp.zeros_like(dq_ref)

    def slot_step(slot, carry):
        dist_acc[...] = jnp.zeros_like(dist_acc)
        part, tile = bias_place(place_ref, slot)
        dkv_acc[...] = jnp.zeros_like(dkv_acc)

        def pair(kb, qb):
            key_block = kb * place_ref[1] + place_ref[2 + slot]
            query_block = qb * place_ref[1] + place_ref[0]
            key, value = kv_ref[slot, kb, :, :GW], kv_ref[slot, kb, :, GW:]
            mask = tile_mask(start_ref[qb], query_block, key_block, size)
            at = tile + qb - kb
            bias = [bias_ref[head, part, at] + mask for head in range(GHEADS)]
            queries, grads = qs_ref[qb], gs_ref[qb]
            raw = dotf(queries, key, NT)
            prob_grad = dotf(grads, value, NT)
            prob = jnp.exp(raw + (jnp.concatenate(bias, axis=0) - lse_ref[qb]))
            score_grad = (prob * (prob_grad - delta_ref[qb])).astype(BF)
            dk = dotf(score_grad, queries, TN)
            dv = dotf(prob.astype(BF), grads, TN)
            dq = dotf(heads_beside(score_grad, size), heads_apart(key, 0.125))
            return kb, qb, at, score_grad, dk, dv, dq

        def add(kb, qb, at, score_grad, dk, dv, dq):
            for head in range(GHEADS):
                dist_acc[head, at] += score_grad[head * size : (head + 1) * size].astype(F32)
            dkv_acc[kb, :, :GW] += dk
            dkv_acc[kb, :, GW:] += dv
            dq_ref[qb] += dq

        def pair_step(step, carry):
            last = (step == groups).astype(jnp.int32)
            late = (step >= groups - 1).astype(jnp.int32)
            one = pair(3 * last, step - last)
            two = pair(1 + late, step + 1 - 2 * late)
            add(*one)
            add(*two)
            return carry

        lax.fori_loop(0, groups + 1, pair_step, 0)
        dkv_ref[slot] = dkv_acc[...].astype(dkv_ref.dtype)
        row = lax.broadcasted_iota(jnp.int32, (size, size), 0)
        lane = lax.broadcasted_iota(jnp.int32, (size, size), 1)
        flip = (row + lane == size - 1).astype(F32)
        for head in range(GHEADS):
            tiles = jnp.concatenate(
                [dist_acc[head, step] for step in range(groups + 1)], axis=1
            )
            tiles = jnp.dot(flip, tiles, precision=HIGHEST)
            for step in range(groups + 1):
                tile_rows = tiles[:, step * size : (step + 1) * size]
                wide = jnp.concatenate((tile_rows, jnp.zeros_like(tile_rows)), axis=1)
                wide = pltpu.roll(wide, 1, 1, stride=1, stride_axis=0)
                dist_ref[slot, head, step : step + 1, :] = jnp.sum(wide, axis=0, keepdims=True)
        return carry

    loop(slots, slot_step, 0)


def attention_backward(place, q, kv, start, bias, lse, full, out_grad, dtype, us):
    groups, size, _ = q.shape
    slots = kv.shape[0]
    tall = GHEADS * size
    return pl.pallas_call(
        backward_kernel,
        in_specs=[SM] + [VM] * 7,
        out_specs=[VM] * 3,
        out_shape=(
            jax.ShapeDtypeStruct((groups, size, GW), F32),
            jax.ShapeDtypeStruct((slots, groups, size, 2 * GW), dtype),
            jax.ShapeDtypeStruct((slots, GHEADS, groups + 1, 2 * size), F32),
        ),
        scratch_shapes=[
            pltpu.VMEM((GHEADS, groups + 1, size, size), F32),
            pltpu.VMEM((groups, tall, GW), BF),
            pltpu.VMEM((groups, tall, GW), BF),
            pltpu.VMEM((groups, tall, size), F32),
            pltpu.VMEM((groups, size, 2 * GW), F32),
        ],
        cost_estimate=cost(us),
        name="attention_backward",
    )(place, q, kv, start, bias, lse, full, out_grad)


def project_kernel(own_ref, h0_ref, h1_ref, h2_ref, h3_ref, w_ref, q_ref, kv_ref, h_ref):
    groups, size, _ = h_ref.shape
    for step, piece_ref in enumerate((h0_ref, h1_ref, h2_ref, h3_ref)):
        h_ref[behind(step, own_ref[0], groups)] = piece_ref[...]
    rows = dotf(h_ref[...].reshape(groups * size, D), w_ref[...]).astype(BF)
    q_ref[...] = rows[:, :GW].reshape(groups, size, GW)
    kv_ref[...] = rows[:, GW:].reshape(groups, size, 2 * GW)


def project(own, pieces, w_cols):
    size = pieces[0].shape[0]
    return pl.pallas_call(
        project_kernel,
        in_specs=[SM] + [VM] * 5,
        out_specs=[VM] * 3,
        out_shape=(
            jax.ShapeDtypeStruct((GROUPS, size, GW), BF),
            jax.ShapeDtypeStruct((GROUPS, size, 2 * GW), BF),
            jax.ShapeDtypeStruct((GROUPS, size, D), BF),
        ),
        cost_estimate=cost(0.05),
        name="project",
    )(own, *pieces, w_cols)


def mlp_in_kernel(
    att_ref, w_ref, x_ref, gain_ref, disp_ref, resid_ref, sent_ref
):
    total = x_ref[...]
    for group in range(GROUPS):
        total = total + dotf(att_ref[group], w_ref[group], TN)
    resid_ref[...] = total
    rate = lax.rsqrt(jnp.mean(total * total, axis=-1, keepdims=True) + EPS)
    low = (total * rate * gain_ref[...]).astype(BF)
    sent_ref[...] = dotf(disp_ref[...], low).astype(BF)


def mlp_in(att, w_attn, x, gain, disp):
    return pl.pallas_call(
        mlp_in_kernel,
        in_specs=[VM] * 5,
        out_specs=[VM] * 2,
        out_shape=(
            jax.ShapeDtypeStruct(x.shape, F32),
            jax.ShapeDtypeStruct((disp.shape[0], D), BF),
        ),
        cost_estimate=cost(0.05),
        name="mlp_in",
    )(att, w_attn, x, gain, disp)


def expert_kernel(
    own_ref,
    x_ref,
    came_ref,
    w_in_ref,
    w_out_ref,
    router_ref,
    active_ref,
    hidden_grad_ref,
    out_grad_ref,
    back_ref,
    out_ref,
    router_grad_ref,
    out_acc,
    back_acc,
    gate_ref,
):
    step = pl.program_id(0)
    rows = x_ref[...]
    lane = lax.broadcasted_iota(jnp.int32, (rows.shape[0], 128), 1)

    @pl.when(step == 0)
    def _():
        logits = dotf(rows, router_ref[...])
        pair = came_ref[:, D:].astype(F32)
        own = jnp.sum(jnp.where(lane == own_ref[0], logits, 0.0), axis=1, keepdims=True)
        other = jnp.where(lane == own_ref[0], 0.0, pair)
        other = jnp.sum(other * logits, axis=1, keepdims=True)
        peak = jnp.maximum(own, other)
        own_e, other_e = jnp.exp(own - peak), jnp.exp(other - peak)
        total = own_e + other_e
        own_gate = own_e / total
        gate_ref[0] = jnp.broadcast_to(own_gate, lane.shape)
        gate_ref[1] = jnp.broadcast_to(other_e / total, lane.shape)
        out_grad_ref[...] = (own_gate * came_ref[:, :D].astype(F32)).astype(BF)
        out_acc[...] = jnp.zeros_like(out_acc)
        back_acc[...] = jnp.zeros_like(back_acc)

    half = rows.shape[0] // 2

    def half_step(part, carry):
        at = pl.ds(pl.multiple_of(part * half, half), half)
        hidden = dotf(x_ref[at, :], w_in_ref[...])
        active_grad = dotf(out_grad_ref[at, :], w_out_ref[...], NT)
        value, slope = gelu_parts(hidden)
        active = value.astype(BF)
        hidden_grad = (slope * active_grad).astype(BF)
        active_ref[at, :] = active
        hidden_grad_ref[at, :] = hidden_grad
        out_acc[at, :] += dotf(active, w_out_ref[...])
        back_acc[at, :] += dotf(hidden_grad, w_in_ref[...], NT)
        return carry

    lax.fori_loop(0, 2, half_step, 0)

    @pl.when(step == pl.num_programs(0) - 1)
    def _():
        produced = out_acc[...].astype(BF).astype(F32)
        own_gate, other_gate = gate_ref[0][:, :1], gate_ref[1][:, :1]
        out_ref[...] = (own_gate * produced).astype(BF)
        gate_grad = jnp.sum(came_ref[:, :D].astype(F32) * produced, axis=1, keepdims=True)
        pull = own_gate * other_gate * gate_grad
        pair = came_ref[:, D:].astype(F32)
        logit_rows = pull * jnp.where(lane == own_ref[0], 1.0, -pair)
        high = logit_rows.astype(BF)
        rest = (logit_rows - high.astype(F32)).astype(BF)
        router = router_ref[...]
        back = back_acc[...].astype(BF).astype(F32)
        back = back + dotf(high, router, NT) + dotf(rest, router, NT)
        back_ref[...] = back.astype(BF)
        router_grad_ref[...] = dotf(rows, high, TN) + dotf(rows, rest, TN)


def expert_layer(own, x, came, w_in, w_out, router):
    count = x.shape[0]
    steps = 4
    part = FF // steps
    whole = lambda *shape: pl.BlockSpec(shape, lambda f, own: (0,) * len(shape))
    piece = pl.BlockSpec((count, part), lambda f, own: (0, own[1 + f]))
    return pl.pallas_call(
        expert_kernel,
        grid_spec=pltpu.PrefetchScalarGridSpec(
            num_scalar_prefetch=1,
            grid=(steps,),
            in_specs=[
                whole(count, D),
                whole(count, D + 128),
                pl.BlockSpec((D, part), lambda f, own: (0, f)),
                pl.BlockSpec((part, D), lambda f, own: (f, 0)),
                whole(D, 128),
            ],
            out_specs=[
                piece,
                piece,
                whole(count, D),
                whole(count, D),
                whole(count, D),
                whole(D, 128),
            ],
            scratch_shapes=[
                pltpu.VMEM((count, D), F32),
                pltpu.VMEM((count, D), F32),
                pltpu.VMEM((2, count, 128), F32),
            ],
        ),
        out_shape=(
            jax.ShapeDtypeStruct((count, FF), BF),
            jax.ShapeDtypeStruct((count, FF), BF),
            jax.ShapeDtypeStruct((count, D), BF),
            jax.ShapeDtypeStruct((count, D), BF),
            jax.ShapeDtypeStruct((count, D), BF),
            jax.ShapeDtypeStruct((D, 128), F32),
        ),
        cost_estimate=cost(0.05),
        name="expert_layer",
    )(own, x, came, w_in, w_out, router)


def mlp_back_kernel(
    back_ref, disp_ref, resid_ref, up_ref, gain_ref, w_ref, grad_ref, low_ref, gain_grad_ref, out_ref
):
    grad = dotf(disp_ref[...], back_ref[...], TN)
    resid = resid_ref[...]
    rate = lax.rsqrt(jnp.mean(resid * resid, axis=-1, keepdims=True) + EPS)
    unit = resid * rate
    gain_grad_ref[...] = jnp.sum(grad * unit, axis=0, keepdims=True)
    scaled = grad * gain_ref[...]
    total = up_ref[...] + rate * (
        scaled - unit * jnp.mean(scaled * unit, axis=-1, keepdims=True)
    )
    grad_ref[...] = total
    low = total.astype(BF)
    low_ref[...] = low
    for group in range(GROUPS):
        out_ref[group] = dotf(w_ref[group], low, NT).astype(BF)


def mlp_back(back, disp, resid, up, gain, w_attn):
    size = resid.shape[0]
    return pl.pallas_call(
        mlp_back_kernel,
        in_specs=[VM] * 6,
        out_specs=[VM] * 4,
        out_shape=(
            jax.ShapeDtypeStruct((size, D), F32),
            jax.ShapeDtypeStruct((size, D), BF),
            jax.ShapeDtypeStruct((1, D), F32),
            jax.ShapeDtypeStruct((GROUPS, GW, size), BF),
        ),
        cost_estimate=cost(4),
        name="mlp_back",
    )(back, disp, resid, up, gain, w_attn)


def project_back_kernel(
    dq_ref,
    dq_other_ref,
    dkv_ref,
    came_ref,
    w_ref,
    h_ref,
    gain_ref,
    dproj_ref,
    gain_grad_ref,
    half_ref,
):
    groups, size, _ = dq_ref.shape
    dq = (dq_ref[...] + dq_other_ref[...]).astype(BF).reshape(groups * size, GW)
    dkv = (dkv_ref[...] + came_ref[...].astype(F32)).astype(BF)
    dkv = dkv.reshape(groups * size, 2 * GW)
    dproj_ref[...] = jnp.concatenate((dq, dkv), axis=1)
    total = jnp.zeros((1, D), F32)
    for block in range(groups):
        half = dotf(dproj_ref[block * size : (block + 1) * size], w_ref[...], NT)
        half_ref[block] = half.astype(BF)
        total = total + jnp.sum(half * h_ref[block].astype(F32), axis=0, keepdims=True)
    gain_grad_ref[...] = total / gain_ref[...]


def project_back(dq, dq_other, dkv, came, w_cols, h_col, gain):
    groups, size, _ = dq.shape
    return pl.pallas_call(
        project_back_kernel,
        in_specs=[VM] * 7,
        out_specs=[VM] * 3,
        out_shape=(
            jax.ShapeDtypeStruct((groups * size, 3 * GW), BF),
            jax.ShapeDtypeStruct((1, D), F32),
            jax.ShapeDtypeStruct((groups, size, D), BF),
        ),
        cost_estimate=cost(4),
        name="project_back",
    )(dq, dq_other, dkv, came, w_cols, h_col, gain)


def qkv_grad_kernel(h_ref, dproj_ref, grad_ref):
    ranks, rows, _ = grad_ref.shape
    groups, size, _ = h_ref.shape
    total = dotf(h_ref[...].reshape(groups * size, D), dproj_ref[...], TN)
    for rank in range(ranks):
        grad_ref[rank] = total[rank * rows : (rank + 1) * rows]


def qkv_grad_of(h_col, dproj, ranks):
    return pl.pallas_call(
        qkv_grad_kernel,
        in_specs=[VM] * 2,
        out_specs=VM,
        out_shape=jax.ShapeDtypeStruct((ranks, D // ranks, 3 * GW), F32),
        cost_estimate=cost(0.05),
        name="qkv_grad",
    )(h_col, dproj)


def side_grad_kernel(att_ref, grad_ref, router_ref, out_ref):
    ranks, rows, _ = out_ref.shape
    inner = ranks // GROUPS
    for block in range(GROUPS):
        total = dotf(att_ref[block], grad_ref[...])
        for part in range(inner):
            out_ref[block * inner + part, :, :D] = total[part * rows : (part + 1) * rows]
    for rank in range(ranks):
        out_ref[rank, :, D:] = router_ref[rank * rows : (rank + 1) * rows]


def side_grad_of(att, grad, router_grad, ranks):
    return pl.pallas_call(
        side_grad_kernel,
        in_specs=[VM] * 3,
        out_specs=VM,
        out_shape=jax.ShapeDtypeStruct((ranks, D // ranks, D + 128), F32),
        cost_estimate=cost(0.05),
        name="side_grad",
    )(att, grad, router_grad)


def assemble_kernel(own_ref, p0_ref, p1_ref, p2_ref, p3_ref, rows_ref, scratch):
    side = D + 128
    wide = side + 3 * GW
    last = side + 3 * D
    width = (p0_ref.shape[1] - wide) // 2
    pieces = [ref[...].astype(F32) for ref in (p0_ref, p1_ref, p2_ref, p3_ref)]
    total = pieces[0] + pieces[1] + pieces[2] + pieces[3]
    rows_ref[:, :side] = total[:, :side].astype(BF)
    small = total[:, wide : wide + width] + total[:, wide + width :]
    high = small.astype(BF)
    rows_ref[:, last : last + width] = high
    rows_ref[:, last + width :] = (small - high.astype(F32)).astype(BF)
    for step, piece in enumerate(pieces):
        scratch[behind(step, own_ref[0], GROUPS)] = piece[:, side:wide]
    for group in range(GROUPS):
        for kind in range(3):
            at = side + (kind * GROUPS + group) * GW
            rows_ref[:, at : at + GW] = scratch[group, :, kind * GW : (kind + 1) * GW].astype(BF)


def assemble(own, parts):
    rows, width = parts[0].shape
    return pl.pallas_call(
        assemble_kernel,
        in_specs=[SM] + [VM] * 4,
        out_specs=VM,
        out_shape=jax.ShapeDtypeStruct((rows, width + 3 * D - 3 * GW), BF),
        scratch_shapes=[pltpu.VMEM((GROUPS, rows, 3 * GW), F32)],
        cost_estimate=cost(0.05),
        name="assemble",
    )(own, *parts)


def unpack_kernel(own_ref, pair_ref, came_ref, attn_ref, router_ref, qkv_ref, small_ref):
    experts = router_ref.shape[2]
    last = 4 * D + 128
    width = small_ref.shape[1]
    small = jnp.zeros(small_ref.shape, F32)
    for near, ref in ((own_ref[0], pair_ref), (1 - own_ref[0], came_ref)):
        for part in range(2):
            value = ref[part].astype(F32)
            attn_ref[near * 2 + part] = value[:, :D]
            router_ref[near * 2 + part] = value[:, D : D + experts]
            qkv_ref[near * 2 + part] = value[:, D + 128 : last]
            small = small + (value[:, last : last + width] + value[:, last + width :])
    small_ref[...] = small


def unpack(own, pair, came, experts):
    rows = pair.shape[1]
    width = (pair.shape[2] - 4 * D - 128) // 2
    outs = pl.pallas_call(
        unpack_kernel,
        in_specs=[SM] + [VM] * 2,
        out_specs=[VM] * 4,
        out_shape=[jax.ShapeDtypeStruct((4, rows, n), F32) for n in (D, experts, 3 * D)]
        + [jax.ShapeDtypeStruct((rows, width), F32)],
        cost_estimate=cost(0.05),
        name="unpack",
    )(own.astype(jnp.int32), pair, came)
    return [out.reshape(4 * rows, -1) for out in outs[:3]] + [outs[3]]


def gelu_parts(hidden):
    scale = math.sqrt(2.0 / math.pi)
    square = hidden * hidden
    bend = jnp.tanh(hidden * (scale + (scale * 0.044715) * square))
    half = 0.5 + 0.5 * bend
    slope = scale + (3 * scale * 0.044715) * square
    return hidden * half, half + (0.5 * hidden) * (1.0 - bend * bend) * slope


def swap(value, axis):
    return lax.ppermute(value, axis, [(0, 1), (1, 0)])


def tie(*values):
    return lax.optimization_barrier(values)


def turn(value, step):
    return lax.ppermute(value, "g", [(j, (j + step) % GROUPS) for j in range(GROUPS)])


def in_turn(pieces, g):
    pieces = jnp.stack(pieces[::-1] * 2)
    return lax.dynamic_slice_in_dim(pieces, GROUPS - 1 - g, GROUPS, 0)


def exchange(value, axes):
    return lax.all_to_all(value, axes, split_axis=0, concat_axis=0, tiled=True)


def in_order(own, came, index):
    return jnp.where(index == 0, jnp.stack((own, came)), jnp.stack((came, own)))


def rep_gather(value, y, c):
    pair = in_order(value, swap(value, "y"), y)
    return in_order(pair, swap(pair, "c"), c)


def halve(value, index, axis):
    count, rows, cols = value.shape
    value = value.reshape(count, 2, rows // 2, cols)
    away = swap(pick(value, 1 - index, 1).astype(BF), axis)
    return pick(value, index, 1) + away.astype(F32)


def pick(value, index, axis):
    return lax.dynamic_index_in_dim(value, index, axis, keepdims=False)


def norm_backward(grad, gain, value):
    rate = lax.rsqrt(jnp.mean(value * value, axis=-1, keepdims=True) + EPS)
    unit = value * rate
    scaled = grad * gain
    return rate * (scaled - unit * jnp.mean(scaled * unit, axis=-1, keepdims=True))


def local(
    tokens,
    cotangent,
    gain_attn,
    gain_mlp,
    w_qkv,
    w_attn_out,
    router,
    rel_table,
    w_in,
    w_out,
    segment_ids,
    expert_ids,
    rel_bucket,
):
    groups, inner = lax.axis_size("g"), lax.axis_size("i")
    g, i = lax.axis_index("g"), lax.axis_index("i")
    y, c = lax.axis_index("y"), lax.axis_index("c")
    ranks = groups * inner
    copies = 4
    size = tokens.shape[1]
    experts = ranks
    capacity = max(2, 4 * size // experts)
    inputs = tokens[0]
    upstream = cotangent[0]
    seg_all = segment_ids[0]
    chosen_ids = expert_ids[0]
    rows = w_qkv.shape[0] // copies
    me = g * inner + i
    own_g = g[None].astype(jnp.int32)

    rate = lax.rsqrt(jnp.mean(inputs * inputs, axis=-1, keepdims=True) + EPS)
    h_attn = (inputs * rate * gain_attn).astype(BF)
    h_pieces = [h_attn] + [turn(h_attn, step) for step in range(1, groups)]

    part = lax.dynamic_slice_in_dim(w_qkv, c * 2 * rows, 2 * rows, 0).astype(BF)
    part = part.reshape(2 * rows, 3, groups, GW).transpose(2, 0, 1, 3)
    part = jnp.broadcast_to(part[:, None], (groups, inner, 2 * rows, 3, GW))
    part = exchange(part.reshape(ranks, 2 * rows, 3 * GW), SEQ)
    both = jnp.concatenate((w_attn_out, jnp.pad(router, ((0, 0), (0, 128 - experts)))), axis=1)
    both = lax.dynamic_slice_in_dim(both, (c * 2 + y) * rows, rows, 0).astype(BF)
    both = jnp.broadcast_to(both[None], (ranks, rows, D + 128))
    w_cols = in_order(part, swap(part, "c"), c).swapaxes(0, 1).reshape(D, 3 * GW)

    expert_iota = jnp.arange(experts, dtype=jnp.int32)
    token_iota = jnp.arange(size, dtype=jnp.int32)
    pair_hot = jnp.any(chosen_ids[:, :, None] == expert_iota[None, None, :], axis=1)
    rank = jnp.dot(
        (token_iota[:, None] > token_iota[None, :]).astype(BF),
        pair_hot.astype(BF),
        preferred_element_type=F32,
    ).astype(jnp.int32)
    disp = (rank.T[:, None, :] == jnp.arange(capacity, dtype=jnp.int32)[None, :, None]) & (
        pair_hot.T[:, None, :]
    )
    disp = disp.astype(BF).reshape(experts * capacity, size)
    early = jnp.concatenate(
        (upstream.astype(BF), jnp.pad(pair_hot.astype(BF), ((0, 0), (0, 128 - experts)))), axis=1
    )
    early = jnp.dot(disp, early, preferred_element_type=F32).astype(BF)
    seg_col = pick(seg_all.reshape(groups, inner, size), i, 1)
    start = jnp.sum(
        (seg_all[None, None, :] < seg_col[:, :, None]).astype(jnp.int32), axis=-1, keepdims=True
    )
    padded = jnp.concatenate(
        (jnp.full((size - 1,), -1, jnp.int32), rel_bucket, jnp.full((1,), -1, jnp.int32))
    )
    reversed_bucket = padded.reshape(ranks + 1, size)[:, ::-1].reshape(-1)
    bucket_hot = (
        jnp.arange(BUCKETS, dtype=jnp.int32)[:, None] == reversed_bucket[None, :]
    ).astype(F32)
    table = lax.dynamic_slice_in_dim(rel_table, g * GHEADS, GHEADS, 0)
    bias_rows = jnp.dot(table, bucket_hot, precision=HIGHEST).reshape(GHEADS, ranks + 1, size)
    bias = bias_tiles(bias_rows, inner)
    bias, start, *h_pieces = tie(bias, start, *h_pieces)

    early = jnp.concatenate((early.reshape(ranks, capacity, D + 128), both), axis=1)
    early, *h_pieces = tie(early, *h_pieces)
    q, kv, h_col = project(own_g, h_pieces, w_cols)
    came_rows = exchange(early, SEQ)
    head_place = jnp.stack((i, jnp.int32(inner)))

    def place_of(columns):
        return jnp.concatenate((head_place, columns, own_g)).astype(jnp.int32)

    if inner == 2:
        kv_came = swap(kv, "i")
        kv_all = (kv, kv_came)
        columns = jnp.stack((i, 1 - i))
    else:
        kv_all = (lax.all_gather(kv, "i"),)
        columns = jnp.arange(inner, dtype=jnp.int32)
    place = place_of(columns)
    mixed, mixed_full, lse = attention_forward(place, q, kv_all, start, bias)
    mixed, came_rows = tie(mixed, came_rows)
    both = came_rows[:, capacity:]
    both = in_order(both, swap(both, "y"), y)
    came_rows = came_rows[:, :capacity].reshape(ranks * capacity, D + 128)
    att = exchange(mixed, "g")
    att, both = tie(att, both)
    both = in_order(both, swap(both, "c"), c)
    both = both.transpose(2, 0, 1, 3, 4).reshape(D, D + 128)
    w_attn_low = both[:, :D].reshape(groups, GW, D)
    router_low = both[:, D:]
    residual, outgoing = mlp_in(att, w_attn_low, inputs, gain_mlp[None], disp)

    arrived = exchange(outgoing.reshape(ranks, capacity, D), SEQ).reshape(ranks * capacity, D)
    active, hidden_grad, produced_grad, back, produced, router_grad = expert_layer(
        jnp.stack([me] + [2 * (c == f % 2) + (y == f // 2) for f in range(4)]).astype(jnp.int32),
        arrived,
        came_rows, w_in[0], w_out[0], router_low
    )
    back_rows = exchange(back.reshape(ranks, capacity, D), SEQ).reshape(ranks * capacity, D)

    part_ff = FF // 4
    slices = [slice(f * part_ff, (f + 1) * part_ff) for f in range(4)]

    def part_grads(f, active=active, hidden_grad=hidden_grad):
        return (
            dotf(active[:, slices[f]], produced_grad, TN),
            dotf(arrived, hidden_grad[:, slices[f]], TN),
        )

    core_far = [swap(grad.astype(BF), "c") for grad in part_grads(0)]
    near = [grad.astype(BF) for grad in part_grads(1)]
    away = [
        (grad + core.astype(F32)).astype(BF) for grad, core in zip(part_grads(2), core_far)
    ]
    far_out = swap(away[0], "y")
    back_rows, *near = tie(back_rows, *near)

    resid_grad, attn_grad, gain_two, out_grad = mlp_back(
        back_rows, disp, residual, upstream, gain_mlp[None], w_attn_low
    )
    out_grad = exchange(out_grad, "g")
    side_grad = side_grad_of(att, attn_grad, router_grad, ranks)
    out_grad, produced, side_grad, away_in = tie(out_grad, produced, side_grad, away[1])
    far_in = swap(away_in, "y")
    near = [swap(grad, "c") for grad in near]
    returned = exchange(produced.reshape(ranks, capacity, D), SEQ)

    def inner_reduce(value):
        value = value.reshape(groups, inner, *value.shape[1:])
        if inner > 2:
            return lax.psum_scatter(value, "i", scatter_dimension=1).astype(BF)
        own = pick(value, i, 1) + swap(pick(value, 1 - i, 1).astype(BF), "i").astype(F32)
        return own.astype(BF)

    if inner == 2:
        dq_other, dkv_other, dist_other = attention_backward(
            place_of(1 - i[None]),
            q,
            kv_came[None],
            start,
            bias,
            lse,
            mixed_full,
            out_grad,
            BF,
            8,
        )
        out_grad, dq_other, dkv_other, far_out = tie(out_grad, dq_other, dkv_other, far_out)
        dkv_came = swap(dkv_other[0], "i")
        dq, dkv_own, dist = attention_backward(
            place_of(i[None]),
            q,
            kv[None],
            start,
            bias,
            lse,
            mixed_full,
            out_grad,
            F32,
            1,
        )
        dkv_own = dkv_own[0]
        dist = jnp.concatenate((dist, dist_other))
    else:
        dq, dkv_all, dist = attention_backward(
            place, q, kv_all[0], start, bias, lse, mixed_full, out_grad, F32, 1
        )
        dkv_own = lax.psum_scatter(dkv_all, "i")
        dkv_came = jnp.zeros(dkv_own.shape, BF)
        dq_other = jnp.zeros_like(dq)
        dist = jnp.take(dist, (i - jnp.arange(inner)) % inner, axis=0)
    dkv_own, returned, far_in = tie(dkv_own, returned, far_in)
    returned = returned.reshape(ranks * capacity, D)
    dproj, gain_one, half = project_back(
        dq, dq_other, dkv_own, dkv_came, w_cols, h_col, gain_attn[None]
    )
    half = exchange(half, "g")
    dproj, side_grad = tie(dproj, side_grad)
    side_grad = halve(side_grad, c, "c")
    dproj, side_grad = tie(dproj, side_grad)
    parts = halve(qkv_grad_of(h_col, dproj, ranks), c, "c")
    parts, gain_one, gain_two, dist = tie(
        jnp.concatenate((side_grad, parts), axis=2), gain_one, gain_two, dist
    )
    parts = halve(parts, y, "y")
    parts, half, active, hidden_grad, *near = tie(parts, half, active, hidden_grad, *near)
    mine_out, mine_in = [
        grad + core.astype(F32) for grad, core in zip(part_grads(3, active, hidden_grad), near)
    ]
    dist = dist[:, :, 1:].transpose(1, 2, 0, 3).reshape(GHEADS, ranks, 2 * size)
    dist_rows = jnp.pad(dist[:, :, size:], ((0, 0), (0, 1), (0, 0))) + jnp.pad(
        dist[:, :, :size], ((0, 0), (1, 0), (0, 0))
    )
    table_grad = jnp.dot(dist_rows.reshape(GHEADS, -1), bucket_hot.T, precision=HIGHEST)
    table_all = lax.dynamic_update_slice(
        jnp.zeros((HEADS, BUCKETS), F32), table_grad, (g * GHEADS, 0)
    )
    small = jnp.concatenate((gain_one[0], gain_two[0], table_all.reshape(-1)))
    count = small.shape[0]
    width = -(-count // (rows * 128)) * 128
    small = jnp.pad(small.reshape(-1, 128), ((0, (rows * width - count) // 128), (0, 0)))
    small = small.reshape(rows, width)
    small = small + (swap(small, "i") if inner == 2 else lax.psum(small, "i") - small)
    high = lax.reduce_precision(small, 8, 7)
    small = jnp.concatenate((high, small - high), axis=1).astype(BF)
    small = jnp.broadcast_to(small[None], (groups, rows, 2 * width))

    parts = jnp.concatenate((inner_reduce(parts), small), axis=2)
    parts = [pick(parts, g, 0)] + [
        turn(pick(parts, lax.rem(g + step, groups), 0), step) for step in range(1, groups)
    ]
    norm_in_grad = jnp.sum(half.astype(F32), axis=0)
    input_grad = resid_grad + norm_backward(norm_in_grad, gain_attn, inputs)
    result = residual + dotf(disp, returned, TN)
    shards = assemble(own_g, parts)
    pair = in_order(shards, swap(shards, "y"), y)
    attn_shard, router_shard, qkv_shard, small = unpack(c[None], pair, swap(pair, "c"), experts)
    small = small.reshape(-1)
    w_in_shard = mine_in + far_in.astype(F32)
    w_out_shard = mine_out + far_out.astype(F32)
    return (
        result[None],
        input_grad[None],
        small[:D],
        small[D : 2 * D],
        qkv_shard,
        attn_shard,
        router_shard,
        small[2 * D : 2 * D + HEADS * BUCKETS].reshape(HEADS, BUCKETS),
        w_in_shard[None],
        w_out_shard[None],
    )


def solution(mesh):
    ranks = mesh.shape["seq"]
    split = Mesh(
        mesh.devices.reshape(2, mesh.shape["rep"] // 2, GROUPS, ranks // GROUPS),
        ("y", "c", "g", "i"),
    )
    placed = (
        P(REP, SEQ, None),
        P(REP, SEQ, None),
        P(),
        P(),
        P(SEQ, None),
        P(SEQ, None),
        P(SEQ, None),
        P(),
        P(SEQ, None, None),
        P(SEQ, None, None),
        P(REP, None),
        P(REP, SEQ, None),
        P(),
    )
    return jax.shard_map(
        local,
        mesh=split,
        in_specs=placed,
        out_specs=(
            P(REP, SEQ, None),
            P(REP, SEQ, None),
            P(),
            P(),
            P(SEQ, None),
            P(SEQ, None),
            P(SEQ, None),
            P(),
            P(SEQ, None, REP),
            P(SEQ, REP, None),
        ),
        check_vma=False,
    )
```

```python
from functools import partial
import math

import jax
import jax.numpy as jnp
from jax import lax
from jax.experimental import pallas as pl
from jax.experimental.pallas import tpu as pltpu
from jax.sharding import Mesh, PartitionSpec as P

D = 768
HEADS = 12
HEAD = 64
BUCKETS = 32
FF = 3072
GROUPS = 4
GHEADS = HEADS // GROUPS
GW = GHEADS * HEAD
EPS = 1e-06
HIGHEST = lax.Precision.HIGHEST
BF = jnp.bfloat16
F32 = jnp.float32
NT = (((1,), (1,)), ((), ()))
TN = (((0,), (0,)), ((), ()))
SEQ = ("g", "i")
REP = ("y", "c")


def dotf(a, b, dims=(((1,), (0,)), ((), ()))):
    return lax.dot_general(a, b, dims, preferred_element_type=F32)


def loop(count, body, init):
    if count <= 2:
        for step in range(count):
            init = body(step, init)
        return init
    return lax.fori_loop(0, count, body, init)


def ahead(block, own, count):
    return lax.rem(block + count - own, count)


def behind(step, own, count):
    return lax.rem(own + count - step, count)


def heads_apart(value, scale):
    lane = lax.broadcasted_iota(jnp.int32, value.shape, 1)
    value = value * jnp.asarray(scale, value.dtype)
    return jnp.concatenate(
        [jnp.where(lane // HEAD == head, value, jnp.zeros_like(value)) for head in range(GHEADS)],
        axis=0,
    )


def heads_beside(value, size):
    return jnp.concatenate(
        [value[head * size : (head + 1) * size] for head in range(GHEADS)], axis=1
    )


def turned(value):
    wide = jnp.concatenate((value, jnp.zeros((value.shape[0], -GW % 128), F32)), axis=1)
    return wide.T[:GW]


def turned_back(value):
    tall = jnp.concatenate((value, jnp.zeros((-GW % 128, value.shape[1]), F32)), axis=0)
    return tall.T[:, :GW]


def tile_mask(start, query_block, key_block, size):
    lane = lax.broadcasted_iota(jnp.int32, (size, size), 1)
    row = lax.broadcasted_iota(jnp.int32, (size, size), 0)
    allowed = (lane >= start - key_block * size) & (
        lane - row <= (query_block - key_block) * size
    )
    return jnp.where(allowed, 0.0, -1e30)


def bias_kernel(rows_ref, tiles_ref):
    heads, inner, count, size, _ = tiles_ref.shape

    def head_step(head, carry):
        for part in range(inner):
            tiles_ref[head, part, 0] = jnp.zeros((size, size), F32)
            for step in range(count - 1):
                gap = step * inner + part
                pair = jnp.concatenate(
                    (rows_ref[head, gap : gap + 1, :], rows_ref[head, gap + 1 : gap + 2, :]),
                    axis=1,
                )
                spread = jnp.broadcast_to(pair, (size, 2 * size))
                spread = pltpu.roll(spread, 0, 1, stride=1, stride_axis=0)
                tiles_ref[head, part, step + 1] = spread[:, :size]
        return carry

    lax.fori_loop(0, heads, head_step, 0)


def cost(us):
    return pl.CostEstimate(flops=0, bytes_accessed=int(us * 3.4e6), transcendentals=0)


def bias_tiles(rows, inner):
    heads, count, size = rows.shape
    return pl.pallas_call(
        bias_kernel,
        out_shape=jax.ShapeDtypeStruct((heads, inner, (count - 1) // inner + 1, size, size), F32),
        cost_estimate=cost(0.05),
        name="bias_tiles",
    )(rows)


def block_of(kv_refs, slot, kb):
    if len(kv_refs) == 1:
        return kv_refs[0][slot, kb]
    return kv_refs[slot][kb]


def bias_place(place_ref, slot):
    shift = place_ref[0] - place_ref[2 + slot]
    below = (shift < 0).astype(jnp.int32)
    return shift + below * place_ref[1], 1 - below


def forward_kernel(
    place_ref,
    q_ref,
    *refs,
):
    groups, size, _ = q_ref.shape
    kv_refs, (start_ref, bias_ref, out_ref, full_ref, lse_ref, s_ref, vs_ref) = refs[:-7], refs[-7:]
    slots = s_ref.shape[0]
    tall = GHEADS * size

    def spread_step(slot, carry):
        for kb in range(groups):
            vs_ref[slot, kb] = heads_apart(block_of(kv_refs, slot, kb)[:, GW:], 1)
        return carry

    loop(slots, spread_step, 0)
    for qb in range(groups):
        queries = heads_apart(q_ref[qb], 0.125)
        start = start_ref[qb]
        query_block = qb * place_ref[1] + place_ref[0]

        def score_step(slot, top):
            part, tile = bias_place(place_ref, slot)
            for kb in range(qb + 1):
                key_block = kb * place_ref[1] + place_ref[2 + slot]
                mask = tile_mask(start, query_block, key_block, size)
                raw = dotf(queries, block_of(kv_refs, slot, kb)[:, :GW], NT)
                bias = [bias_ref[head, part, tile + qb - kb] + mask for head in range(GHEADS)]
                score = raw + jnp.concatenate(bias, axis=0)
                s_ref[slot, kb] = score
                top = jnp.maximum(top, score)
            return top

        top = loop(slots, score_step, jnp.full((tall, size), -1e30, F32))
        top = jnp.broadcast_to(jnp.max(top, axis=1, keepdims=True), (tall, size))

        def exp_step(slot, total):
            for kb in range(qb + 1):
                value = jnp.exp(s_ref[slot, kb] - top)
                s_ref[slot, kb] = value
                total = total + value
            return total

        total = loop(slots, exp_step, jnp.zeros((tall, size), F32))
        total = jnp.broadcast_to(jnp.sum(total, axis=1, keepdims=True), (tall, size))
        scale = 1.0 / total
        lse_ref[qb] = top + jnp.log(total)

        def out_step(slot, sums):
            low_sum, rest_sum = sums
            for kb in range(qb + 1):
                prob = s_ref[slot, kb] * scale
                prob_low = prob.astype(BF)
                rest = (prob - prob_low.astype(F32)).astype(BF)
                values = vs_ref[slot, kb]
                low_sum = low_sum + dotf(heads_beside(prob_low, size), values)
                rest_sum = rest_sum + dotf(heads_beside(rest, size), values)
            return (low_sum, rest_sum)

        zero = jnp.zeros((size, GW), F32)
        low_sum, rest_sum = loop(slots, out_step, (zero, zero))
        full_ref[qb] = low_sum + rest_sum
        out_ref[qb] = turned(low_sum).astype(BF)


VM = pl.BlockSpec(memory_space=pltpu.VMEM)
SM = pl.BlockSpec(memory_space=pltpu.SMEM)


def attention_forward(place, q, kv, start, bias):
    groups, size, _ = q.shape
    slots = kv[0].shape[0] if len(kv) == 1 else len(kv)
    return pl.pallas_call(
        forward_kernel,
        in_specs=[SM] + [VM] * (3 + len(kv)),
        out_specs=[VM] * 3,
        out_shape=(
            jax.ShapeDtypeStruct((groups, GW, size), BF),
            jax.ShapeDtypeStruct((groups, size, GW), F32),
            jax.ShapeDtypeStruct((groups, GHEADS * size, size), F32),
        ),
        scratch_shapes=[
            pltpu.VMEM((slots, groups, GHEADS * size, size), F32),
            pltpu.VMEM((slots, groups, GHEADS * size, GW), BF),
        ],
        cost_estimate=cost(7),
        name="attention_forward",
    )(place, q, *kv, start, bias)


def backward_kernel(
    place_ref,
    q_ref,
    kv_ref,
    start_ref,
    bias_ref,
    lse_ref,
    full_ref,
    out_grad_ref,
    dq_ref,
    dkv_ref,
    dist_ref,
    dist_acc,
    qs_ref,
    gs_ref,
    delta_ref,
    dkv_acc,
):
    groups, size, _ = q_ref.shape
    slots = kv_ref.shape[0]
    tall = GHEADS * size
    for block in range(groups):
        spread = heads_apart(turned_back(out_grad_ref[block].astype(F32)).astype(BF), 1)
        gs_ref[block] = spread
        full = full_ref[block]
        product = spread.astype(F32) * jnp.concatenate([full] * GHEADS, axis=0)
        delta = jnp.sum(product, axis=1, keepdims=True)
        delta_ref[block] = jnp.broadcast_to(delta, (tall, size))
    for qb in range(groups):
        qs_ref[qb] = heads_apart(q_ref[qb], 0.125)
    dq_ref[...] = jnp.zeros_like(dq_ref)

    def slot_step(slot, carry):
        dist_acc[...] = jnp.zeros_like(dist_acc)
        part, tile = bias_place(place_ref, slot)
        dkv_acc[...] = jnp.zeros_like(dkv_acc)

        def pair(kb, qb):
            key_block = kb * place_ref[1] + place_ref[2 + slot]
            query_block = qb * place_ref[1] + place_ref[0]
            key, value = kv_ref[slot, kb, :, :GW], kv_ref[slot, kb, :, GW:]
            mask = tile_mask(start_ref[qb], query_block, key_block, size)
            at = tile + qb - kb
            bias = [bias_ref[head, part, at] + mask for head in range(GHEADS)]
            queries, grads = qs_ref[qb], gs_ref[qb]
            raw = dotf(queries, key, NT)
            prob_grad = dotf(grads, value, NT)
            prob = jnp.exp(raw + (jnp.concatenate(bias, axis=0) - lse_ref[qb]))
            score_grad = (prob * (prob_grad - delta_ref[qb])).astype(BF)
            dk = dotf(score_grad, queries, TN)
            dv = dotf(prob.astype(BF), grads, TN)
            dq = dotf(heads_beside(score_grad, size), heads_apart(key, 0.125))
            return kb, qb, at, score_grad, dk, dv, dq

        def add(kb, qb, at, score_grad, dk, dv, dq):
            for head in range(GHEADS):
                dist_acc[head, at] += score_grad[head * size : (head + 1) * size].astype(F32)
            dkv_acc[kb, :, :GW] += dk
            dkv_acc[kb, :, GW:] += dv
            dq_ref[qb] += dq

        def pair_step(step, carry):
            last = (step == groups).astype(jnp.int32)
            late = (step >= groups - 1).astype(jnp.int32)
            one = pair(3 * last, step - last)
            two = pair(1 + late, step + 1 - 2 * late)
            add(*one)
            add(*two)
            return carry

        lax.fori_loop(0, groups + 1, pair_step, 0)
        dkv_ref[slot] = dkv_acc[...].astype(dkv_ref.dtype)
        row = lax.broadcasted_iota(jnp.int32, (size, size), 0)
        lane = lax.broadcasted_iota(jnp.int32, (size, size), 1)
        flip = (row + lane == size - 1).astype(F32)
        for head in range(GHEADS):
            tiles = jnp.concatenate(
                [dist_acc[head, step] for step in range(groups + 1)], axis=1
            )
            tiles = jnp.dot(flip, tiles, precision=HIGHEST)
            for step in range(groups + 1):
                tile_rows = tiles[:, step * size : (step + 1) * size]
                wide = jnp.concatenate((tile_rows, jnp.zeros_like(tile_rows)), axis=1)
                wide = pltpu.roll(wide, 1, 1, stride=1, stride_axis=0)
                dist_ref[slot, head, step : step + 1, :] = jnp.sum(wide, axis=0, keepdims=True)
        return carry

    loop(slots, slot_step, 0)


def attention_backward(place, q, kv, start, bias, lse, full, out_grad, dtype, us):
    groups, size, _ = q.shape
    slots = kv.shape[0]
    tall = GHEADS * size
    return pl.pallas_call(
        backward_kernel,
        in_specs=[SM] + [VM] * 7,
        out_specs=[VM] * 3,
        out_shape=(
            jax.ShapeDtypeStruct((groups, size, GW), F32),
            jax.ShapeDtypeStruct((slots, groups, size, 2 * GW), dtype),
            jax.ShapeDtypeStruct((slots, GHEADS, groups + 1, 2 * size), F32),
        ),
        scratch_shapes=[
            pltpu.VMEM((GHEADS, groups + 1, size, size), F32),
            pltpu.VMEM((groups, tall, GW), BF),
            pltpu.VMEM((groups, tall, GW), BF),
            pltpu.VMEM((groups, tall, size), F32),
            pltpu.VMEM((groups, size, 2 * GW), F32),
        ],
        cost_estimate=cost(us),
        name="attention_backward",
    )(place, q, kv, start, bias, lse, full, out_grad)


def project_kernel(own_ref, h0_ref, h1_ref, h2_ref, h3_ref, w_ref, q_ref, kv_ref, h_ref):
    groups, size, _ = h_ref.shape
    for step, piece_ref in enumerate((h0_ref, h1_ref, h2_ref, h3_ref)):
        h_ref[behind(step, own_ref[0], groups)] = piece_ref[...]
    rows = dotf(h_ref[...].reshape(groups * size, D), w_ref[...]).astype(BF)
    q_ref[...] = rows[:, :GW].reshape(groups, size, GW)
    kv_ref[...] = rows[:, GW:].reshape(groups, size, 2 * GW)


def project(own, pieces, w_cols):
    size = pieces[0].shape[0]
    return pl.pallas_call(
        project_kernel,
        in_specs=[SM] + [VM] * 5,
        out_specs=[VM] * 3,
        out_shape=(
            jax.ShapeDtypeStruct((GROUPS, size, GW), BF),
            jax.ShapeDtypeStruct((GROUPS, size, 2 * GW), BF),
            jax.ShapeDtypeStruct((GROUPS, size, D), BF),
        ),
        cost_estimate=cost(0.05),
        name="project",
    )(own, *pieces, w_cols)


def mlp_in_kernel(
    att_ref, w_ref, x_ref, gain_ref, disp_ref, resid_ref, sent_ref
):
    total = x_ref[...]
    for group in range(GROUPS):
        total = total + dotf(att_ref[group], w_ref[group], TN)
    resid_ref[...] = total
    rate = lax.rsqrt(jnp.mean(total * total, axis=-1, keepdims=True) + EPS)
    low = (total * rate * gain_ref[...]).astype(BF)
    sent_ref[...] = dotf(disp_ref[...], low).astype(BF)


def mlp_in(att, w_attn, x, gain, disp):
    return pl.pallas_call(
        mlp_in_kernel,
        in_specs=[VM] * 5,
        out_specs=[VM] * 2,
        out_shape=(
            jax.ShapeDtypeStruct(x.shape, F32),
            jax.ShapeDtypeStruct((disp.shape[0], D), BF),
        ),
        cost_estimate=cost(0.05),
        name="mlp_in",
    )(att, w_attn, x, gain, disp)


def expert_kernel(
    own_ref,
    x_ref,
    came_ref,
    w_in_ref,
    w_out_ref,
    router_ref,
    active_ref,
    hidden_grad_ref,
    out_grad_ref,
    back_ref,
    out_ref,
    router_grad_ref,
    out_acc,
    back_acc,
    gate_ref,
):
    step = pl.program_id(0)
    rows = x_ref[...]
    lane = lax.broadcasted_iota(jnp.int32, (rows.shape[0], 128), 1)

    @pl.when(step == 0)
    def _():
        logits = dotf(rows, router_ref[...])
        pair = came_ref[:, D:].astype(F32)
        own = jnp.sum(jnp.where(lane == own_ref[0], logits, 0.0), axis=1, keepdims=True)
        other = jnp.where(lane == own_ref[0], 0.0, pair)
        other = jnp.sum(other * logits, axis=1, keepdims=True)
        peak = jnp.maximum(own, other)
        own_e, other_e = jnp.exp(own - peak), jnp.exp(other - peak)
        total = own_e + other_e
        own_gate = own_e / total
        gate_ref[0] = jnp.broadcast_to(own_gate, lane.shape)
        gate_ref[1] = jnp.broadcast_to(other_e / total, lane.shape)
        out_grad_ref[...] = (own_gate * came_ref[:, :D].astype(F32)).astype(BF)
        out_acc[...] = jnp.zeros_like(out_acc)
        back_acc[...] = jnp.zeros_like(back_acc)

    half = rows.shape[0] // 2

    def half_step(part, carry):
        at = pl.ds(pl.multiple_of(part * half, half), half)
        hidden = dotf(x_ref[at, :], w_in_ref[...])
        active_grad = dotf(out_grad_ref[at, :], w_out_ref[...], NT)
        value, slope = gelu_parts(hidden)
        active = value.astype(BF)
        hidden_grad = (slope * active_grad).astype(BF)
        active_ref[at, :] = active
        hidden_grad_ref[at, :] = hidden_grad
        out_acc[at, :] += dotf(active, w_out_ref[...])
        back_acc[at, :] += dotf(hidden_grad, w_in_ref[...], NT)
        return carry

    lax.fori_loop(0, 2, half_step, 0)

    @pl.when(step == pl.num_programs(0) - 1)
    def _():
        produced = out_acc[...].astype(BF).astype(F32)
        own_gate, other_gate = gate_ref[0][:, :1], gate_ref[1][:, :1]
        out_ref[...] = (own_gate * produced).astype(BF)
        gate_grad = jnp.sum(came_ref[:, :D].astype(F32) * produced, axis=1, keepdims=True)
        pull = own_gate * other_gate * gate_grad
        pair = came_ref[:, D:].astype(F32)
        logit_rows = pull * jnp.where(lane == own_ref[0], 1.0, -pair)
        high = logit_rows.astype(BF)
        rest = (logit_rows - high.astype(F32)).astype(BF)
        router = router_ref[...]
        back = back_acc[...].astype(BF).astype(F32)
        back = back + dotf(high, router, NT) + dotf(rest, router, NT)
        back_ref[...] = back.astype(BF)
        router_grad_ref[...] = dotf(rows, high, TN) + dotf(rows, rest, TN)


def expert_layer(own, x, came, w_in, w_out, router):
    count = x.shape[0]
    steps = 4
    part = FF // steps
    whole = lambda *shape: pl.BlockSpec(shape, lambda f, own: (0,) * len(shape))
    piece = pl.BlockSpec((count, part), lambda f, own: (0, own[1 + f]))
    return pl.pallas_call(
        expert_kernel,
        grid_spec=pltpu.PrefetchScalarGridSpec(
            num_scalar_prefetch=1,
            grid=(steps,),
            in_specs=[
                whole(count, D),
                whole(count, D + 128),
                pl.BlockSpec((D, part), lambda f, own: (0, f)),
                pl.BlockSpec((part, D), lambda f, own: (f, 0)),
                whole(D, 128),
            ],
            out_specs=[
                piece,
                piece,
                whole(count, D),
                whole(count, D),
                whole(count, D),
                whole(D, 128),
            ],
            scratch_shapes=[
                pltpu.VMEM((count, D), F32),
                pltpu.VMEM((count, D), F32),
                pltpu.VMEM((2, count, 128), F32),
            ],
        ),
        out_shape=(
            jax.ShapeDtypeStruct((count, FF), BF),
            jax.ShapeDtypeStruct((count, FF), BF),
            jax.ShapeDtypeStruct((count, D), BF),
            jax.ShapeDtypeStruct((count, D), BF),
            jax.ShapeDtypeStruct((count, D), BF),
            jax.ShapeDtypeStruct((D, 128), F32),
        ),
        cost_estimate=cost(0.05),
        name="expert_layer",
    )(own, x, came, w_in, w_out, router)


def mlp_back_kernel(
    back_ref, disp_ref, resid_ref, up_ref, gain_ref, w_ref, grad_ref, low_ref, gain_grad_ref, out_ref
):
    grad = dotf(disp_ref[...], back_ref[...], TN)
    resid = resid_ref[...]
    rate = lax.rsqrt(jnp.mean(resid * resid, axis=-1, keepdims=True) + EPS)
    unit = resid * rate
    gain_grad_ref[...] = jnp.sum(grad * unit, axis=0, keepdims=True)
    scaled = grad * gain_ref[...]
    total = up_ref[...] + rate * (
        scaled - unit * jnp.mean(scaled * unit, axis=-1, keepdims=True)
    )
    grad_ref[...] = total
    low = total.astype(BF)
    low_ref[...] = low
    for group in range(GROUPS):
        out_ref[group] = dotf(w_ref[group], low, NT).astype(BF)


def mlp_back(back, disp, resid, up, gain, w_attn):
    size = resid.shape[0]
    return pl.pallas_call(
        mlp_back_kernel,
        in_specs=[VM] * 6,
        out_specs=[VM] * 4,
        out_shape=(
            jax.ShapeDtypeStruct((size, D), F32),
            jax.ShapeDtypeStruct((size, D), BF),
            jax.ShapeDtypeStruct((1, D), F32),
            jax.ShapeDtypeStruct((GROUPS, GW, size), BF),
        ),
        cost_estimate=cost(4),
        name="mlp_back",
    )(back, disp, resid, up, gain, w_attn)


def project_back_kernel(
    dq_ref,
    dq_other_ref,
    dkv_ref,
    came_ref,
    w_ref,
    h_ref,
    gain_ref,
    dproj_ref,
    gain_grad_ref,
    half_ref,
):
    groups, size, _ = dq_ref.shape
    dq = (dq_ref[...] + dq_other_ref[...]).astype(BF).reshape(groups * size, GW)
    dkv = (dkv_ref[...] + came_ref[...].astype(F32)).astype(BF)
    dkv = dkv.reshape(groups * size, 2 * GW)
    dproj_ref[...] = jnp.concatenate((dq, dkv), axis=1)
    total = jnp.zeros((1, D), F32)
    for block in range(groups):
        half = dotf(dproj_ref[block * size : (block + 1) * size], w_ref[...], NT)
        half_ref[block] = half.astype(BF)
        total = total + jnp.sum(half * h_ref[block].astype(F32), axis=0, keepdims=True)
    gain_grad_ref[...] = total / gain_ref[...]


def project_back(dq, dq_other, dkv, came, w_cols, h_col, gain):
    groups, size, _ = dq.shape
    return pl.pallas_call(
        project_back_kernel,
        in_specs=[VM] * 7,
        out_specs=[VM] * 3,
        out_shape=(
            jax.ShapeDtypeStruct((groups * size, 3 * GW), BF),
            jax.ShapeDtypeStruct((1, D), F32),
            jax.ShapeDtypeStruct((groups, size, D), BF),
        ),
        cost_estimate=cost(4),
        name="project_back",
    )(dq, dq_other, dkv, came, w_cols, h_col, gain)


def qkv_grad_kernel(h_ref, dproj_ref, grad_ref):
    ranks, rows, _ = grad_ref.shape
    groups, size, _ = h_ref.shape
    total = dotf(h_ref[...].reshape(groups * size, D), dproj_ref[...], TN)
    for rank in range(ranks):
        grad_ref[rank] = total[rank * rows : (rank + 1) * rows]


def qkv_grad_of(h_col, dproj, ranks):
    return pl.pallas_call(
        qkv_grad_kernel,
        in_specs=[VM] * 2,
        out_specs=VM,
        out_shape=jax.ShapeDtypeStruct((ranks, D // ranks, 3 * GW), F32),
        cost_estimate=cost(0.05),
        name="qkv_grad",
    )(h_col, dproj)


def side_grad_kernel(att_ref, grad_ref, router_ref, out_ref):
    ranks, rows, _ = out_ref.shape
    inner = ranks // GROUPS
    for block in range(GROUPS):
        total = dotf(att_ref[block], grad_ref[...])
        for part in range(inner):
            out_ref[block * inner + part, :, :D] = total[part * rows : (part + 1) * rows]
    for rank in range(ranks):
        out_ref[rank, :, D:] = router_ref[rank * rows : (rank + 1) * rows]


def side_grad_of(att, grad, router_grad, ranks):
    return pl.pallas_call(
        side_grad_kernel,
        in_specs=[VM] * 3,
        out_specs=VM,
        out_shape=jax.ShapeDtypeStruct((ranks, D // ranks, D + 128), F32),
        cost_estimate=cost(0.05),
        name="side_grad",
    )(att, grad, router_grad)


def assemble_kernel(own_ref, p0_ref, p1_ref, p2_ref, p3_ref, rows_ref, scratch):
    side = D + 128
    wide = side + 3 * GW
    last = side + 3 * D
    width = (p0_ref.shape[1] - wide) // 2
    pieces = [ref[...].astype(F32) for ref in (p0_ref, p1_ref, p2_ref, p3_ref)]
    total = pieces[0] + pieces[1] + pieces[2] + pieces[3]
    rows_ref[:, :side] = total[:, :side].astype(BF)
    small = total[:, wide : wide + width] + total[:, wide + width :]
    high = small.astype(BF)
    rows_ref[:, last : last + width] = high
    rows_ref[:, last + width :] = (small - high.astype(F32)).astype(BF)
    for step, piece in enumerate(pieces):
        scratch[behind(step, own_ref[0], GROUPS)] = piece[:, side:wide]
    for group in range(GROUPS):
        for kind in range(3):
            at = side + (kind * GROUPS + group) * GW
            rows_ref[:, at : at + GW] = scratch[group, :, kind * GW : (kind + 1) * GW].astype(BF)


def assemble(own, parts):
    rows, width = parts[0].shape
    return pl.pallas_call(
        assemble_kernel,
        in_specs=[SM] + [VM] * 4,
        out_specs=VM,
        out_shape=jax.ShapeDtypeStruct((rows, width + 3 * D - 3 * GW), BF),
        scratch_shapes=[pltpu.VMEM((GROUPS, rows, 3 * GW), F32)],
        cost_estimate=cost(0.05),
        name="assemble",
    )(own, *parts)


def unpack_kernel(own_ref, pair_ref, came_ref, attn_ref, router_ref, qkv_ref, small_ref):
    experts = router_ref.shape[2]
    last = 4 * D + 128
    width = small_ref.shape[1]
    small = jnp.zeros(small_ref.shape, F32)
    for near, ref in ((own_ref[0], pair_ref), (1 - own_ref[0], came_ref)):
        for part in range(2):
            value = ref[part].astype(F32)
            attn_ref[near * 2 + part] = value[:, :D]
            router_ref[near * 2 + part] = value[:, D : D + experts]
            qkv_ref[near * 2 + part] = value[:, D + 128 : last]
            small = small + (value[:, last : last + width] + value[:, last + width :])
    small_ref[...] = small


def unpack(own, pair, came, experts):
    rows = pair.shape[1]
    width = (pair.shape[2] - 4 * D - 128) // 2
    outs = pl.pallas_call(
        unpack_kernel,
        in_specs=[SM] + [VM] * 2,
        out_specs=[VM] * 4,
        out_shape=[jax.ShapeDtypeStruct((4, rows, n), F32) for n in (D, experts, 3 * D)]
        + [jax.ShapeDtypeStruct((rows, width), F32)],
        cost_estimate=cost(0.05),
        name="unpack",
    )(own.astype(jnp.int32), pair, came)
    return [out.reshape(4 * rows, -1) for out in outs[:3]] + [outs[3]]


def gelu_parts(hidden):
    scale = math.sqrt(2.0 / math.pi)
    square = hidden * hidden
    bend = jnp.tanh(hidden * (scale + (scale * 0.044715) * square))
    half = 0.5 + 0.5 * bend
    slope = scale + (3 * scale * 0.044715) * square
    return hidden * half, half + (0.5 * hidden) * (1.0 - bend * bend) * slope


def swap(value, axis):
    return lax.ppermute(value, axis, [(0, 1), (1, 0)])


def tie(*values):
    return lax.optimization_barrier(values)


def turn(value, step):
    return lax.ppermute(value, "g", [(j, (j + step) % GROUPS) for j in range(GROUPS)])


def in_turn(pieces, g):
    pieces = jnp.stack(pieces[::-1] * 2)
    return lax.dynamic_slice_in_dim(pieces, GROUPS - 1 - g, GROUPS, 0)


def exchange(value, axes):
    return lax.all_to_all(value, axes, split_axis=0, concat_axis=0, tiled=True)


def in_order(own, came, index):
    return jnp.where(index == 0, jnp.stack((own, came)), jnp.stack((came, own)))


def rep_gather(value, y, c):
    pair = in_order(value, swap(value, "y"), y)
    return in_order(pair, swap(pair, "c"), c)


def halve(value, index, axis):
    count, rows, cols = value.shape
    value = value.reshape(count, 2, rows // 2, cols)
    away = swap(pick(value, 1 - index, 1).astype(BF), axis)
    return pick(value, index, 1) + away.astype(F32)


def pick(value, index, axis):
    return lax.dynamic_index_in_dim(value, index, axis, keepdims=False)


def norm_backward(grad, gain, value):
    rate = lax.rsqrt(jnp.mean(value * value, axis=-1, keepdims=True) + EPS)
    unit = value * rate
    scaled = grad * gain
    return rate * (scaled - unit * jnp.mean(scaled * unit, axis=-1, keepdims=True))


def local(
    tokens,
    cotangent,
    gain_attn,
    gain_mlp,
    w_qkv,
    w_attn_out,
    router,
    rel_table,
    w_in,
    w_out,
    segment_ids,
    expert_ids,
    rel_bucket,
):
    groups, inner = lax.axis_size("g"), lax.axis_size("i")
    g, i = lax.axis_index("g"), lax.axis_index("i")
    y, c = lax.axis_index("y"), lax.axis_index("c")
    ranks = groups * inner
    copies = 4
    size = tokens.shape[1]
    experts = ranks
    capacity = max(2, 4 * size // experts)
    inputs = tokens[0]
    upstream = cotangent[0]
    seg_all = segment_ids[0]
    chosen_ids = expert_ids[0]
    rows = w_qkv.shape[0] // copies
    me = g * inner + i
    own_g = g[None].astype(jnp.int32)

    rate = lax.rsqrt(jnp.mean(inputs * inputs, axis=-1, keepdims=True) + EPS)
    h_attn = (inputs * rate * gain_attn).astype(BF)
    h_pieces = [h_attn] + [turn(h_attn, step) for step in range(1, groups)]

    part = lax.dynamic_slice_in_dim(w_qkv, c * 2 * rows, 2 * rows, 0).astype(BF)
    part = part.reshape(2 * rows, 3, groups, GW).transpose(2, 0, 1, 3)
    part = jnp.broadcast_to(part[:, None], (groups, inner, 2 * rows, 3, GW))
    part = exchange(part.reshape(ranks, 2 * rows, 3 * GW), SEQ)
    both = jnp.concatenate((w_attn_out, jnp.pad(router, ((0, 0), (0, 128 - experts)))), axis=1)
    both = lax.dynamic_slice_in_dim(both, (c * 2 + y) * rows, rows, 0).astype(BF)
    both = jnp.broadcast_to(both[None], (ranks, rows, D + 128))
    w_cols = in_order(part, swap(part, "c"), c).swapaxes(0, 1).reshape(D, 3 * GW)

    expert_iota = jnp.arange(experts, dtype=jnp.int32)
    token_iota = jnp.arange(size, dtype=jnp.int32)
    pair_hot = jnp.any(chosen_ids[:, :, None] == expert_iota[None, None, :], axis=1)
    rank = jnp.dot(
        (token_iota[:, None] > token_iota[None, :]).astype(BF),
        pair_hot.astype(BF),
        preferred_element_type=F32,
    ).astype(jnp.int32)
    disp = (rank.T[:, None, :] == jnp.arange(capacity, dtype=jnp.int32)[None, :, None]) & (
        pair_hot.T[:, None, :]
    )
    disp = disp.astype(BF).reshape(experts * capacity, size)
    early = jnp.concatenate(
        (upstream.astype(BF), jnp.pad(pair_hot.astype(BF), ((0, 0), (0, 128 - experts)))), axis=1
    )
    early = jnp.dot(disp, early, preferred_element_type=F32).astype(BF)
    seg_col = pick(seg_all.reshape(groups, inner, size), i, 1)
    start = jnp.sum(
        (seg_all[None, None, :] < seg_col[:, :, None]).astype(jnp.int32), axis=-1, keepdims=True
    )
    padded = jnp.concatenate(
        (jnp.full((size - 1,), -1, jnp.int32), rel_bucket, jnp.full((1,), -1, jnp.int32))
    )
    reversed_bucket = padded.reshape(ranks + 1, size)[:, ::-1].reshape(-1)
    bucket_hot = (
        jnp.arange(BUCKETS, dtype=jnp.int32)[:, None] == reversed_bucket[None, :]
    ).astype(F32)
    table = lax.dynamic_slice_in_dim(rel_table, g * GHEADS, GHEADS, 0)
    bias_rows = jnp.dot(table, bucket_hot, precision=HIGHEST).reshape(GHEADS, ranks + 1, size)
    bias = bias_tiles(bias_rows, inner)
    bias, start, *h_pieces = tie(bias, start, *h_pieces)

    early = jnp.concatenate((early.reshape(ranks, capacity, D + 128), both), axis=1)
    early, *h_pieces = tie(early, *h_pieces)
    q, kv, h_col = project(own_g, h_pieces, w_cols)
    came_rows = exchange(early, SEQ)
    head_place = jnp.stack((i, jnp.int32(inner)))

    def place_of(columns):
        return jnp.concatenate((head_place, columns, own_g)).astype(jnp.int32)

    if inner == 2:
        kv_came = swap(kv, "i")
        kv_all = (kv, kv_came)
        columns = jnp.stack((i, 1 - i))
    else:
        kv_all = (lax.all_gather(kv, "i"),)
        columns = jnp.arange(inner, dtype=jnp.int32)
    place = place_of(columns)
    mixed, mixed_full, lse = attention_forward(place, q, kv_all, start, bias)
    mixed, came_rows = tie(mixed, came_rows)
    both = came_rows[:, capacity:]
    both = in_order(both, swap(both, "y"), y)
    came_rows = came_rows[:, :capacity].reshape(ranks * capacity, D + 128)
    att = exchange(mixed, "g")
    att, both = tie(att, both)
    both = in_order(both, swap(both, "c"), c)
    both = both.transpose(2, 0, 1, 3, 4).reshape(D, D + 128)
    w_attn_low = both[:, :D].reshape(groups, GW, D)
    router_low = both[:, D:]
    residual, outgoing = mlp_in(att, w_attn_low, inputs, gain_mlp[None], disp)

    arrived = exchange(outgoing.reshape(ranks, capacity, D), SEQ).reshape(ranks * capacity, D)
    active, hidden_grad, produced_grad, back, produced, router_grad = expert_layer(
        jnp.stack([me] + [2 * (c == f % 2) + (y == f // 2) for f in range(4)]).astype(jnp.int32),
        arrived,
        came_rows, w_in[0], w_out[0], router_low
    )
    back_rows = exchange(back.reshape(ranks, capacity, D), SEQ).reshape(ranks * capacity, D)

    part_ff = FF // 4
    slices = [slice(f * part_ff, (f + 1) * part_ff) for f in range(4)]

    def part_grads(f, active=active, hidden_grad=hidden_grad):
        return (
            dotf(active[:, slices[f]], produced_grad, TN),
            dotf(arrived, hidden_grad[:, slices[f]], TN),
        )

    core_far = [swap(grad.astype(BF), "c") for grad in part_grads(0)]
    near = [grad.astype(BF) for grad in part_grads(1)]
    away = [
        (grad + core.astype(F32)).astype(BF) for grad, core in zip(part_grads(2), core_far)
    ]
    far_out = swap(away[0], "y")
    back_rows, *near = tie(back_rows, *near)

    resid_grad, attn_grad, gain_two, out_grad = mlp_back(
        back_rows, disp, residual, upstream, gain_mlp[None], w_attn_low
    )
    out_grad = exchange(out_grad, "g")
    side_grad = side_grad_of(att, attn_grad, router_grad, ranks)
    out_grad, produced, side_grad, away_in = tie(out_grad, produced, side_grad, away[1])
    far_in = swap(away_in, "y")
    side_grad = halve(side_grad, c, "c")
    near = [swap(grad, "c") for grad in near]
    returned = exchange(produced.reshape(ranks, capacity, D), SEQ)

    def inner_reduce(value):
        value = value.reshape(groups, inner, *value.shape[1:])
        if inner > 2:
            return lax.psum_scatter(value, "i", scatter_dimension=1).astype(BF)
        own = pick(value, i, 1) + swap(pick(value, 1 - i, 1).astype(BF), "i").astype(F32)
        return own.astype(BF)

    if inner == 2:
        dq_other, dkv_other, dist_other = attention_backward(
            place_of(1 - i[None]),
            q,
            kv_came[None],
            start,
            bias,
            lse,
            mixed_full,
            out_grad,
            BF,
            8,
        )
        out_grad, dq_other, dkv_other, far_out, side_grad = tie(
            out_grad, dq_other, dkv_other, far_out, side_grad
        )
        dkv_came = swap(dkv_other[0], "i")
        dq, dkv_own, dist = attention_backward(
            place_of(i[None]),
            q,
            kv[None],
            start,
            bias,
            lse,
            mixed_full,
            out_grad,
            F32,
            1,
        )
        dkv_own = dkv_own[0]
        dist = jnp.concatenate((dist, dist_other))
    else:
        dq, dkv_all, dist = attention_backward(
            place, q, kv_all[0], start, bias, lse, mixed_full, out_grad, F32, 1
        )
        dkv_own = lax.psum_scatter(dkv_all, "i")
        dkv_came = jnp.zeros(dkv_own.shape, BF)
        dq_other = jnp.zeros_like(dq)
        dist = jnp.take(dist, (i - jnp.arange(inner)) % inner, axis=0)
    dkv_own, returned, far_in, side_grad = tie(dkv_own, returned, far_in, side_grad)
    side_grad = halve(side_grad, y, "y")
    returned = returned.reshape(ranks * capacity, D)
    dproj, gain_one, half = project_back(
        dq, dq_other, dkv_own, dkv_came, w_cols, h_col, gain_attn[None]
    )
    half = exchange(half, "g")
    parts = halve(qkv_grad_of(h_col, dproj, ranks), c, "c")
    parts, gain_one, gain_two, dist = tie(parts, gain_one, gain_two, dist)
    parts = jnp.concatenate((side_grad, halve(parts, y, "y")), axis=2)
    parts, active, hidden_grad, *near = tie(parts, active, hidden_grad, *near)
    mine_out, mine_in = [
        grad + core.astype(F32) for grad, core in zip(part_grads(3, active, hidden_grad), near)
    ]
    dist = dist[:, :, 1:].transpose(1, 2, 0, 3).reshape(GHEADS, ranks, 2 * size)
    dist_rows = jnp.pad(dist[:, :, size:], ((0, 0), (0, 1), (0, 0))) + jnp.pad(
        dist[:, :, :size], ((0, 0), (1, 0), (0, 0))
    )
    table_grad = jnp.dot(dist_rows.reshape(GHEADS, -1), bucket_hot.T, precision=HIGHEST)
    table_all = lax.dynamic_update_slice(
        jnp.zeros((HEADS, BUCKETS), F32), table_grad, (g * GHEADS, 0)
    )
    small = jnp.concatenate((gain_one[0], gain_two[0], table_all.reshape(-1)))
    count = small.shape[0]
    width = -(-count // (rows * 128)) * 128
    small = jnp.pad(small.reshape(-1, 128), ((0, (rows * width - count) // 128), (0, 0)))
    small = small.reshape(rows, width)
    small = small + (swap(small, "i") if inner == 2 else lax.psum(small, "i") - small)
    high = lax.reduce_precision(small, 8, 7)
    small = jnp.concatenate((high, small - high), axis=1).astype(BF)
    small = jnp.broadcast_to(small[None], (groups, rows, 2 * width))

    parts, half = tie(jnp.concatenate((inner_reduce(parts), small), axis=2), half)
    parts = [pick(parts, g, 0)] + [
        turn(pick(parts, lax.rem(g + step, groups), 0), step) for step in range(1, groups)
    ]
    norm_in_grad = jnp.sum(half.astype(F32), axis=0)
    input_grad = resid_grad + norm_backward(norm_in_grad, gain_attn, inputs)
    result = residual + dotf(disp, returned, TN)
    shards = assemble(own_g, parts)
    pair = in_order(shards, swap(shards, "y"), y)
    attn_shard, router_shard, qkv_shard, small = unpack(c[None], pair, swap(pair, "c"), experts)
    small = small.reshape(-1)
    w_in_shard = mine_in + far_in.astype(F32)
    w_out_shard = mine_out + far_out.astype(F32)
    return (
        result[None],
        input_grad[None],
        small[:D],
        small[D : 2 * D],
        qkv_shard,
        attn_shard,
        router_shard,
        small[2 * D : 2 * D + HEADS * BUCKETS].reshape(HEADS, BUCKETS),
        w_in_shard[None],
        w_out_shard[None],
    )


def solution(mesh):
    ranks = mesh.shape["seq"]
    split = Mesh(
        mesh.devices.reshape(2, mesh.shape["rep"] // 2, GROUPS, ranks // GROUPS),
        ("y", "c", "g", "i"),
    )
    placed = (
        P(REP, SEQ, None),
        P(REP, SEQ, None),
        P(),
        P(),
        P(SEQ, None),
        P(SEQ, None),
        P(SEQ, None),
        P(),
        P(SEQ, None, None),
        P(SEQ, None, None),
        P(REP, None),
        P(REP, SEQ, None),
        P(),
    )
    return jax.shard_map(
        local,
        mesh=split,
        in_specs=placed,
        out_specs=(
            P(REP, SEQ, None),
            P(REP, SEQ, None),
            P(),
            P(),
            P(SEQ, None),
            P(SEQ, None),
            P(SEQ, None),
            P(),
            P(SEQ, None, REP),
            P(SEQ, REP, None),
        ),
        check_vma=False,
    )
```

```python
from functools import partial
import math

import jax
import jax.numpy as jnp
from jax import lax
from jax.experimental import pallas as pl
from jax.experimental.pallas import tpu as pltpu
from jax.sharding import Mesh, PartitionSpec as P

D = 768
HEADS = 12
HEAD = 64
BUCKETS = 32
FF = 3072
GROUPS = 4
GHEADS = HEADS // GROUPS
GW = GHEADS * HEAD
EPS = 1e-06
HIGHEST = lax.Precision.HIGHEST
BF = jnp.bfloat16
F32 = jnp.float32
NT = (((1,), (1,)), ((), ()))
TN = (((0,), (0,)), ((), ()))
SEQ = ("g", "i")
REP = ("y", "c")


def dotf(a, b, dims=(((1,), (0,)), ((), ()))):
    return lax.dot_general(a, b, dims, preferred_element_type=F32)


def loop(count, body, init):
    if count <= 2:
        for step in range(count):
            init = body(step, init)
        return init
    return lax.fori_loop(0, count, body, init)


def ahead(block, own, count):
    return lax.rem(block + count - own, count)


def behind(step, own, count):
    return lax.rem(own + count - step, count)


def heads_apart(value, scale):
    lane = lax.broadcasted_iota(jnp.int32, value.shape, 1)
    value = value * jnp.asarray(scale, value.dtype)
    return jnp.concatenate(
        [jnp.where(lane // HEAD == head, value, jnp.zeros_like(value)) for head in range(GHEADS)],
        axis=0,
    )


def heads_beside(value, size):
    return jnp.concatenate(
        [value[head * size : (head + 1) * size] for head in range(GHEADS)], axis=1
    )


def turned(value):
    wide = jnp.concatenate((value, jnp.zeros((value.shape[0], -GW % 128), F32)), axis=1)
    return wide.T[:GW]


def turned_back(value):
    tall = jnp.concatenate((value, jnp.zeros((-GW % 128, value.shape[1]), F32)), axis=0)
    return tall.T[:, :GW]


def tile_mask(start, query_block, key_block, size):
    lane = lax.broadcasted_iota(jnp.int32, (size, size), 1)
    row = lax.broadcasted_iota(jnp.int32, (size, size), 0)
    allowed = (lane >= start - key_block * size) & (
        lane - row <= (query_block - key_block) * size
    )
    return jnp.where(allowed, 0.0, -1e30)


def bias_kernel(rows_ref, tiles_ref):
    heads, inner, count, size, _ = tiles_ref.shape

    def head_step(head, carry):
        for part in range(inner):
            tiles_ref[head, part, 0] = jnp.zeros((size, size), F32)
            for step in range(count - 1):
                gap = step * inner + part
                pair = jnp.concatenate(
                    (rows_ref[head, gap : gap + 1, :], rows_ref[head, gap + 1 : gap + 2, :]),
                    axis=1,
                )
                spread = jnp.broadcast_to(pair, (size, 2 * size))
                spread = pltpu.roll(spread, 0, 1, stride=1, stride_axis=0)
                tiles_ref[head, part, step + 1] = spread[:, :size]
        return carry

    lax.fori_loop(0, heads, head_step, 0)


def cost(us):
    return pl.CostEstimate(flops=0, bytes_accessed=int(us * 3.4e6), transcendentals=0)


def bias_tiles(rows, inner):
    heads, count, size = rows.shape
    return pl.pallas_call(
        bias_kernel,
        out_shape=jax.ShapeDtypeStruct((heads, inner, (count - 1) // inner + 1, size, size), F32),
        cost_estimate=cost(0.05),
        name="bias_tiles",
    )(rows)


def block_of(kv_refs, slot, kb):
    if len(kv_refs) == 1:
        return kv_refs[0][slot, kb]
    return kv_refs[slot][kb]


def bias_place(place_ref, slot):
    shift = place_ref[0] - place_ref[2 + slot]
    below = (shift < 0).astype(jnp.int32)
    return shift + below * place_ref[1], 1 - below


def forward_kernel(
    place_ref,
    q_ref,
    *refs,
):
    groups, size, _ = q_ref.shape
    kv_refs, (start_ref, bias_ref, out_ref, full_ref, lse_ref, s_ref, vs_ref) = refs[:-7], refs[-7:]
    slots = s_ref.shape[0]
    tall = GHEADS * size

    def spread_step(slot, carry):
        for kb in range(groups):
            vs_ref[slot, kb] = heads_apart(block_of(kv_refs, slot, kb)[:, GW:], 1)
        return carry

    loop(slots, spread_step, 0)
    for qb in range(groups):
        queries = heads_apart(q_ref[qb], 0.125)
        start = start_ref[qb]
        query_block = qb * place_ref[1] + place_ref[0]

        def score_step(slot, top):
            part, tile = bias_place(place_ref, slot)
            for kb in range(qb + 1):
                key_block = kb * place_ref[1] + place_ref[2 + slot]
                mask = tile_mask(start, query_block, key_block, size)
                raw = dotf(queries, block_of(kv_refs, slot, kb)[:, :GW], NT)
                bias = [bias_ref[head, part, tile + qb - kb] + mask for head in range(GHEADS)]
                score = raw + jnp.concatenate(bias, axis=0)
                s_ref[slot, kb] = score
                top = jnp.maximum(top, score)
            return top

        top = loop(slots, score_step, jnp.full((tall, size), -1e30, F32))
        top = jnp.broadcast_to(jnp.max(top, axis=1, keepdims=True), (tall, size))

        def exp_step(slot, total):
            for kb in range(qb + 1):
                value = jnp.exp(s_ref[slot, kb] - top)
                s_ref[slot, kb] = value
                total = total + value
            return total

        total = loop(slots, exp_step, jnp.zeros((tall, size), F32))
        total = jnp.broadcast_to(jnp.sum(total, axis=1, keepdims=True), (tall, size))
        scale = 1.0 / total
        lse_ref[qb] = top + jnp.log(total)

        def out_step(slot, sums):
            low_sum, rest_sum = sums
            for kb in range(qb + 1):
                prob = s_ref[slot, kb] * scale
                prob_low = prob.astype(BF)
                rest = (prob - prob_low.astype(F32)).astype(BF)
                values = vs_ref[slot, kb]
                low_sum = low_sum + dotf(heads_beside(prob_low, size), values)
                rest_sum = rest_sum + dotf(heads_beside(rest, size), values)
            return (low_sum, rest_sum)

        zero = jnp.zeros((size, GW), F32)
        low_sum, rest_sum = loop(slots, out_step, (zero, zero))
        full_ref[qb] = low_sum + rest_sum
        out_ref[qb] = turned(low_sum).astype(BF)


VM = pl.BlockSpec(memory_space=pltpu.VMEM)
SM = pl.BlockSpec(memory_space=pltpu.SMEM)


def attention_forward(place, q, kv, start, bias):
    groups, size, _ = q.shape
    slots = kv[0].shape[0] if len(kv) == 1 else len(kv)
    return pl.pallas_call(
        forward_kernel,
        in_specs=[SM] + [VM] * (3 + len(kv)),
        out_specs=[VM] * 3,
        out_shape=(
            jax.ShapeDtypeStruct((groups, GW, size), BF),
            jax.ShapeDtypeStruct((groups, size, GW), F32),
            jax.ShapeDtypeStruct((groups, GHEADS * size, size), F32),
        ),
        scratch_shapes=[
            pltpu.VMEM((slots, groups, GHEADS * size, size), F32),
            pltpu.VMEM((slots, groups, GHEADS * size, GW), BF),
        ],
        cost_estimate=cost(7),
        name="attention_forward",
    )(place, q, *kv, start, bias)


def backward_kernel(
    place_ref,
    q_ref,
    kv_ref,
    start_ref,
    bias_ref,
    lse_ref,
    full_ref,
    out_grad_ref,
    dq_ref,
    dkv_ref,
    dist_ref,
    dist_acc,
    qs_ref,
    gs_ref,
    delta_ref,
    dkv_acc,
):
    groups, size, _ = q_ref.shape
    slots = kv_ref.shape[0]
    tall = GHEADS * size
    for block in range(groups):
        spread = heads_apart(turned_back(out_grad_ref[block].astype(F32)).astype(BF), 1)
        gs_ref[block] = spread
        full = full_ref[block]
        product = spread.astype(F32) * jnp.concatenate([full] * GHEADS, axis=0)
        delta = jnp.sum(product, axis=1, keepdims=True)
        delta_ref[block] = jnp.broadcast_to(delta, (tall, size))
    for qb in range(groups):
        qs_ref[qb] = heads_apart(q_ref[qb], 0.125)
    dq_ref[...] = jnp.zeros_like(dq_ref)

    def slot_step(slot, carry):
        dist_acc[...] = jnp.zeros_like(dist_acc)
        part, tile = bias_place(place_ref, slot)
        dkv_acc[...] = jnp.zeros_like(dkv_acc)

        def pair(kb, qb):
            key_block = kb * place_ref[1] + place_ref[2 + slot]
            query_block = qb * place_ref[1] + place_ref[0]
            key, value = kv_ref[slot, kb, :, :GW], kv_ref[slot, kb, :, GW:]
            mask = tile_mask(start_ref[qb], query_block, key_block, size)
            at = tile + qb - kb
            bias = [bias_ref[head, part, at] + mask for head in range(GHEADS)]
            queries, grads = qs_ref[qb], gs_ref[qb]
            raw = dotf(queries, key, NT)
            prob_grad = dotf(grads, value, NT)
            prob = jnp.exp(raw + (jnp.concatenate(bias, axis=0) - lse_ref[qb]))
            score_grad = (prob * (prob_grad - delta_ref[qb])).astype(BF)
            dk = dotf(score_grad, queries, TN)
            dv = dotf(prob.astype(BF), grads, TN)
            dq = dotf(heads_beside(score_grad, size), heads_apart(key, 0.125))
            return kb, qb, at, score_grad, dk, dv, dq

        def add(kb, qb, at, score_grad, dk, dv, dq):
            for head in range(GHEADS):
                dist_acc[head, at] += score_grad[head * size : (head + 1) * size].astype(F32)
            dkv_acc[kb, :, :GW] += dk
            dkv_acc[kb, :, GW:] += dv
            dq_ref[qb] += dq

        def pair_step(step, carry):
            last = (step == groups).astype(jnp.int32)
            late = (step >= groups - 1).astype(jnp.int32)
            one = pair(3 * last, step - last)
            two = pair(1 + late, step + 1 - 2 * late)
            add(*one)
            add(*two)
            return carry

        lax.fori_loop(0, groups + 1, pair_step, 0)
        dkv_ref[slot] = dkv_acc[...].astype(dkv_ref.dtype)
        row = lax.broadcasted_iota(jnp.int32, (size, size), 0)
        lane = lax.broadcasted_iota(jnp.int32, (size, size), 1)
        flip = (row + lane == size - 1).astype(F32)
        for head in range(GHEADS):
            tiles = jnp.concatenate(
                [dist_acc[head, step] for step in range(groups + 1)], axis=1
            )
            tiles = jnp.dot(flip, tiles, precision=HIGHEST)
            for step in range(groups + 1):
                tile_rows = tiles[:, step * size : (step + 1) * size]
                wide = jnp.concatenate((tile_rows, jnp.zeros_like(tile_rows)), axis=1)
                wide = pltpu.roll(wide, 1, 1, stride=1, stride_axis=0)
                dist_ref[slot, head, step : step + 1, :] = jnp.sum(wide, axis=0, keepdims=True)
        return carry

    loop(slots, slot_step, 0)


def attention_backward(place, q, kv, start, bias, lse, full, out_grad, dtype, us):
    groups, size, _ = q.shape
    slots = kv.shape[0]
    tall = GHEADS * size
    return pl.pallas_call(
        backward_kernel,
        in_specs=[SM] + [VM] * 7,
        out_specs=[VM] * 3,
        out_shape=(
            jax.ShapeDtypeStruct((groups, size, GW), F32),
            jax.ShapeDtypeStruct((slots, groups, size, 2 * GW), dtype),
            jax.ShapeDtypeStruct((slots, GHEADS, groups + 1, 2 * size), F32),
        ),
        scratch_shapes=[
            pltpu.VMEM((GHEADS, groups + 1, size, size), F32),
            pltpu.VMEM((groups, tall, GW), BF),
            pltpu.VMEM((groups, tall, GW), BF),
            pltpu.VMEM((groups, tall, size), F32),
            pltpu.VMEM((groups, size, 2 * GW), F32),
        ],
        cost_estimate=cost(us),
        name="attention_backward",
    )(place, q, kv, start, bias, lse, full, out_grad)


def project_kernel(own_ref, h0_ref, h1_ref, h2_ref, h3_ref, w_ref, q_ref, kv_ref, h_ref):
    groups, size, _ = h_ref.shape
    for step, piece_ref in enumerate((h0_ref, h1_ref, h2_ref, h3_ref)):
        h_ref[behind(step, own_ref[0], groups)] = piece_ref[...]
    rows = dotf(h_ref[...].reshape(groups * size, D), w_ref[...]).astype(BF)
    q_ref[...] = rows[:, :GW].reshape(groups, size, GW)
    kv_ref[...] = rows[:, GW:].reshape(groups, size, 2 * GW)


def project(own, pieces, w_cols):
    size = pieces[0].shape[0]
    return pl.pallas_call(
        project_kernel,
        in_specs=[SM] + [VM] * 5,
        out_specs=[VM] * 3,
        out_shape=(
            jax.ShapeDtypeStruct((GROUPS, size, GW), BF),
            jax.ShapeDtypeStruct((GROUPS, size, 2 * GW), BF),
            jax.ShapeDtypeStruct((GROUPS, size, D), BF),
        ),
        cost_estimate=cost(0.05),
        name="project",
    )(own, *pieces, w_cols)


def mlp_in_kernel(
    att_ref, w_ref, x_ref, gain_ref, disp_ref, resid_ref, sent_ref
):
    total = x_ref[...]
    for group in range(GROUPS):
        total = total + dotf(att_ref[group], w_ref[group], TN)
    resid_ref[...] = total
    rate = lax.rsqrt(jnp.mean(total * total, axis=-1, keepdims=True) + EPS)
    low = (total * rate * gain_ref[...]).astype(BF)
    sent_ref[...] = dotf(disp_ref[...], low).astype(BF)


def mlp_in(att, w_attn, x, gain, disp):
    return pl.pallas_call(
        mlp_in_kernel,
        in_specs=[VM] * 5,
        out_specs=[VM] * 2,
        out_shape=(
            jax.ShapeDtypeStruct(x.shape, F32),
            jax.ShapeDtypeStruct((disp.shape[0], D), BF),
        ),
        cost_estimate=cost(0.05),
        name="mlp_in",
    )(att, w_attn, x, gain, disp)


def expert_kernel(
    own_ref,
    x_ref,
    came_ref,
    w_in_ref,
    w_out_ref,
    router_ref,
    active_ref,
    hidden_grad_ref,
    out_grad_ref,
    back_ref,
    out_ref,
    router_grad_ref,
    out_acc,
    back_acc,
    gate_ref,
):
    step = pl.program_id(0)
    rows = x_ref[...]
    lane = lax.broadcasted_iota(jnp.int32, (rows.shape[0], 128), 1)

    @pl.when(step == 0)
    def _():
        logits = dotf(rows, router_ref[...])
        pair = came_ref[:, D:].astype(F32)
        own = jnp.sum(jnp.where(lane == own_ref[0], logits, 0.0), axis=1, keepdims=True)
        other = jnp.where(lane == own_ref[0], 0.0, pair)
        other = jnp.sum(other * logits, axis=1, keepdims=True)
        peak = jnp.maximum(own, other)
        own_e, other_e = jnp.exp(own - peak), jnp.exp(other - peak)
        total = own_e + other_e
        own_gate = own_e / total
        gate_ref[0] = jnp.broadcast_to(own_gate, lane.shape)
        gate_ref[1] = jnp.broadcast_to(other_e / total, lane.shape)
        out_grad_ref[...] = (own_gate * came_ref[:, :D].astype(F32)).astype(BF)
        out_acc[...] = jnp.zeros_like(out_acc)
        back_acc[...] = jnp.zeros_like(back_acc)

    half = rows.shape[0] // 2

    def half_step(part, carry):
        at = pl.ds(pl.multiple_of(part * half, half), half)
        hidden = dotf(x_ref[at, :], w_in_ref[...])
        active_grad = dotf(out_grad_ref[at, :], w_out_ref[...], NT)
        value, slope = gelu_parts(hidden)
        active = value.astype(BF)
        hidden_grad = (slope * active_grad).astype(BF)
        active_ref[at, :] = active
        hidden_grad_ref[at, :] = hidden_grad
        out_acc[at, :] += dotf(active, w_out_ref[...])
        back_acc[at, :] += dotf(hidden_grad, w_in_ref[...], NT)
        return carry

    lax.fori_loop(0, 2, half_step, 0)

    @pl.when(step == pl.num_programs(0) - 1)
    def _():
        produced = out_acc[...].astype(BF).astype(F32)
        own_gate, other_gate = gate_ref[0][:, :1], gate_ref[1][:, :1]
        out_ref[...] = (own_gate * produced).astype(BF)
        gate_grad = jnp.sum(came_ref[:, :D].astype(F32) * produced, axis=1, keepdims=True)
        pull = own_gate * other_gate * gate_grad
        pair = came_ref[:, D:].astype(F32)
        logit_rows = pull * jnp.where(lane == own_ref[0], 1.0, -pair)
        high = logit_rows.astype(BF)
        rest = (logit_rows - high.astype(F32)).astype(BF)
        router = router_ref[...]
        back = back_acc[...].astype(BF).astype(F32)
        back = back + dotf(high, router, NT) + dotf(rest, router, NT)
        back_ref[...] = back.astype(BF)
        router_grad_ref[...] = dotf(rows, high, TN) + dotf(rows, rest, TN)


def expert_layer(own, x, came, w_in, w_out, router):
    count = x.shape[0]
    steps = 4
    part = FF // steps
    whole = lambda *shape: pl.BlockSpec(shape, lambda f, own: (0,) * len(shape))
    piece = pl.BlockSpec((count, part), lambda f, own: (0, own[1 + f]))
    return pl.pallas_call(
        expert_kernel,
        grid_spec=pltpu.PrefetchScalarGridSpec(
            num_scalar_prefetch=1,
            grid=(steps,),
            in_specs=[
                whole(count, D),
                whole(count, D + 128),
                pl.BlockSpec((D, part), lambda f, own: (0, f)),
                pl.BlockSpec((part, D), lambda f, own: (f, 0)),
                whole(D, 128),
            ],
            out_specs=[
                piece,
                piece,
                whole(count, D),
                whole(count, D),
                whole(count, D),
                whole(D, 128),
            ],
            scratch_shapes=[
                pltpu.VMEM((count, D), F32),
                pltpu.VMEM((count, D), F32),
                pltpu.VMEM((2, count, 128), F32),
            ],
        ),
        out_shape=(
            jax.ShapeDtypeStruct((count, FF), BF),
            jax.ShapeDtypeStruct((count, FF), BF),
            jax.ShapeDtypeStruct((count, D), BF),
            jax.ShapeDtypeStruct((count, D), BF),
            jax.ShapeDtypeStruct((count, D), BF),
            jax.ShapeDtypeStruct((D, 128), F32),
        ),
        cost_estimate=cost(0.05),
        name="expert_layer",
    )(own, x, came, w_in, w_out, router)


def mlp_back_kernel(
    back_ref, disp_ref, resid_ref, up_ref, gain_ref, w_ref, grad_ref, low_ref, gain_grad_ref, out_ref
):
    grad = dotf(disp_ref[...], back_ref[...], TN)
    resid = resid_ref[...]
    rate = lax.rsqrt(jnp.mean(resid * resid, axis=-1, keepdims=True) + EPS)
    unit = resid * rate
    gain_grad_ref[...] = jnp.sum(grad * unit, axis=0, keepdims=True)
    scaled = grad * gain_ref[...]
    total = up_ref[...] + rate * (
        scaled - unit * jnp.mean(scaled * unit, axis=-1, keepdims=True)
    )
    grad_ref[...] = total
    low = total.astype(BF)
    low_ref[...] = low
    for group in range(GROUPS):
        out_ref[group] = dotf(w_ref[group], low, NT).astype(BF)


def mlp_back(back, disp, resid, up, gain, w_attn):
    size = resid.shape[0]
    return pl.pallas_call(
        mlp_back_kernel,
        in_specs=[VM] * 6,
        out_specs=[VM] * 4,
        out_shape=(
            jax.ShapeDtypeStruct((size, D), F32),
            jax.ShapeDtypeStruct((size, D), BF),
            jax.ShapeDtypeStruct((1, D), F32),
            jax.ShapeDtypeStruct((GROUPS, GW, size), BF),
        ),
        cost_estimate=cost(4),
        name="mlp_back",
    )(back, disp, resid, up, gain, w_attn)


def project_back_kernel(
    dq_ref,
    dq_other_ref,
    dkv_ref,
    came_ref,
    w_ref,
    h_ref,
    gain_ref,
    dproj_ref,
    gain_grad_ref,
    half_ref,
):
    groups, size, _ = dq_ref.shape
    dq = (dq_ref[...] + dq_other_ref[...]).astype(BF).reshape(groups * size, GW)
    dkv = (dkv_ref[...] + came_ref[...].astype(F32)).astype(BF)
    dkv = dkv.reshape(groups * size, 2 * GW)
    dproj_ref[...] = jnp.concatenate((dq, dkv), axis=1)
    total = jnp.zeros((1, D), F32)
    for block in range(groups):
        half = dotf(dproj_ref[block * size : (block + 1) * size], w_ref[...], NT)
        half_ref[block] = half.astype(BF)
        total = total + jnp.sum(half * h_ref[block].astype(F32), axis=0, keepdims=True)
    gain_grad_ref[...] = total / gain_ref[...]


def project_back(dq, dq_other, dkv, came, w_cols, h_col, gain):
    groups, size, _ = dq.shape
    return pl.pallas_call(
        project_back_kernel,
        in_specs=[VM] * 7,
        out_specs=[VM] * 3,
        out_shape=(
            jax.ShapeDtypeStruct((groups * size, 3 * GW), BF),
            jax.ShapeDtypeStruct((1, D), F32),
            jax.ShapeDtypeStruct((groups, size, D), BF),
        ),
        cost_estimate=cost(4),
        name="project_back",
    )(dq, dq_other, dkv, came, w_cols, h_col, gain)


def qkv_grad_kernel(h_ref, dproj_ref, grad_ref):
    ranks, rows, _ = grad_ref.shape
    groups, size, _ = h_ref.shape
    total = dotf(h_ref[...].reshape(groups * size, D), dproj_ref[...], TN)
    for rank in range(ranks):
        grad_ref[rank] = total[rank * rows : (rank + 1) * rows]


def qkv_grad_of(h_col, dproj, ranks):
    return pl.pallas_call(
        qkv_grad_kernel,
        in_specs=[VM] * 2,
        out_specs=VM,
        out_shape=jax.ShapeDtypeStruct((ranks, D // ranks, 3 * GW), F32),
        cost_estimate=cost(0.05),
        name="qkv_grad",
    )(h_col, dproj)


def side_grad_kernel(att_ref, grad_ref, router_ref, out_ref):
    ranks, rows, _ = out_ref.shape
    inner = ranks // GROUPS
    for block in range(GROUPS):
        total = dotf(att_ref[block], grad_ref[...])
        for part in range(inner):
            out_ref[block * inner + part, :, :D] = total[part * rows : (part + 1) * rows]
    for rank in range(ranks):
        out_ref[rank, :, D:] = router_ref[rank * rows : (rank + 1) * rows]


def side_grad_of(att, grad, router_grad, ranks):
    return pl.pallas_call(
        side_grad_kernel,
        in_specs=[VM] * 3,
        out_specs=VM,
        out_shape=jax.ShapeDtypeStruct((ranks, D // ranks, D + 128), F32),
        cost_estimate=cost(0.05),
        name="side_grad",
    )(att, grad, router_grad)


def assemble_kernel(own_ref, p0_ref, p1_ref, p2_ref, p3_ref, rows_ref, scratch):
    side = D + 128
    wide = side + 3 * GW
    last = side + 3 * D
    width = (p0_ref.shape[1] - wide) // 2
    pieces = [ref[...].astype(F32) for ref in (p0_ref, p1_ref, p2_ref, p3_ref)]
    total = pieces[0] + pieces[1] + pieces[2] + pieces[3]
    rows_ref[:, :side] = total[:, :side].astype(BF)
    small = total[:, wide : wide + width] + total[:, wide + width :]
    high = small.astype(BF)
    rows_ref[:, last : last + width] = high
    rows_ref[:, last + width :] = (small - high.astype(F32)).astype(BF)
    for step, piece in enumerate(pieces):
        scratch[behind(step, own_ref[0], GROUPS)] = piece[:, side:wide]
    for group in range(GROUPS):
        for kind in range(3):
            at = side + (kind * GROUPS + group) * GW
            rows_ref[:, at : at + GW] = scratch[group, :, kind * GW : (kind + 1) * GW].astype(BF)


def assemble(own, parts):
    rows, width = parts[0].shape
    return pl.pallas_call(
        assemble_kernel,
        in_specs=[SM] + [VM] * 4,
        out_specs=VM,
        out_shape=jax.ShapeDtypeStruct((rows, width + 3 * D - 3 * GW), BF),
        scratch_shapes=[pltpu.VMEM((GROUPS, rows, 3 * GW), F32)],
        cost_estimate=cost(0.05),
        name="assemble",
    )(own, *parts)


def unpack_kernel(own_ref, pair_ref, came_ref, attn_ref, router_ref, qkv_ref, small_ref, *scratch):
    experts = router_ref.shape[0] if scratch else router_ref.shape[-1]
    last = 4 * D + 128
    width = small_ref.shape[1]
    small = jnp.zeros(small_ref.shape, F32)
    for near, ref in ((own_ref[0], pair_ref), (1 - own_ref[0], came_ref)):
        for part in range(2):
            value = ref[part].astype(F32)
            attn_ref[near * 2 + part] = value[:, :D]
            if scratch:
                scratch[0][near * 2 + part] = value[:, D : D + 128]
            else:
                router_ref[near * 2 + part] = value[:, D : D + experts]
            qkv_ref[near * 2 + part] = value[:, D + 128 : last]
            small = small + (value[:, last : last + width] + value[:, last + width :])
    small_ref[...] = small
    if scratch:
        count, lanes = router_ref.shape
        wide = scratch[0][...].reshape(lanes, 128)
        wide = jnp.concatenate((wide, jnp.zeros((-lanes % 128, 128), F32)), axis=0)
        router_ref[...] = wide.T[:count, :lanes]


def unpack(own, pair, came, experts):
    rows = pair.shape[1]
    width = (pair.shape[2] - 4 * D - 128) // 2
    flip = rows % 8 == 0 and 4 * rows <= 128
    router_shape = (experts, 4 * rows) if flip else (4, rows, experts)
    shapes = [(4, rows, D), router_shape, (4, rows, 3 * D), (rows, width)]
    outs = pl.pallas_call(
        unpack_kernel,
        in_specs=[SM] + [VM] * 2,
        out_specs=[VM] * 4,
        out_shape=[jax.ShapeDtypeStruct(shape, F32) for shape in shapes],
        scratch_shapes=[pltpu.VMEM((4, rows, 128), F32)] if flip else [],
        cost_estimate=cost(0.05),
        name="unpack",
    )(own.astype(jnp.int32), pair, came)
    attn, router, qkv, small = outs
    router = router.T if flip else router.reshape(4 * rows, experts)
    return attn.reshape(4 * rows, -1), router, qkv.reshape(4 * rows, -1), small


def gelu_parts(hidden):
    scale = math.sqrt(2.0 / math.pi)
    square = hidden * hidden
    bend = jnp.tanh(hidden * (scale + (scale * 0.044715) * square))
    half = 0.5 + 0.5 * bend
    slope = scale + (3 * scale * 0.044715) * square
    return hidden * half, half + (0.5 * hidden) * (1.0 - bend * bend) * slope


def swap(value, axis):
    return lax.ppermute(value, axis, [(0, 1), (1, 0)])


def tie(*values):
    return lax.optimization_barrier(values)


def turn(value, step):
    return lax.ppermute(value, "g", [(j, (j + step) % GROUPS) for j in range(GROUPS)])


def in_turn(pieces, g):
    pieces = jnp.stack(pieces[::-1] * 2)
    return lax.dynamic_slice_in_dim(pieces, GROUPS - 1 - g, GROUPS, 0)


def exchange(value, axes):
    return lax.all_to_all(value, axes, split_axis=0, concat_axis=0, tiled=True)


def in_order(own, came, index):
    return jnp.where(index == 0, jnp.stack((own, came)), jnp.stack((came, own)))


def rep_gather(value, y, c):
    pair = in_order(value, swap(value, "y"), y)
    return in_order(pair, swap(pair, "c"), c)


def halve(value, index, axis):
    count, rows, cols = value.shape
    value = value.reshape(count, 2, rows // 2, cols)
    away = swap(pick(value, 1 - index, 1).astype(BF), axis)
    return pick(value, index, 1) + away.astype(F32)


def pick(value, index, axis):
    return lax.dynamic_index_in_dim(value, index, axis, keepdims=False)


def norm_backward(grad, gain, value):
    rate = lax.rsqrt(jnp.mean(value * value, axis=-1, keepdims=True) + EPS)
    unit = value * rate
    scaled = grad * gain
    return rate * (scaled - unit * jnp.mean(scaled * unit, axis=-1, keepdims=True))


def local(
    tokens,
    cotangent,
    gain_attn,
    gain_mlp,
    w_qkv,
    w_attn_out,
    router,
    rel_table,
    w_in,
    w_out,
    segment_ids,
    expert_ids,
    rel_bucket,
):
    groups, inner = lax.axis_size("g"), lax.axis_size("i")
    g, i = lax.axis_index("g"), lax.axis_index("i")
    y, c = lax.axis_index("y"), lax.axis_index("c")
    ranks = groups * inner
    copies = 4
    size = tokens.shape[1]
    experts = ranks
    capacity = max(2, 4 * size // experts)
    inputs = tokens[0]
    upstream = cotangent[0]
    seg_all = segment_ids[0]
    chosen_ids = expert_ids[0]
    rows = w_qkv.shape[0] // copies
    me = g * inner + i
    own_g = g[None].astype(jnp.int32)

    rate = lax.rsqrt(jnp.mean(inputs * inputs, axis=-1, keepdims=True) + EPS)
    h_attn = (inputs * rate * gain_attn).astype(BF)
    h_pieces = [h_attn] + [turn(h_attn, step) for step in range(1, groups)]

    part = lax.dynamic_slice_in_dim(w_qkv, c * 2 * rows, 2 * rows, 0).astype(BF)
    part = part.reshape(2 * rows, 3, groups, GW).transpose(2, 0, 1, 3)
    part = jnp.broadcast_to(part[:, None], (groups, inner, 2 * rows, 3, GW))
    part = exchange(part.reshape(ranks, 2 * rows, 3 * GW), SEQ)
    both = jnp.concatenate((w_attn_out, jnp.pad(router, ((0, 0), (0, 128 - experts)))), axis=1)
    both = lax.dynamic_slice_in_dim(both, (c * 2 + y) * rows, rows, 0).astype(BF)
    both = jnp.broadcast_to(both[None], (ranks, rows, D + 128))
    w_cols = in_order(part, swap(part, "c"), c).swapaxes(0, 1).reshape(D, 3 * GW)

    expert_iota = jnp.arange(experts, dtype=jnp.int32)
    token_iota = jnp.arange(size, dtype=jnp.int32)
    pair_hot = jnp.any(chosen_ids[:, :, None] == expert_iota[None, None, :], axis=1)
    rank = jnp.dot(
        (token_iota[:, None] > token_iota[None, :]).astype(BF),
        pair_hot.astype(BF),
        preferred_element_type=F32,
    ).astype(jnp.int32)
    disp = (rank.T[:, None, :] == jnp.arange(capacity, dtype=jnp.int32)[None, :, None]) & (
        pair_hot.T[:, None, :]
    )
    disp = disp.astype(BF).reshape(experts * capacity, size)
    early = jnp.concatenate(
        (upstream.astype(BF), jnp.pad(pair_hot.astype(BF), ((0, 0), (0, 128 - experts)))), axis=1
    )
    early = jnp.dot(disp, early, preferred_element_type=F32).astype(BF)
    seg_col = pick(seg_all.reshape(groups, inner, size), i, 1)
    start = jnp.sum(
        (seg_all[None, None, :] < seg_col[:, :, None]).astype(jnp.int32), axis=-1, keepdims=True
    )
    padded = jnp.concatenate(
        (jnp.full((size - 1,), -1, jnp.int32), rel_bucket, jnp.full((1,), -1, jnp.int32))
    )
    reversed_bucket = padded.reshape(ranks + 1, size)[:, ::-1].reshape(-1)
    bucket_hot = (
        jnp.arange(BUCKETS, dtype=jnp.int32)[:, None] == reversed_bucket[None, :]
    ).astype(F32)
    table = lax.dynamic_slice_in_dim(rel_table, g * GHEADS, GHEADS, 0)
    bias_rows = jnp.dot(table, bucket_hot, precision=HIGHEST).reshape(GHEADS, ranks + 1, size)
    bias = bias_tiles(bias_rows, inner)
    bias, start, *h_pieces = tie(bias, start, *h_pieces)

    early = jnp.concatenate((early.reshape(ranks, capacity, D + 128), both), axis=1)
    early, *h_pieces = tie(early, *h_pieces)
    q, kv, h_col = project(own_g, h_pieces, w_cols)
    came_rows = exchange(early, SEQ)
    head_place = jnp.stack((i, jnp.int32(inner)))

    def place_of(columns):
        return jnp.concatenate((head_place, columns, own_g)).astype(jnp.int32)

    if inner == 2:
        kv_came = swap(kv, "i")
        kv_all = (kv, kv_came)
        columns = jnp.stack((i, 1 - i))
    else:
        kv_all = (lax.all_gather(kv, "i"),)
        columns = jnp.arange(inner, dtype=jnp.int32)
    place = place_of(columns)
    mixed, mixed_full, lse = attention_forward(place, q, kv_all, start, bias)
    mixed, came_rows = tie(mixed, came_rows)
    both = came_rows[:, capacity:]
    both = in_order(both, swap(both, "y"), y)
    came_rows = came_rows[:, :capacity].reshape(ranks * capacity, D + 128)
    att = exchange(mixed, "g")
    att, both = tie(att, both)
    both = in_order(both, swap(both, "c"), c)
    both = both.transpose(2, 0, 1, 3, 4).reshape(D, D + 128)
    w_attn_low = both[:, :D].reshape(groups, GW, D)
    router_low = both[:, D:]
    residual, outgoing = mlp_in(att, w_attn_low, inputs, gain_mlp[None], disp)

    arrived = exchange(outgoing.reshape(ranks, capacity, D), SEQ).reshape(ranks * capacity, D)
    active, hidden_grad, produced_grad, back, produced, router_grad = expert_layer(
        jnp.stack([me] + [2 * (c == f % 2) + (y == f // 2) for f in range(4)]).astype(jnp.int32),
        arrived,
        came_rows, w_in[0], w_out[0], router_low
    )
    back_rows = exchange(back.reshape(ranks, capacity, D), SEQ).reshape(ranks * capacity, D)

    part_ff = FF // 4
    slices = [slice(f * part_ff, (f + 1) * part_ff) for f in range(4)]

    def part_grads(f, active=active, hidden_grad=hidden_grad):
        return (
            dotf(active[:, slices[f]], produced_grad, TN),
            dotf(arrived, hidden_grad[:, slices[f]], TN),
        )

    core_far = [swap(grad.astype(BF), "c") for grad in part_grads(0)]
    near = [grad.astype(BF) for grad in part_grads(1)]
    away = [
        (grad + core.astype(F32)).astype(BF) for grad, core in zip(part_grads(2), core_far)
    ]
    far_out = swap(away[0], "y")
    back_rows, *near = tie(back_rows, *near)

    resid_grad, attn_grad, gain_two, out_grad = mlp_back(
        back_rows, disp, residual, upstream, gain_mlp[None], w_attn_low
    )
    out_grad = exchange(out_grad, "g")
    side_grad = side_grad_of(att, attn_grad, router_grad, ranks)
    out_grad, produced, side_grad, away_in = tie(out_grad, produced, side_grad, away[1])
    far_in = swap(away_in, "y")
    side_grad = halve(side_grad, c, "c")
    near = [swap(grad, "c") for grad in near]
    returned = exchange(produced.reshape(ranks, capacity, D), SEQ)

    def inner_reduce(value):
        value = value.reshape(groups, inner, *value.shape[1:])
        if inner > 2:
            return lax.psum_scatter(value, "i", scatter_dimension=1).astype(BF)
        own = pick(value, i, 1) + swap(pick(value, 1 - i, 1).astype(BF), "i").astype(F32)
        return own.astype(BF)

    if inner == 2:
        dq_other, dkv_other, dist_other = attention_backward(
            place_of(1 - i[None]),
            q,
            kv_came[None],
            start,
            bias,
            lse,
            mixed_full,
            out_grad,
            BF,
            8,
        )
        out_grad, dq_other, dkv_other, far_out, side_grad = tie(
            out_grad, dq_other, dkv_other, far_out, side_grad
        )
        dkv_came = swap(dkv_other[0], "i")
        dq, dkv_own, dist = attention_backward(
            place_of(i[None]),
            q,
            kv[None],
            start,
            bias,
            lse,
            mixed_full,
            out_grad,
            F32,
            1,
        )
        dkv_own = dkv_own[0]
        dist = jnp.concatenate((dist, dist_other))
    else:
        dq, dkv_all, dist = attention_backward(
            place, q, kv_all[0], start, bias, lse, mixed_full, out_grad, F32, 1
        )
        dkv_own = lax.psum_scatter(dkv_all, "i")
        dkv_came = jnp.zeros(dkv_own.shape, BF)
        dq_other = jnp.zeros_like(dq)
        dist = jnp.take(dist, (i - jnp.arange(inner)) % inner, axis=0)
    dkv_own, returned, far_in, side_grad = tie(dkv_own, returned, far_in, side_grad)
    side_grad = halve(side_grad, y, "y")
    returned = returned.reshape(ranks * capacity, D)
    dproj, gain_one, half = project_back(
        dq, dq_other, dkv_own, dkv_came, w_cols, h_col, gain_attn[None]
    )
    half = exchange(half, "g")
    parts = halve(qkv_grad_of(h_col, dproj, ranks), c, "c")
    parts, gain_one, gain_two, dist = tie(parts, gain_one, gain_two, dist)
    parts = jnp.concatenate((side_grad, halve(parts, y, "y")), axis=2)
    parts, active, hidden_grad, *near = tie(parts, active, hidden_grad, *near)
    mine_out, mine_in = [
        grad + core.astype(F32) for grad, core in zip(part_grads(3, active, hidden_grad), near)
    ]
    dist = dist[:, :, 1:].transpose(1, 2, 0, 3).reshape(GHEADS, ranks, 2 * size)
    dist_rows = jnp.pad(dist[:, :, size:], ((0, 0), (0, 1), (0, 0))) + jnp.pad(
        dist[:, :, :size], ((0, 0), (1, 0), (0, 0))
    )
    table_grad = jnp.dot(dist_rows.reshape(GHEADS, -1), bucket_hot.T, precision=HIGHEST)
    table_all = lax.dynamic_update_slice(
        jnp.zeros((HEADS, BUCKETS), F32), table_grad, (g * GHEADS, 0)
    )
    small = jnp.concatenate((gain_one[0], gain_two[0], table_all.reshape(-1)))
    count = small.shape[0]
    width = -(-count // (rows * 128)) * 128
    small = jnp.pad(small.reshape(-1, 128), ((0, (rows * width - count) // 128), (0, 0)))
    small = small.reshape(rows, width)
    small = small + (swap(small, "i") if inner == 2 else lax.psum(small, "i") - small)
    high = lax.reduce_precision(small, 8, 7)
    small = jnp.concatenate((high, small - high), axis=1).astype(BF)
    small = jnp.broadcast_to(small[None], (groups, rows, 2 * width))

    parts, half = tie(jnp.concatenate((inner_reduce(parts), small), axis=2), half)
    parts = [pick(parts, g, 0)] + [
        turn(pick(parts, lax.rem(g + step, groups), 0), step) for step in range(1, groups)
    ]
    norm_in_grad = jnp.sum(half.astype(F32), axis=0)
    input_grad = resid_grad + norm_backward(norm_in_grad, gain_attn, inputs)
    result = residual + dotf(disp, returned, TN)
    shards = assemble(own_g, parts)
    pair = in_order(shards, swap(shards, "y"), y)
    attn_shard, router_shard, qkv_shard, small = unpack(c[None], pair, swap(pair, "c"), experts)
    small = small.reshape(-1)
    w_in_shard = mine_in + far_in.astype(F32)
    w_out_shard = mine_out + far_out.astype(F32)
    return (
        result[None],
        input_grad[None],
        small[:D],
        small[D : 2 * D],
        qkv_shard,
        attn_shard,
        router_shard,
        small[2 * D : 2 * D + HEADS * BUCKETS].reshape(HEADS, BUCKETS),
        w_in_shard[None],
        w_out_shard[None],
    )


def solution(mesh):
    ranks = mesh.shape["seq"]
    split = Mesh(
        mesh.devices.reshape(2, mesh.shape["rep"] // 2, GROUPS, ranks // GROUPS),
        ("y", "c", "g", "i"),
    )
    placed = (
        P(REP, SEQ, None),
        P(REP, SEQ, None),
        P(),
        P(),
        P(SEQ, None),
        P(SEQ, None),
        P(SEQ, None),
        P(),
        P(SEQ, None, None),
        P(SEQ, None, None),
        P(REP, None),
        P(REP, SEQ, None),
        P(),
    )
    return jax.shard_map(
        local,
        mesh=split,
        in_specs=placed,
        out_specs=(
            P(REP, SEQ, None),
            P(REP, SEQ, None),
            P(),
            P(),
            P(SEQ, None),
            P(SEQ, None),
            P(SEQ, None),
            P(),
            P(SEQ, None, REP),
            P(SEQ, REP, None),
        ),
        check_vma=False,
    )
```
